32 devices in a mesh: gz: 4 (over z), gx: 2 (over x), gy: 4 (over y, core).
Axes of the slice: x: 2, y: 2, z: 4, core: 2. Of those that a mesh axis runs over, the one named last changes fastest.
Arguments:
- density: float32 [128, 256, 512], P('gx', 'gy', 'gz'), may hold values from 0.01 to 1
- design_mask: int32 [128, 256, 512], P('gx', 'gy', 'gz'), may hold values from 0 to 2
- energy: bfloat16 [4, 128, 256, 512], P(None, 'gx', 'gy', 'gz'), may hold values from 0.099609375 to 3
- decay: float32 [4, 512], P(None, 'gz'), may hold values from 0.3 to 1
- case_index: int32 [4], replicated, may hold values from 0 to 15
- case_weight: float32 [16], replicated, may hold values from 0.2 to 1
Outputs:
- sensitivity: float32 [128, 256, 512], P('gx', 'gy', 'gz')
- compliance: float32 [4], replicated
The draws below stay inside these ranges and needn't reach their ends.
All inputs are finite; a program needn't handle non-finite values.
Results may differ from the reference program's by a relative error of at most 0.0006.
Values may be sent and summed in bfloat16 or wider, within the bound.
No kernel may reach another device: no remote copies, remote signals or barrier semaphores. Data moves between devices by JAX's collectives and lax.ppermute only.
A program may use at most 128 MiB of HBM per device.

```python
import math
import jax
import jax.numpy as jnp
from jax import lax

CASES = 4
LOADS = 16
RADIUS = 3
NX = 128
NY = 256
NZ = 512


def draw_decay(key, part):
    key_order = jax.random.fold_in(key, 11)
    key_rough = jax.random.fold_in(key, 12)
    key_where = jax.random.fold_in(key, 13)
    key_depth = jax.random.fold_in(key, 14)
    order = jax.random.permutation(key_order, CASES)
    slow_case = order < (CASES + 1) // 2
    rough = jax.random.uniform(key_rough, (CASES, NZ), jnp.float32, 0.5, 1.5)
    slow_rate = jnp.log(1.0 / 0.3) / NZ
    rates = jnp.where(slow_case, slow_rate, 1.0 / 40.0).astype(jnp.float32)
    retained = jnp.exp(-rates[:, None] * rough)
    positions = jax.random.randint(key_where, (CASES, 2), 0, NZ)
    depths = jax.random.uniform(key_depth, (CASES, 2), jnp.float32, 0.55, 0.8)
    cells = jnp.arange(NZ)[None, :]
    factor = jnp.where(cells == positions[:, 0:1], depths[:, 0:1], 1.0)
    factor = factor * jnp.where(cells == positions[:, 1:2], depths[:, 1:2], 1.0)
    return (retained * factor).astype(jnp.float32)


def with_ends(result, key, smallest, top_value):
    dims = result.shape
    index_at = [jax.random.randint(jax.random.fold_in(key, axis), (), 0, dims[axis]) for axis in range(len(dims))]
    result = result.at[tuple(index_at)].set(smallest)
    longest = dims.index(max(dims))
    index_at[longest] = (index_at[longest] + 1) % dims[longest]
    return result.at[tuple(index_at)].set(top_value)


def steps_of(own_key, extent, shards, smallest, largest):
    gain = 1.0
    for axis_at, parts in shards:
        steps = jax.random.uniform(jax.random.fold_in(jax.random.fold_in(own_key, 6), axis_at), (parts,), jnp.float32, smallest / len(shards), largest / len(shards))
        gain = gain * jnp.repeat(jnp.exp(steps), extent[axis_at] // parts).reshape((-1,) + (1,) * (len(extent) - 1 - axis_at))
    return gain


def setup_inputs(seed: int = 0) -> dict:
    key_of = jax.random.split(jax.random.key(seed), 7)
    density = jnp.clip(jnp.exp(math.log(1.0) - 4.6051702 * jax.random.uniform(key_of[0], (NX, NY, NZ), jnp.float32) ** steps_of(key_of[0], (NX, NY, NZ), ((0, 2), (1, 4), (2, 4)), -0.2, 0.2)), 0.01, 1.0)
    design_mask = with_ends(jax.random.randint(key_of[1], (NX, NY, NZ), 0, 3), jax.random.fold_in(key_of[1], 1), 0, 2).astype(jnp.int32)
    energy = jnp.clip(jnp.exp(math.log(3.0) - 3.4051113 * jax.random.uniform(key_of[2], (CASES, NX, NY, NZ), jnp.float32) ** steps_of(key_of[2], (CASES, NX, NY, NZ), ((1, 2), (2, 4), (3, 4)), -0.2, 0.2)), 0.099609375, 3.0).astype(jnp.bfloat16)
    decay = draw_decay(jax.random.fold_in(key_of[6], 71), 0)
    case_index = with_ends(jax.random.randint(key_of[4], (CASES,), 0, LOADS), jax.random.fold_in(key_of[4], 1), 0, LOADS - 1).astype(jnp.int32)
    case_weight = jnp.clip(jax.random.uniform(key_of[5], (LOADS,), jnp.float32, 0.2, 1.0), 0.2, 1.0)
    return dict(density=density, design_mask=design_mask, energy=energy, decay=decay, case_index=case_index, case_weight=case_weight)


def kernel_taps():
    offsets = jnp.arange(-RADIUS, RADIUS + 1).astype(jnp.float32)
    raw_taps = jnp.exp(-2.0 * offsets * offsets / (RADIUS * RADIUS))
    return raw_taps / jnp.sum(raw_taps)


def planar_filter(padded, width_x, width_y):
    taps = kernel_taps()
    along_x = taps[0] * padded[:, 0:width_x]
    for offset in range(1, 2 * RADIUS + 1):
        along_x = along_x + taps[offset] * padded[:, offset:offset + width_x]
    along_y = taps[0] * along_x[:, :, 0:width_y]
    for offset in range(1, 2 * RADIUS + 1):
        along_y = along_y + taps[offset] * along_x[:, :, offset:offset + width_y]
    return along_y


def solid_density(density, design_mask):
    return jnp.where(design_mask == 1, 0.001, jnp.where(design_mask == 2, 1.0, density)).astype(jnp.float32)


def smooth_step(state, inputs):
    values, rate = inputs
    state = rate[:, None, None] * state + (1.0 - rate)[:, None, None] * values
    return state, state


def reference(density, design_mask, energy, decay, case_index, case_weight):
    dense = solid_density(density, design_mask)
    source = -3.0 * (dense ** 3)[None] * energy.astype(jnp.float32)
    padded = jnp.pad(source, ((0, 0), (RADIUS, RADIUS), (RADIUS, RADIUS), (0, 0)))
    planar = planar_filter(padded, NX, NY)
    columns = jnp.moveaxis(planar, 3, 0)
    rates = jnp.transpose(decay)
    initial = jnp.zeros((CASES, NX, NY), jnp.float32)
    _, forward = lax.scan(smooth_step, initial, (columns, rates))
    _, backward = lax.scan(smooth_step, initial, (forward, rates), reverse=True)
    smooth = jnp.moveaxis(backward, 0, 3)
    filtered = smooth / jnp.maximum(dense, 0.1)[None]
    selector = (case_index[:, None] == jnp.arange(LOADS).astype(jnp.int32)[None, :]).astype(jnp.float32)
    weights = jnp.sum(selector * case_weight[None, :], axis=1)
    combined = jnp.sum(weights[:, None, None, None] * filtered, axis=0)
    sensitivity = jnp.where(design_mask == 0, combined, 0.0).astype(jnp.float32)
    compliance = jnp.sum((dense ** 3)[None] * energy.astype(jnp.float32), axis=(1, 2, 3)) / (NX * NY * NZ)
    return sensitivity, compliance
```

```python
import functools
import jax
import jax.numpy as jnp
from jax import lax
from jax.experimental import pallas as pl
from jax.experimental.pallas import tpu as pltpu
from jax.sharding import PartitionSpec as P
import math

RADIUS = 3
LANES = 128
F32 = jnp.float32
BF16 = jnp.bfloat16
HIGH = lax.Precision.HIGHEST


def taps_1d():
    raw = [math.exp(-2.0 * k * k / (RADIUS * RADIUS)) for k in range(-RADIUS, RADIUS + 1)]
    total = sum(raw)
    return [r / total for r in raw]


def dot_hi(a, b, dims=((1,), (0,))):
    return lax.dot_general(a, b, (dims, ((), ())), precision=HIGH, preferred_element_type=F32)


def split2(v):
    hi = v.astype(BF16)
    lo = (v - hi.astype(F32)).astype(BF16)
    return hi, lo


def slab_kernel(cases, depth, bx, ny, nsteps, *refs):
    (index_ref, weight_ref, decay_ref, density_ref, mask_ref, energy_ref,
     t_ref, states_ref, umap_ref, rmat, wmat, acc) = refs
    step = pl.program_id(0)
    cols = bx * ny

    @pl.when(step == 0)
    def _():
        acc[...] = jnp.zeros_like(acc)
        states_ref[...] = jnp.zeros_like(states_ref)
        decay = decay_ref[...]
        logs = jnp.log(decay)
        row = lax.broadcasted_iota(jnp.int32, (depth, depth), 0)
        col = lax.broadcasted_iota(jnp.int32, (depth, depth), 1)
        upto = (row <= col).astype(F32)
        up = dot_hi(logs, upto)
        up_ex = up - logs
        up_t = jnp.transpose(up)
        logs_t = jnp.transpose(logs)
        keep_t = 1.0 - jnp.transpose(decay)
        up_ex_t = up_t - logs_t
        total = up[:, depth - 1:depth]
        zero_row = jnp.zeros((1, depth), F32)
        e_rows, h_rows, a_rows, c_rows = [], [], [], []
        d_col, k_col = [], []
        for c in range(cases):
            scale = -3.0 * weight_ref[index_ref[c]]
            keep = keep_t[:, c:c + 1]
            gap_f = up[c:c + 1, :] - up_t[:, c:c + 1]
            f_t = jnp.where(col >= row, jnp.exp(jnp.minimum(gap_f, 0.0)), 0.0) * keep
            gap_b = up_ex_t[:, c:c + 1] - up_ex[c:c + 1, :]
            b_t = jnp.where(col <= row, jnp.exp(jnp.minimum(gap_b, 0.0)), 0.0) * keep
            full = dot_hi(f_t, b_t) * scale
            hi, lo = split2(full)
            rmat[c * depth:(c + 1) * depth, 0:depth] = hi
            rmat[c * depth:(c + 1) * depth, depth:2 * depth] = lo
            e_row = jnp.exp(total[c:c + 1] - up[c:c + 1, :]) * (1.0 - decay[c:c + 1, :]) * scale
            b_row = jnp.exp(up_ex[c:c + 1, :]) * (1.0 - decay[c:c + 1, :])
            h_row = dot_hi(b_row, f_t, ((1,), (1,))) * scale
            pads = lambda r: jnp.concatenate([zero_row] * c + [r] + [zero_row] * (cases - 1 - c), axis=1)
            e_rows.append(pads(e_row))
            h_rows.append(pads(h_row))
            lead = jnp.exp(up[c:c + 1, :])
            a_row = dot_hi(lead, b_t)
            c_row = jnp.exp(total[c:c + 1] - up_ex[c:c + 1, :])
            a_rows.append(a_row)
            c_rows.append(c_row)
        w_hi, w_lo = split2(jnp.concatenate(e_rows + h_rows, axis=0))
        wmat[...] = jnp.concatenate([w_hi, w_lo], axis=0)
        a_all = jnp.concatenate(a_rows, axis=0)
        u_all = jnp.concatenate([a_all] + c_rows, axis=0)
        u_hi = u_all.astype(BF16).astype(F32)
        u_lo = u_all - u_hi
        umap_ref[...] = jnp.concatenate([u_hi, u_hi, u_lo, jnp.zeros_like(u_lo)], axis=0)
        aux = nsteps * cols
        lane = lax.broadcasted_iota(jnp.int32, (cases, LANES), 1)
        states_ref[0:cases, aux:aux + LANES] = jnp.where(
            lane == 0, jnp.exp(total), jnp.where(lane == 1, a_all[:, 0:1], 0.0))

    mask = mask_ref[...]
    dense = jnp.where(mask == 1, 0.001, jnp.where(mask == 2, 1.0, density_ref[...]))
    cube = dense * dense * dense
    parts = []
    for c in range(cases):
        work = cube * energy_ref[c].astype(F32)
        acc[c] += jnp.sum(work.reshape(cols // 8, 8, depth), axis=0)
        parts.append(work.astype(BF16).reshape(cols, depth))
    source = jnp.concatenate(parts, axis=1)
    both = lax.dot_general(source, rmat[...], (((1,), (0,)), ((), ())), preferred_element_type=F32)
    t_ref[...] = (both[:, 0:depth] + both[:, depth:2 * depth]).reshape(bx, ny, depth)
    faces = lax.dot_general(wmat[...], source, (((1,), (1,)), ((), ())), preferred_element_type=F32)
    start = pl.multiple_of(step * cols, LANES)
    states_ref[:, pl.ds(start, cols)] = faces[0:2 * cases] + faces[2 * cases:4 * cases]

    @pl.when(step == nsteps - 1)
    def _():
        aux = nsteps * cols
        lane = lax.broadcasted_iota(jnp.int32, (cases, LANES), 1)
        sums = jnp.sum(jnp.sum(acc[...], axis=1), axis=1, keepdims=True)
        now = states_ref[0:cases, aux:aux + LANES]
        states_ref[0:cases, aux:aux + LANES] = jnp.where(lane == 2, sums, now)


def slab_call(density, design_mask, energy, decay, case_index, case_weight):
    cases, nx, ny, depth = energy.shape
    bx = 8
    nsteps = nx // bx
    body = functools.partial(slab_kernel, cases, depth, bx, ny, nsteps)
    smem = pl.BlockSpec(memory_space=pltpu.SMEM)
    whole = lambda shape: pl.BlockSpec(shape, lambda i: (0,) * len(shape))
    return pl.pallas_call(
        body,
        grid=(nsteps,),
        in_specs=[
            smem, smem, whole((cases, depth)),
            pl.BlockSpec((bx, ny, depth), lambda i: (i, 0, 0)),
            pl.BlockSpec((bx, ny, depth), lambda i: (i, 0, 0)),
            pl.BlockSpec((cases, bx, ny, depth), lambda i: (0, i, 0, 0)),
        ],
        out_specs=[
            pl.BlockSpec((bx, ny, depth), lambda i: (i, 0, 0)),
            whole((2 * cases, nx * ny + LANES)),
            whole((8 * cases, depth)),
        ],
        out_shape=[
            jax.ShapeDtypeStruct((nx, ny, depth), F32),
            jax.ShapeDtypeStruct((2 * cases, nx * ny + LANES), F32),
            jax.ShapeDtypeStruct((8 * cases, depth), F32),
        ],
        scratch_shapes=[
            pltpu.VMEM((cases * depth, 2 * depth), BF16),
            pltpu.VMEM((4 * cases, cases * depth), BF16),
            pltpu.VMEM((cases, 8, depth), F32),
        ],
        compiler_params=pltpu.CompilerParams(
            dimension_semantics=("arbitrary",), vmem_limit_bytes=24 * 2**20),
        name="slab",
    )(case_index, case_weight, decay, density, design_mask, energy)


def couple_kernel(cases, nslabs, nx, ny, depth, *refs):
    slot_ref, msgs, t_ref, umap_ref = refs[0], refs[1:1 + nslabs], refs[1 + nslabs], refs[2 + nslabs]
    out_ref, xedge_ref, sums_ref, gains = refs[3 + nslabs:]
    cols = nx * ny
    mine = slot_ref[0]
    up_x = slot_ref[1]

    def pick(j):
        return None

    stack = gains
    for m in range(nslabs):
        stack[m] = msgs[m][...]
    comp = jnp.zeros((2 * cases, LANES), F32)
    for m in range(nslabs):
        comp = comp + stack[m, :, cols:cols + LANES]
    sums_ref[...] = comp
    state = jnp.zeros((cases, cols), F32)
    entering = jnp.zeros((cases, cols), F32)
    tops = []
    scalars = []
    for j in range(nslabs):
        at = slot_ref[2 + j]
        aux = stack[at, 0:cases, cols:cols + LANES]
        gain, turn = aux[:, 0:1], aux[:, 1:2]
        scalars.append((at, gain))
        entering = jnp.where(mine == j, state, entering)
        tops.append(stack[at, cases:2 * cases, 0:cols] + turn * state)
        state = gain * state + stack[at, 0:cases, 0:cols]
    state = jnp.zeros((cases, cols), F32)
    above = jnp.zeros((cases, cols), F32)
    for j in reversed(range(nslabs)):
        gain = scalars[j][1]
        above = jnp.where(mine == j, state, above)
        state = tops[j] + gain * state
    faces = jnp.concatenate([entering, above], axis=0)
    hi = faces.astype(BF16).astype(F32)
    lo = faces - hi
    lhs = jnp.concatenate([hi, lo, hi, jnp.zeros_like(hi)], axis=0).astype(BF16)
    add = lax.dot_general(lhs, umap_ref[...].astype(BF16), (((0,), (0,)), ((), ())), preferred_element_type=F32)
    out_ref[...] = t_ref[...] + add.reshape(nx, ny, depth)
    xedge_ref[...] = out_ref[pl.ds(up_x, RADIUS)].astype(BF16)


def couple_call(slots, msgs, t_local, umap, cases):
    nx, ny, depth = t_local.shape
    nslabs = len(msgs)
    body = functools.partial(couple_kernel, cases, nslabs, nx, ny, depth)
    vm = pl.BlockSpec(memory_space=pltpu.VMEM)
    return pl.pallas_call(
        body,
        in_specs=[pl.BlockSpec(memory_space=pltpu.SMEM)] + [vm] * (nslabs + 2),
        out_specs=[vm, vm, vm],
        out_shape=[
            jax.ShapeDtypeStruct((nx, ny, depth), F32),
            jax.ShapeDtypeStruct((RADIUS, ny, depth), BF16),
            jax.ShapeDtypeStruct((2 * cases, LANES), F32),
        ],
        scratch_shapes=[pltpu.VMEM((nslabs, 2 * cases, nx * ny + LANES), F32)],
        compiler_params=pltpu.CompilerParams(vmem_limit_bytes=32 * 2**20),
        name="couple",
    )(slots, *msgs, t_local, umap)


def yedge_kernel(nx, ny, depth, t_ref, xb_ref, xa_ref, first_ref, last_ref):
    lead = jnp.zeros((RADIUS + 2, depth), F32)
    for k in range(RADIUS):
        for ref, y in ((first_ref, k), (last_ref, ny - RADIUS + k)):
            mid = t_ref[:, y, :]
            before = xb_ref[:, y, :].astype(F32)
            after = xa_ref[:, y, :].astype(F32)
            ref[k] = jnp.concatenate([before, mid, after, jnp.zeros((10, depth), F32)], axis=0).astype(BF16)


YPAD = 8


def plane_kernel(nx, ny, depth, bx, *refs):
    (t_ref, xb_ref, xa_ref, yb_ref, ya_ref, density_ref, mask_ref, out_ref, pad, line) = refs
    step = pl.program_id(0)
    taps = taps_1d()

    @pl.when(step == 0)
    def _():
        pad[RADIUS:RADIUS + nx, YPAD:YPAD + ny, :] = t_ref[...]
        pad[0:RADIUS, YPAD:YPAD + ny, :] = xb_ref[...].astype(F32)
        pad[RADIUS + nx:, YPAD:YPAD + ny, :] = xa_ref[...].astype(F32)
        rows = nx + 2 * RADIUS
        for k in range(RADIUS):
            pad[:, YPAD - RADIUS + k, :] = yb_ref[k, 0:rows].astype(F32)
            pad[:, YPAD + ny + k, :] = ya_ref[k, 0:rows].astype(F32)

    def one(i, carry):
        x = step * bx + i
        acc = taps[RADIUS] * pad[x + RADIUS]
        for k in range(RADIUS):
            acc = acc + taps[k] * (pad[x + k] + pad[x + 2 * RADIUS - k])
        line[...] = acc
        res = taps[RADIUS] * line[YPAD:YPAD + ny, :]
        for k in range(RADIUS):
            off = RADIUS - k
            res = res + taps[k] * (line[YPAD - off:YPAD - off + ny, :] + line[YPAD + off:YPAD + off + ny, :])
        out_ref[i] = jnp.where(mask_ref[i] == 0, res / jnp.maximum(density_ref[i], 0.1), 0.0)
        return carry

    lax.fori_loop(0, bx, one, 0, unroll=2)


def plane_call(t, xb, xa, yb, ya, density, design_mask):
    nx, ny, depth = t.shape
    bx = 8
    whole = lambda a: pl.BlockSpec(a.shape, lambda i: (0,) * a.ndim)
    blk = pl.BlockSpec((bx, ny, depth), lambda i: (i, 0, 0))
    return pl.pallas_call(
        functools.partial(plane_kernel, nx, ny, depth, bx),
        grid=(nx // bx,),
        in_specs=[whole(t), whole(xb), whole(xa), whole(yb), whole(ya), blk, blk],
        out_specs=blk,
        out_shape=jax.ShapeDtypeStruct(t.shape, F32),
        scratch_shapes=[
            pltpu.VMEM((nx + 2 * RADIUS, ny + 2 * YPAD, depth), F32),
            pltpu.VMEM((ny + 2 * YPAD, depth), F32),
        ],
        compiler_params=pltpu.CompilerParams(
            dimension_semantics=("arbitrary",), vmem_limit_bytes=24 * 2**20),
        name="plane",
    )(t, xb, xa, yb, ya, density, design_mask)


def pairs_of(count, first):
    out = []
    for i in range(first, count - 1, 2):
        out += [(i, i + 1), (i + 1, i)]
    return out


def xor_pairs(count, m):
    return [(i, i ^ m) for i in range(count)]


def shards(density, design_mask, energy, decay, case_index, case_weight):
    cases = energy.shape[0]
    nx, ny, depth = density.shape
    nz, gx, gy = (lax.axis_size(a) for a in ("gz", "gx", "gy"))
    iz, ix, iy = (lax.axis_index(a) for a in ("gz", "gx", "gy"))
    t_local, states, umap = slab_call(density, design_mask, energy, decay, case_index, case_weight)
    if nz & (nz - 1) == 0 and nz <= 4:
        msgs = [states] + [lax.ppermute(states, "gz", xor_pairs(nz, m)) for m in range(1, nz)]
        order = [iz ^ j for j in range(nz)]
    else:
        every = lax.all_gather(states, "gz")
        msgs = [every[j] for j in range(nz)]
        order = [jnp.int32(j) for j in range(nz)]
    even_x, even_y = ix % 2 == 0, iy % 2 == 0
    slots = jnp.stack([iz, jnp.where(even_x, nx - RADIUS, 0)] + order).astype(jnp.int32)
    t, xedge, sums = couple_call(slots, msgs, t_local, umap, cases)
    totals = sums[0:cases, 2]
    none = jnp.zeros_like(xedge)
    if gx > 1:
        swap = lax.ppermute(xedge, "gx", pairs_of(gx, 0))
        other = none
        if gx > 2:
            far = jnp.where(even_x, t[0:RADIUS], t[nx - RADIUS:]).astype(BF16)
            other = lax.ppermute(far, "gx", pairs_of(gx, 1))
        before = jnp.where(even_x, other, swap)
        after = jnp.where(even_x, swap, other)
    else:
        before = after = none
    rows = nx + 16
    first, last = pl.pallas_call(
        functools.partial(yedge_kernel, nx, ny, depth),
        out_shape=[jax.ShapeDtypeStruct((RADIUS, rows, depth), BF16)] * 2,
        compiler_params=pltpu.CompilerParams(vmem_limit_bytes=16 * 2**20),
        name="yedge",
    )(t, before, after)
    none = jnp.zeros_like(first)
    if gy > 1:
        swap = lax.ppermute(jnp.where(even_y, last, first), "gy", pairs_of(gy, 0))
        other = none
        if gy > 2:
            other = lax.ppermute(jnp.where(even_y, first, last), "gy", pairs_of(gy, 1))
        y_before = jnp.where(even_y, other, swap)
        y_after = jnp.where(even_y, swap, other)
    else:
        y_before = y_after = none
    sensitivity = plane_call(t, before, after, y_before, y_after, density, design_mask)
    for axis, n in (("gx", gx), ("gy", gy)):
        step = 1
        while step < n:
            totals = totals + lax.ppermute(totals, axis, xor_pairs(n, step))
            step *= 2
    all_cells = nx * ny * depth * nz * gx * gy
    return sensitivity, totals / all_cells


def solution(mesh):
    placed = (
        P("gx", "gy", "gz"),
        P("gx", "gy", "gz"),
        P(None, "gx", "gy", "gz"),
        P(None, "gz"),
        P(),
        P(),
    )
    return jax.shard_map(
        shards, mesh=mesh, in_specs=placed, out_specs=(P("gx", "gy", "gz"), P()), check_vma=False
    )
```

```python
import functools
import math
import jax
import jax.numpy as jnp
from jax import lax
from jax.experimental import pallas as pl
from jax.experimental.pallas import tpu as pltpu
from jax.sharding import PartitionSpec as P

RADIUS = 3
LANES = 128
MIB = 2**20
F32 = jnp.float32
BF16 = jnp.bfloat16
HIGH = lax.Precision.HIGHEST
HBM = pl.BlockSpec(memory_space=pltpu.HBM)
VMEM = pl.BlockSpec(memory_space=pltpu.VMEM)
SMEM = pl.BlockSpec(memory_space=pltpu.SMEM)


def taps_1d():
    raw = [math.exp(-2.0 * k * k / (RADIUS * RADIUS)) for k in range(-RADIUS, RADIUS + 1)]
    total = sum(raw)
    return [r / total for r in raw]


def dot_high(a, b, dims=((1,), (0,))):
    return lax.dot_general(a, b, (dims, ((), ())), precision=HIGH, preferred_element_type=F32)


def split2(v):
    hi = v.astype(BF16)
    return hi, (v - hi.astype(F32)).astype(BF16)


def split3(v):
    a = v.astype(BF16).astype(F32)
    b = (v - a).astype(BF16).astype(F32)
    return a, b, v - a - b


def put_lanes(columns):
    rows = columns[0].shape[0]
    lane = lax.broadcasted_iota(jnp.int32, (rows, LANES), 1)
    out = jnp.zeros((rows, LANES), F32)
    for k, col in enumerate(columns):
        out = jnp.where(lane == k, col, out)
    return out


def pad_rows(v, rows):
    return jnp.concatenate([v, jnp.zeros((rows - v.shape[0],) + v.shape[1:], v.dtype)], axis=0)


def sum3(block, at):
    return block[:, at : at + 1] + block[:, at + 1 : at + 2] + block[:, at + 2 : at + 3]


class Slab:
    def __init__(self, decay):
        cases, depth = decay.shape
        self.decay = decay
        self.row = lax.broadcasted_iota(jnp.int32, (depth, depth), 0)
        self.col = lax.broadcasted_iota(jnp.int32, (depth, depth), 1)
        logs = jnp.log(decay)
        self.up = dot_high(logs, (self.row <= self.col).astype(F32))
        self.up_ex = self.up - logs
        wide = lambda v: jnp.transpose(pad_rows(v, 8))
        self.up_t = wide(self.up)
        self.up_ex_t = wide(self.up_ex)
        self.keep_t = wide(1.0 - decay)
        self.total = self.up[:, depth - 1 : depth]

    def forward_t(self, c):
        gap = self.up[c : c + 1, :] - self.up_t[:, c : c + 1]
        weight = jnp.exp(jnp.minimum(gap, 0.0)) * self.keep_t[:, c : c + 1]
        return jnp.where(self.col >= self.row, weight, 0.0)

    def backward_t(self, c):
        gap = self.up_ex_t[:, c : c + 1] - self.up_ex[c : c + 1, :]
        weight = jnp.exp(jnp.minimum(gap, 0.0)) * self.keep_t[:, c : c + 1]
        return jnp.where(self.col <= self.row, weight, 0.0)


def case_scale(weight_ref, index_ref, c):
    return -3.0 * weight_ref[index_ref[c]]


def faces_kernel(shape, bx, *refs):
    cases, nx, ny, depth = shape
    (index_hbm, weight_hbm, decay_hbm, density_hbm, mask_hbm, energy_hbm,
     send_ref, own_ref, source_ref,
     index_ref, weight_ref, decay_ref, density_ref, mask_ref, energy_ref, small_sem, sem) = refs
    steps, cols = nx // bx, bx * ny
    small = [
        pltpu.make_async_copy(decay_hbm, decay_ref, small_sem.at[0]),
        pltpu.make_async_copy(index_hbm, index_ref, small_sem.at[1]),
        pltpu.make_async_copy(weight_hbm, weight_ref, small_sem.at[2]),
    ]
    big = []
    for s in range(steps):
        at = pl.ds(s * bx, bx)
        big.append([
            pltpu.make_async_copy(density_hbm.at[at], density_ref.at[at], sem.at[0, s]),
            pltpu.make_async_copy(mask_hbm.at[at], mask_ref.at[at], sem.at[1, s]),
            pltpu.make_async_copy(energy_hbm.at[:, at], energy_ref.at[:, at], sem.at[2, s]),
        ])
    for copy in small:
        copy.start()
    for group in big:
        for copy in group:
            copy.start()
    for copy in small:
        copy.wait()

    decay = decay_ref[...]
    slab = Slab(decay)
    zero_row = jnp.zeros((1, depth), F32)
    e_rows, h_rows, turns = [], [], []
    for c in range(cases):
        scale = case_scale(weight_ref, index_ref, c)
        f_t = slab.forward_t(c)
        keep = 1.0 - decay[c : c + 1, :]
        e_row = jnp.exp(slab.total[c : c + 1] - slab.up[c : c + 1, :]) * keep
        b_row = jnp.exp(slab.up_ex[c : c + 1, :]) * keep
        h_row = dot_high(b_row, f_t, ((1,), (1,)))
        turns.append(jnp.sum(b_row * jnp.exp(slab.up[c : c + 1, :]), axis=1, keepdims=True))
        place = lambda r: jnp.concatenate([zero_row] * c + [r * scale] + [zero_row] * (cases - 1 - c), axis=1)
        e_rows.append(place(e_row))
        h_rows.append(place(h_row))
    w_hi, w_lo = split2(jnp.concatenate(e_rows + h_rows, axis=0))
    wmat = jnp.concatenate([w_hi, w_lo], axis=0)

    sums = [jnp.zeros((8, depth), F32) for _ in range(cases)]
    for s in range(steps):
        for copy in big[s]:
            copy.wait()
        at = pl.ds(s * bx, bx)
        mask = mask_ref[at]
        dense = jnp.where(mask == 1, 0.001, jnp.where(mask == 2, 1.0, density_ref[at]))
        cube = dense * dense * dense
        span = pl.ds(s * cols, cols)
        for c in range(cases):
            work = cube * energy_ref[c, at].astype(F32)
            sums[c] = sums[c] + jnp.sum(work.reshape(cols // 8, 8, depth), axis=0)
            source_ref[span, c * depth : (c + 1) * depth] = work.astype(BF16).reshape(cols, depth)
        faces = lax.dot_general(
            wmat, source_ref[span, :], (((1,), (1,)), ((), ())), preferred_element_type=F32)
        faces = faces[0 : 2 * cases] + faces[2 * cases : 4 * cases]
        own_ref[:, span] = faces
        send_ref[:, span] = faces.astype(BF16)

    total = jnp.concatenate([jnp.sum(jnp.sum(v, axis=0, keepdims=True), axis=1, keepdims=True) for v in sums], axis=0)
    turn = jnp.concatenate(turns, axis=0)
    aux = put_lanes(split3(jnp.exp(slab.total)) + split3(turn) + split3(total))
    aux = pad_rows(aux, 2 * cases)
    tail = pl.ds(nx * ny, LANES)
    own_ref[:, tail] = aux
    send_ref[:, tail] = aux.astype(BF16)


def faces_call(density, design_mask, energy, decay, case_index, case_weight):
    cases, nx, ny, depth = energy.shape
    bx = 8
    width = nx * ny + LANES
    return pl.pallas_call(
        functools.partial(faces_kernel, energy.shape, bx),
        in_specs=[HBM] * 6,
        out_specs=[VMEM] * 3,
        out_shape=[
            jax.ShapeDtypeStruct((2 * cases, width), BF16),
            jax.ShapeDtypeStruct((2 * cases, width), F32),
            jax.ShapeDtypeStruct((nx * ny, cases * depth), BF16),
        ],
        scratch_shapes=[
            pltpu.SMEM(case_index.shape, case_index.dtype),
            pltpu.SMEM(case_weight.shape, F32),
            pltpu.VMEM(decay.shape, F32),
            pltpu.VMEM(density.shape, F32),
            pltpu.VMEM(density.shape, jnp.int32),
            pltpu.VMEM(energy.shape, BF16),
            pltpu.SemaphoreType.DMA((3,)),
            pltpu.SemaphoreType.DMA((3, nx // bx)),
        ],
        compiler_params=pltpu.CompilerParams(vmem_limit_bytes=20 * MIB),
        name="faces",
    )(case_index, case_weight, decay, density, design_mask, energy)


def local_kernel(shape, bx, *refs):
    cases, nx, ny, depth = shape
    (index_hbm, weight_hbm, decay_hbm, density_hbm, mask_hbm, source_ref,
     t_ref, factor_ref, umap_ref,
     index_ref, weight_ref, decay_ref, mask_ref, rmat, small_sem, sem) = refs
    steps, cols = nx // bx, bx * ny
    small = [
        pltpu.make_async_copy(decay_hbm, decay_ref, small_sem.at[0]),
        pltpu.make_async_copy(index_hbm, index_ref, small_sem.at[1]),
        pltpu.make_async_copy(weight_hbm, weight_ref, small_sem.at[2]),
    ]
    big = [
        pltpu.make_async_copy(density_hbm, factor_ref, sem.at[0]),
        pltpu.make_async_copy(mask_hbm, mask_ref, sem.at[1]),
    ]
    for copy in small + big:
        copy.start()
    for copy in small:
        copy.wait()
    slab = Slab(decay_ref[...])
    a_rows, c_rows = [], []
    for c in range(cases):
        f_t, b_t = slab.forward_t(c), slab.backward_t(c)
        hi, lo = split2(dot_high(f_t, b_t) * case_scale(weight_ref, index_ref, c))
        rmat[c * depth : (c + 1) * depth, 0:depth] = hi
        rmat[c * depth : (c + 1) * depth, depth : 2 * depth] = lo
        a_rows.append(dot_high(jnp.exp(slab.up[c : c + 1, :]), b_t))
        c_rows.append(jnp.exp(slab.total[c : c + 1] - slab.up_ex[c : c + 1, :]))
    u_all = jnp.concatenate(a_rows + c_rows, axis=0)
    u_hi = u_all.astype(BF16).astype(F32)
    umap_ref[...] = jnp.concatenate([u_hi, u_hi, u_all - u_hi, jnp.zeros_like(u_hi)], axis=0).astype(BF16)
    for copy in big:
        copy.wait()

    def one(s, carry):
        span = pl.ds(pl.multiple_of(s * cols, cols), cols)
        both = lax.dot_general(
            source_ref[span, :], rmat[...], (((1,), (0,)), ((), ())), preferred_element_type=F32)
        at = pl.ds(s * bx, bx)
        t_ref[at] = (both[:, 0:depth] + both[:, depth : 2 * depth]).reshape(bx, ny, depth)
        factor_ref[at] = jnp.where(mask_ref[at] == 0, 1.0 / jnp.maximum(factor_ref[at], 0.1), 0.0)
        return carry

    lax.fori_loop(0, steps, one, 0)


def local_call(density, design_mask, source, decay, case_index, case_weight):
    nx, ny, depth = density.shape
    cases = decay.shape[0]
    return pl.pallas_call(
        functools.partial(local_kernel, (cases, nx, ny, depth), 8),
        in_specs=[HBM] * 5 + [VMEM],
        out_specs=[VMEM] * 3,
        out_shape=[
            jax.ShapeDtypeStruct(density.shape, F32),
            jax.ShapeDtypeStruct(density.shape, F32),
            jax.ShapeDtypeStruct((8 * cases, depth), BF16),
        ],
        scratch_shapes=[
            pltpu.SMEM(case_index.shape, case_index.dtype),
            pltpu.SMEM(case_weight.shape, F32),
            pltpu.VMEM(decay.shape, F32),
            pltpu.VMEM(density.shape, jnp.int32),
            pltpu.VMEM((cases * depth, 2 * depth), BF16),
            pltpu.SemaphoreType.DMA((3,)),
            pltpu.SemaphoreType.DMA((2,)),
        ],
        compiler_params=pltpu.CompilerParams(vmem_limit_bytes=20 * MIB),
        name="local",
    )(case_index, case_weight, decay, density, design_mask, source)


def couple_kernel(shape, nslabs, nsends, *refs):
    cases, nx, ny, depth = shape
    slot_ref, own_ref = refs[0:2]
    msgs = refs[2 : 1 + nslabs]
    t_ref, umap_ref, out_ref = refs[1 + nslabs : 4 + nslabs]
    sends = refs[4 + nslabs : 4 + nslabs + nsends]
    stack = refs[-1]
    cols = nx * ny
    mine = slot_ref[0]
    stack[0] = own_ref[...]
    for m, msg in enumerate(msgs):
        stack[m + 1] = msg[...].astype(F32)
    total = jnp.zeros((cases, 1), F32)
    for m in range(nslabs):
        total = total + sum3(stack[m, 0:cases, cols : cols + LANES], 6)
    state = jnp.zeros((cases, cols), F32)
    entering, above = state, state
    tops, gains = [], []
    for j in range(nslabs):
        at = slot_ref[2 + j]
        aux = stack[at, 0:cases, cols : cols + LANES]
        gains.append(sum3(aux, 0))
        entering = jnp.where(mine == j, state, entering)
        tops.append(stack[at, cases : 2 * cases, 0:cols] + sum3(aux, 3) * state)
        state = gains[j] * state + stack[at, 0:cases, 0:cols]
    state = jnp.zeros((cases, cols), F32)
    for j in reversed(range(nslabs)):
        above = jnp.where(mine == j, state, above)
        state = tops[j] + gains[j] * state
    faces = jnp.concatenate([entering, above], axis=0)
    hi = faces.astype(BF16).astype(F32)
    lhs = jnp.concatenate([hi, faces - hi, hi, jnp.zeros_like(hi)], axis=0).astype(BF16)
    add = lax.dot_general(lhs, umap_ref[...], (((0,), (0,)), ((), ())), preferred_element_type=F32)
    out_ref[...] = t_ref[...] + add.reshape(nx, ny, depth)
    aux = pad_rows(put_lanes(split3(total)), 16).astype(BF16)
    for k, ref in enumerate(sends):
        edge = out_ref[pl.ds(slot_ref[1] if k == 0 else nx - RADIUS - slot_ref[1], RADIUS)]
        ref[0 : RADIUS * ny, :] = edge.reshape(RADIUS * ny, depth).astype(BF16)
        ref[RADIUS * ny :, :] = aux


def couple_call(slots, own, msgs, t_local, umap, nsends):
    nx, ny, depth = t_local.shape
    cases = own.shape[0] // 2
    nslabs = len(msgs) + 1
    return pl.pallas_call(
        functools.partial(couple_kernel, (cases, nx, ny, depth), nslabs, nsends),
        in_specs=[SMEM] + [VMEM] * (nslabs + 2),
        out_specs=[VMEM] * (1 + nsends),
        out_shape=[jax.ShapeDtypeStruct(t_local.shape, F32)]
        + [jax.ShapeDtypeStruct((RADIUS * ny + 16, depth), BF16)] * nsends,
        scratch_shapes=[pltpu.VMEM((nslabs,) + own.shape, F32)],
        compiler_params=pltpu.CompilerParams(vmem_limit_bytes=28 * MIB),
        name="couple",
    )(slots, own, *msgs, t_local, umap)


def sided(even, got):
    a = got[0]
    b = got[1] if len(got) > 1 else jnp.zeros_like(a)
    return jnp.where(even, b, a), jnp.where(even, a, b)


def edge_kernel(shape, nx_sends, ny_sends, *refs):
    cases, nx, ny, depth = shape
    slot_ref, t_ref = refs[0:2]
    got_refs = refs[2 : 2 + nx_sends]
    own_send = refs[2 + nx_sends]
    sends = refs[3 + nx_sends : 3 + nx_sends + ny_sends]
    xb_ref, xa_ref, sums_ref, line = refs[3 + nx_sends + ny_sends :]
    taps = taps_1d()
    edge = RADIUS * ny
    even_x = slot_ref[2] == 0
    flip_y = slot_ref[3] == 1
    blocks = [r[0:edge, :].astype(F32) for r in got_refs]
    before, after = sided(even_x, blocks)
    xb_ref[...] = before
    xa_ref[...] = after
    total = sum3(own_send[edge : edge + 16, :].astype(F32), 0)
    for ref in got_refs:
        total = total + sum3(ref[edge : edge + 16, :].astype(F32), 0)
    sums_ref[...] = jnp.broadcast_to(total[0:8], (8, LANES))
    aux = put_lanes(split3(total)).astype(BF16)
    flat = t_ref.reshape(nx * ny, depth)
    columns = []
    for k in range(2 * RADIUS):
        y = k if k < RADIUS else ny - 2 * RADIUS + k
        line[8 : 8 + nx, :] = flat[pl.ds(y, nx, stride=ny), :]
        line[8 - RADIUS : 8, :] = xb_ref[pl.ds(y, RADIUS, stride=ny), :]
        line[8 + nx : 8 + nx + RADIUS, :] = xa_ref[pl.ds(y, RADIUS, stride=ny), :]
        acc = taps[RADIUS] * line[8 : 8 + nx, :]
        for d in range(1, RADIUS + 1):
            acc = acc + taps[RADIUS + d] * (line[8 - d : 8 - d + nx, :] + line[8 + d : 8 + d + nx, :])
        columns.append(acc)
    for m, ref in enumerate(sends):
        for k in range(RADIUS):
            first, last = columns[k], columns[RADIUS + k]
            pick = jnp.where(flip_y == (m == 0), first, last)
            ref[k * nx : (k + 1) * nx, :] = pick.astype(BF16)
        ref[RADIUS * nx :, :] = aux


def edge_call(slots, t, got, own_send, ny_sends, cases):
    nx, ny, depth = t.shape
    return pl.pallas_call(
        functools.partial(edge_kernel, (cases, nx, ny, depth), len(got), ny_sends),
        in_specs=[SMEM] + [VMEM] * (2 + len(got)),
        out_specs=[VMEM] * (ny_sends + 3),
        out_shape=[jax.ShapeDtypeStruct((RADIUS * nx + 16, depth), BF16)] * ny_sends
        + [jax.ShapeDtypeStruct((RADIUS * ny, depth), F32)] * 2
        + [jax.ShapeDtypeStruct((8, LANES), F32)],
        scratch_shapes=[pltpu.VMEM((nx + 16, depth), F32)],
        compiler_params=pltpu.CompilerParams(vmem_limit_bytes=16 * MIB),
        name="edge",
    )(slots, t, *got, own_send)


def plane_kernel(shape, bx, *refs):
    nx, ny, depth = shape
    (t_ref, xb_ref, xa_ref, factor_ref, out_hbm, first_ref, last_ref,
     pad, line, out_ref, sem) = refs
    taps = taps_1d()
    steps = nx // bx
    pad[0:RADIUS] = xb_ref[...].reshape(RADIUS, ny, depth)
    pad[RADIUS : 2 * RADIUS] = t_ref[0:RADIUS]
    pad[2 * RADIUS : 3 * RADIUS] = t_ref[RADIUS : 2 * RADIUS]
    tail = 3 * RADIUS
    pad[tail : tail + 2 * RADIUS] = t_ref[nx - 2 * RADIUS : nx]
    pad[tail + 2 * RADIUS :] = xa_ref[...].reshape(RADIUS, ny, depth)
    zeros = jnp.zeros((8, depth), F32)
    for slot in range(2):
        line[slot, 0:8, :] = zeros
        line[slot, 8 + ny :, :] = zeros

    def row(ref, x, at, slot):
        acc = taps[RADIUS] * ref[at]
        for d in range(1, RADIUS + 1):
            acc = acc + taps[RADIUS + d] * (ref[at - d] + ref[at + d])
        line[slot, 8 : 8 + ny, :] = acc
        res = taps[RADIUS] * acc
        for d in range(1, RADIUS + 1):
            res = res + taps[RADIUS + d] * (line[slot, 8 - d : 8 - d + ny, :] + line[slot, 8 + d : 8 + d + ny, :])
        res = res * factor_ref[x]
        out_ref[x] = res
        first_ref[x] = res[0:8]
        last_ref[x] = res[ny - 8 : ny]

    copies = [
        pltpu.make_async_copy(out_ref.at[pl.ds(s * bx, bx)], out_hbm.at[pl.ds(s * bx, bx)], sem.at[s])
        for s in range(steps)
    ]
    for s in range(steps):
        lo, hi = s * bx, (s + 1) * bx
        if s == 0:
            for x in range(RADIUS):
                row(pad, x, x + RADIUS, x % 2)
            lo = RADIUS
        if s == steps - 1:
            for x in range(nx - RADIUS, nx):
                row(pad, x, x - (nx - RADIUS) + tail + RADIUS, x % 2)
            hi = nx - RADIUS

        def pair(i, carry):
            row(t_ref, i, i, i % 2)
            return carry

        lax.fori_loop(lo, hi, pair, 0)
        copies[s].start()
    for copy in copies:
        copy.wait()


def plane_call(t, xb, xa, factor):
    nx, ny, depth = t.shape
    bx = 8
    return pl.pallas_call(
        functools.partial(plane_kernel, t.shape, bx),
        in_specs=[VMEM] * 4,
        out_specs=[HBM, VMEM, VMEM],
        out_shape=[
            jax.ShapeDtypeStruct(t.shape, F32),
            jax.ShapeDtypeStruct((nx, 8, depth), F32),
            jax.ShapeDtypeStruct((nx, 8, depth), F32),
        ],
        scratch_shapes=[
            pltpu.VMEM((7 * RADIUS - RADIUS, ny, depth), F32),
            pltpu.VMEM((2, ny + 16, depth), F32),
            pltpu.VMEM(t.shape, F32),
            pltpu.SemaphoreType.DMA((nx // bx,)),
        ],
        compiler_params=pltpu.CompilerParams(vmem_limit_bytes=20 * MIB),
        name="plane",
    )(t, xb, xa, factor)


def finish_kernel(shape, cells, ngot, nextra, cases, *refs):
    nx, ny, depth = shape
    slot_ref = refs[0]
    got_refs = refs[1 : 1 + ngot]
    sums_ref = refs[1 + ngot]
    extra_refs = refs[2 + ngot : 2 + ngot + nextra]
    first_ref, last_ref, factor_ref, _, out_hbm, comp_ref, strip, sem = refs[2 + ngot + nextra :]
    taps = taps_1d()
    edge = RADIUS * nx
    even_y = slot_ref[3] == 0
    blocks = [r[0:edge, :].astype(F32) for r in got_refs]
    before, after = sided(even_y, blocks) if blocks else (jnp.zeros((edge, depth), F32),) * 2
    flat = factor_ref.reshape(nx * ny, depth)
    for ref, side in ((first_ref, 0), (last_ref, 1)):
        strip[side] = ref[...]
        view = strip.at[side].reshape(nx * 8, depth)
        for y in range(RADIUS):
            add = jnp.zeros((nx, depth), F32)
            for k in range(RADIUS):
                if side == 0:
                    d, halo, own = y + RADIUS - k, before[k * nx : (k + 1) * nx], y
                else:
                    d, halo, own = k + 1 + RADIUS - 1 - y, after[k * nx : (k + 1) * nx], ny - RADIUS + y
                if d <= RADIUS:
                    add = add + taps[RADIUS + d] * halo
            at = own if side == 0 else own - (ny - 8)
            view[pl.ds(at, nx, stride=8), :] += flat[pl.ds(own, nx, stride=ny), :] * add
    copies = [
        pltpu.make_async_copy(strip.at[0], out_hbm.at[:, 0:8, :], sem.at[0]),
        pltpu.make_async_copy(strip.at[1], out_hbm.at[:, ny - 8 : ny, :], sem.at[1]),
    ]
    for copy in copies:
        copy.start()
    total = sums_ref[...]
    for ref in extra_refs:
        total = total + ref[...]
    for c in range(cases):
        comp_ref[c] = total[c, 0] / cells
    for copy in copies:
        copy.wait()


def finish_call(slots, got, sums, extra, first, last, factor, out, cells, cases):
    nx, ny, depth = out.shape
    nin = 1 + len(got) + 1 + len(extra)
    return pl.pallas_call(
        functools.partial(finish_kernel, out.shape, cells, len(got), len(extra), cases),
        in_specs=[SMEM] + [VMEM] * (nin - 1 + 3) + [HBM],
        out_specs=[HBM, SMEM],
        out_shape=[jax.ShapeDtypeStruct(out.shape, F32), jax.ShapeDtypeStruct((cases,), F32)],
        input_output_aliases={nin + 3: 0},
        scratch_shapes=[pltpu.VMEM((2, nx, 8, depth), F32), pltpu.SemaphoreType.DMA((2,))],
        compiler_params=pltpu.CompilerParams(vmem_limit_bytes=16 * MIB),
        name="finish",
    )(slots, *got, sums, *extra, first, last, factor, out)


def swap_pairs(count, first):
    return [q for i in range(first, count - 1, 2) for q in ((i, i + 1), (i + 1, i))]


def swaps_of(count):
    return min(count - 1, 2)


def xor_pairs(count, m):
    return [(i, i ^ m) for i in range(count)]


def shards(density, design_mask, energy, decay, case_index, case_weight):
    cases = energy.shape[0]
    nx, ny, depth = density.shape
    nz, gx, gy = (lax.axis_size(a) for a in ("gz", "gx", "gy"))
    iz, ix, iy = (lax.axis_index(a) for a in ("gz", "gx", "gy"))
    send, own, source = faces_call(density, design_mask, energy, decay, case_index, case_weight)
    if nz in (1, 2, 4):
        msgs = [lax.ppermute(send, "gz", xor_pairs(nz, m)) for m in range(1, nz)]
        order = [iz ^ j for j in range(nz)]
    else:
        every = lax.all_gather(send, "gz")
        msgs = [every[j] for j in range(nz)]
        order = [jnp.int32(j) for j in range(nz)]
    t_local, factor, umap = local_call(density, design_mask, source, decay, case_index, case_weight)
    flip_x, flip_y = ix % 2, iy % 2
    slots = jnp.stack([iz, (1 - flip_x) * (nx - RADIUS)] + order).astype(jnp.int32)
    if nz not in (1, 2, 4):
        own, msgs = msgs[0].astype(F32), msgs[1:]
    t, *x_sends = couple_call(slots, own, msgs, t_local, umap, max(swaps_of(gx), 1))
    x_got = [lax.ppermute(x_sends[k], "gx", swap_pairs(gx, k)) for k in range(swaps_of(gx))]
    marks = jnp.stack([iz, ix, flip_x, flip_y]).astype(jnp.int32)
    *y_sends, xb, xa, sums = edge_call(marks, t, x_got, x_sends[0], swaps_of(gy), cases)
    y_got = [lax.ppermute(y_sends[k], "gy", swap_pairs(gy, k)) for k in range(swaps_of(gy))]
    extra = [lax.ppermute(sums, "gy", xor_pairs(gy, m)) for m in range(1, gy)]
    partial, first, last = plane_call(t, xb, xa, factor)
    cells = nx * ny * depth * nz * gx * gy
    return tuple(finish_call(marks, y_got, sums, extra, first, last, factor, partial, float(cells), cases))


def solution(mesh):
    placed = (
        P("gx", "gy", "gz"),
        P("gx", "gy", "gz"),
        P(None, "gx", "gy", "gz"),
        P(None, "gz"),
        P(),
        P(),
    )
    return jax.shard_map(
        shards, mesh=mesh, in_specs=placed, out_specs=(P("gx", "gy", "gz"), P()), check_vma=False
    )
```

```python
import functools
import math
import jax
import jax.numpy as jnp
from jax import lax
from jax.experimental import pallas as pl
from jax.experimental.pallas import tpu as pltpu
from jax.sharding import PartitionSpec as P

RADIUS = 3
LANES = 128
MIB = 2**20
F32 = jnp.float32
BF16 = jnp.bfloat16
HIGH = lax.Precision.HIGHEST
HBM = pl.BlockSpec(memory_space=pltpu.HBM)
VMEM = pl.BlockSpec(memory_space=pltpu.VMEM)
SMEM = pl.BlockSpec(memory_space=pltpu.SMEM)


def in_hbm(*arrays):
    return [pltpu.with_memory_space_constraint(a, pltpu.HBM) for a in arrays]


def in_vmem(*arrays):
    return [pltpu.with_memory_space_constraint(a, pltpu.VMEM) for a in arrays]


def taps_1d():
    raw = [math.exp(-2.0 * k * k / (RADIUS * RADIUS)) for k in range(-RADIUS, RADIUS + 1)]
    total = sum(raw)
    return [r / total for r in raw]


def dot_high(a, b, dims=((1,), (0,))):
    return lax.dot_general(a, b, (dims, ((), ())), precision=HIGH, preferred_element_type=F32)


def split2(v):
    hi = v.astype(BF16)
    return hi, (v - hi.astype(F32)).astype(BF16)


def split3(v):
    a = v.astype(BF16).astype(F32)
    b = (v - a).astype(BF16).astype(F32)
    return a, b, v - a - b


def put_lanes(columns):
    rows = columns[0].shape[0]
    lane = lax.broadcasted_iota(jnp.int32, (rows, LANES), 1)
    out = jnp.zeros((rows, LANES), F32)
    for k, col in enumerate(columns):
        out = jnp.where(lane == k, col, out)
    return out


def pad_rows(v, rows):
    return jnp.concatenate([v, jnp.zeros((rows - v.shape[0],) + v.shape[1:], v.dtype)], axis=0)


def sum3(block, at):
    return block[:, at : at + 1] + block[:, at + 1 : at + 2] + block[:, at + 2 : at + 3]


class Slab:
    def __init__(self, decay):
        cases, depth = decay.shape
        self.decay = decay
        self.row = lax.broadcasted_iota(jnp.int32, (depth, depth), 0)
        self.col = lax.broadcasted_iota(jnp.int32, (depth, depth), 1)
        logs = jnp.log(decay)
        self.up = dot_high(logs, (self.row <= self.col).astype(F32))
        self.up_ex = self.up - logs
        wide = lambda v: jnp.transpose(pad_rows(v, 8))
        self.up_t = wide(self.up)
        self.up_ex_t = wide(self.up_ex)
        self.keep_t = wide(1.0 - decay)
        self.total = self.up[:, depth - 1 : depth]

    def forward_t(self, c):
        gap = self.up[c : c + 1, :] - self.up_t[:, c : c + 1]
        weight = jnp.exp(jnp.minimum(gap, 0.0)) * self.keep_t[:, c : c + 1]
        return jnp.where(self.col >= self.row, weight, 0.0)

    def backward_t(self, c):
        gap = self.up_ex_t[:, c : c + 1] - self.up_ex[c : c + 1, :]
        weight = jnp.exp(jnp.minimum(gap, 0.0)) * self.keep_t[:, c : c + 1]
        return jnp.where(self.col <= self.row, weight, 0.0)


def case_scale(weight_ref, index_ref, c):
    return -3.0 * weight_ref[index_ref[c]]


def faces_kernel(shape, bx, *refs):
    cases, nx, ny, depth = shape
    (index_hbm, weight_hbm, decay_hbm, density_hbm, mask_hbm, energy_hbm,
     send_ref, own_ref, source_ref,
     index_ref, weight_ref, decay_ref, density_ref, mask_ref, energy_ref, small_sem, sem) = refs
    steps, cols = nx // bx, bx * ny
    small = [
        pltpu.make_async_copy(decay_hbm, decay_ref, small_sem.at[0]),
        pltpu.make_async_copy(index_hbm, index_ref, small_sem.at[1]),
        pltpu.make_async_copy(weight_hbm, weight_ref, small_sem.at[2]),
    ]
    big = []
    for s in range(steps):
        at = pl.ds(s * bx, bx)
        big.append([
            pltpu.make_async_copy(density_hbm.at[at], density_ref.at[at], sem.at[0, s]),
            pltpu.make_async_copy(mask_hbm.at[at], mask_ref.at[at], sem.at[1, s]),
            pltpu.make_async_copy(energy_hbm.at[:, at], energy_ref.at[:, at], sem.at[2, s]),
        ])
    for copy in small:
        copy.start()
    for group in big:
        for copy in group:
            copy.start()
    for copy in small:
        copy.wait()

    decay = decay_ref[...]
    slab = Slab(decay)
    zero_row = jnp.zeros((1, depth), F32)
    e_rows, h_rows, turns = [], [], []
    for c in range(cases):
        scale = case_scale(weight_ref, index_ref, c)
        f_t = slab.forward_t(c)
        keep = 1.0 - decay[c : c + 1, :]
        e_row = jnp.exp(slab.total[c : c + 1] - slab.up[c : c + 1, :]) * keep
        b_row = jnp.exp(slab.up_ex[c : c + 1, :]) * keep
        h_row = dot_high(b_row, f_t, ((1,), (1,)))
        turns.append(jnp.sum(b_row * jnp.exp(slab.up[c : c + 1, :]), axis=1, keepdims=True))
        place = lambda r: jnp.concatenate([zero_row] * c + [r * scale] + [zero_row] * (cases - 1 - c), axis=1)
        e_rows.append(place(e_row))
        h_rows.append(place(h_row))
    w_hi, w_lo = split2(jnp.concatenate(e_rows + h_rows, axis=0))
    wmat = jnp.concatenate([w_hi, w_lo], axis=0)

    sums = [jnp.zeros((8, depth), F32) for _ in range(cases)]
    for s in range(steps):
        for copy in big[s]:
            copy.wait()
        at = pl.ds(s * bx, bx)
        mask = mask_ref[at]
        dense = jnp.where(mask == 1, 0.001, jnp.where(mask == 2, 1.0, density_ref[at]))
        cube = dense * dense * dense
        span = pl.ds(s * cols, cols)
        for c in range(cases):
            work = cube * energy_ref[c, at].astype(F32)
            sums[c] = sums[c] + jnp.sum(work.reshape(cols // 8, 8, depth), axis=0)
            source_ref[span, c * depth : (c + 1) * depth] = work.astype(BF16).reshape(cols, depth)
        faces = lax.dot_general(
            wmat, source_ref[span, :], (((1,), (1,)), ((), ())), preferred_element_type=F32)
        faces = faces[0 : 2 * cases] + faces[2 * cases : 4 * cases]
        own_ref[:, span] = faces
        send_ref[:, span] = faces.astype(BF16)

    total = jnp.concatenate([jnp.sum(jnp.sum(v, axis=0, keepdims=True), axis=1, keepdims=True) for v in sums], axis=0)
    turn = jnp.concatenate(turns, axis=0)
    aux = put_lanes(split3(jnp.exp(slab.total)) + split3(turn) + split3(total))
    aux = pad_rows(aux, 2 * cases)
    tail = pl.ds(nx * ny, LANES)
    own_ref[:, tail] = aux
    send_ref[:, tail] = aux.astype(BF16)


def faces_call(density, design_mask, energy, decay, case_index, case_weight):
    cases, nx, ny, depth = energy.shape
    bx = 8
    width = nx * ny + LANES
    return pl.pallas_call(
        functools.partial(faces_kernel, energy.shape, bx),
        in_specs=[HBM] * 6,
        out_specs=[VMEM] * 3,
        out_shape=[
            pltpu.VMEM((2 * cases, width), BF16),
            pltpu.VMEM((2 * cases, width), F32),
            pltpu.VMEM((nx * ny, cases * depth), BF16),
        ],
        scratch_shapes=[
            pltpu.SMEM(case_index.shape, case_index.dtype),
            pltpu.SMEM(case_weight.shape, F32),
            pltpu.VMEM(decay.shape, F32),
            pltpu.VMEM(density.shape, F32),
            pltpu.VMEM(density.shape, jnp.int32),
            pltpu.VMEM(energy.shape, BF16),
            pltpu.SemaphoreType.DMA((3,)),
            pltpu.SemaphoreType.DMA((3, nx // bx)),
        ],
        compiler_params=pltpu.CompilerParams(vmem_limit_bytes=20 * MIB),
        name="faces",
    )(*in_hbm(case_index, case_weight, decay, density, design_mask, energy))


def local_kernel(shape, bx, *refs):
    cases, nx, ny, depth = shape
    (index_hbm, weight_hbm, decay_hbm, density_hbm, mask_hbm, source_ref,
     t_ref, factor_ref, umap_ref,
     index_ref, weight_ref, decay_ref, mask_ref, rmat, small_sem, sem) = refs
    steps, cols = nx // bx, bx * ny
    small = [
        pltpu.make_async_copy(decay_hbm, decay_ref, small_sem.at[0]),
        pltpu.make_async_copy(index_hbm, index_ref, small_sem.at[1]),
        pltpu.make_async_copy(weight_hbm, weight_ref, small_sem.at[2]),
    ]
    big = [
        pltpu.make_async_copy(density_hbm, factor_ref, sem.at[0]),
        pltpu.make_async_copy(mask_hbm, mask_ref, sem.at[1]),
    ]
    for copy in small + big:
        copy.start()
    for copy in small:
        copy.wait()
    slab = Slab(decay_ref[...])
    a_rows, c_rows = [], []
    for c in range(cases):
        f_t, b_t = slab.forward_t(c), slab.backward_t(c)
        hi, lo = split2(dot_high(f_t, b_t) * case_scale(weight_ref, index_ref, c))
        rmat[c * depth : (c + 1) * depth, 0:depth] = hi
        rmat[c * depth : (c + 1) * depth, depth : 2 * depth] = lo
        a_rows.append(dot_high(jnp.exp(slab.up[c : c + 1, :]), b_t))
        c_rows.append(jnp.exp(slab.total[c : c + 1] - slab.up_ex[c : c + 1, :]))
    u_all = jnp.concatenate(a_rows + c_rows, axis=0)
    u_hi = u_all.astype(BF16).astype(F32)
    umap_ref[...] = jnp.concatenate([u_hi, u_hi, u_all - u_hi, jnp.zeros_like(u_hi)], axis=0).astype(BF16)
    for copy in big:
        copy.wait()

    def one(s, carry):
        span = pl.ds(pl.multiple_of(s * cols, cols), cols)
        both = lax.dot_general(
            source_ref[span, :], rmat[...], (((1,), (0,)), ((), ())), preferred_element_type=F32)
        at = pl.ds(s * bx, bx)
        t_ref[at] = (both[:, 0:depth] + both[:, depth : 2 * depth]).reshape(bx, ny, depth)
        factor_ref[at] = jnp.where(mask_ref[at] == 0, 1.0 / jnp.maximum(factor_ref[at], 0.1), 0.0)
        return carry

    lax.fori_loop(0, steps, one, 0)


def local_call(density, design_mask, source, decay, case_index, case_weight):
    nx, ny, depth = density.shape
    cases = decay.shape[0]
    return pl.pallas_call(
        functools.partial(local_kernel, (cases, nx, ny, depth), 8),
        in_specs=[HBM] * 5 + [VMEM],
        out_specs=[VMEM] * 3,
        out_shape=[
            pltpu.VMEM(density.shape, F32),
            pltpu.VMEM(density.shape, F32),
            pltpu.VMEM((8 * cases, depth), BF16),
        ],
        scratch_shapes=[
            pltpu.SMEM(case_index.shape, case_index.dtype),
            pltpu.SMEM(case_weight.shape, F32),
            pltpu.VMEM(decay.shape, F32),
            pltpu.VMEM(density.shape, jnp.int32),
            pltpu.VMEM((cases * depth, 2 * depth), BF16),
            pltpu.SemaphoreType.DMA((3,)),
            pltpu.SemaphoreType.DMA((2,)),
        ],
        compiler_params=pltpu.CompilerParams(vmem_limit_bytes=20 * MIB),
        name="local",
    )(*in_hbm(case_index, case_weight, decay, density, design_mask), *in_vmem(source))


def couple_kernel(shape, nslabs, nsends, swapped, *refs):
    cases, nx, ny, depth = shape
    own_ref = refs[0]
    msgs = refs[1:nslabs]
    t_ref, umap_ref, out_ref = refs[nslabs : 3 + nslabs]
    sends = refs[3 + nslabs : 3 + nslabs + nsends]
    stack = refs[-1]
    cols = nx * ny
    mine = lax.axis_index("gz")
    high = (1 - lax.axis_index("gx") % 2) * (nx - RADIUS)
    stack[0] = own_ref[...].astype(F32)
    for m, msg in enumerate(msgs):
        stack[m + 1] = msg[...].astype(F32)
    total = jnp.zeros((cases, 1), F32)
    for m in range(nslabs):
        total = total + sum3(stack[m, 0:cases, cols : cols + LANES], 6)
    state = jnp.zeros((cases, cols), F32)
    entering, above = state, state
    tops, gains = [], []
    for j in range(nslabs):
        at = mine ^ j if swapped else j
        aux = stack[at, 0:cases, cols : cols + LANES]
        gains.append(sum3(aux, 0))
        entering = jnp.where(mine == j, state, entering)
        tops.append(stack[at, cases : 2 * cases, 0:cols] + sum3(aux, 3) * state)
        state = gains[j] * state + stack[at, 0:cases, 0:cols]
    state = jnp.zeros((cases, cols), F32)
    for j in reversed(range(nslabs)):
        above = jnp.where(mine == j, state, above)
        state = tops[j] + gains[j] * state
    faces = jnp.concatenate([entering, above], axis=0)
    hi = faces.astype(BF16).astype(F32)
    lhs = jnp.concatenate([hi, faces - hi, hi, jnp.zeros_like(hi)], axis=0).astype(BF16)
    add = lax.dot_general(lhs, umap_ref[...], (((0,), (0,)), ((), ())), preferred_element_type=F32)
    out_ref[...] = t_ref[...] + add.reshape(nx, ny, depth)
    aux = pad_rows(put_lanes(split3(total)), 16).astype(BF16)
    for k, ref in enumerate(sends):
        edge = out_ref[pl.ds(high if k == 0 else nx - RADIUS - high, RADIUS)]
        ref[0 : RADIUS * ny, :] = edge.reshape(RADIUS * ny, depth).astype(BF16)
        ref[RADIUS * ny :, :] = aux


def couple_call(own, msgs, t_local, umap, nsends, swapped):
    nx, ny, depth = t_local.shape
    cases = own.shape[0] // 2
    nslabs = len(msgs) + 1
    return pl.pallas_call(
        functools.partial(couple_kernel, (cases, nx, ny, depth), nslabs, nsends, swapped),
        in_specs=[VMEM] * (nslabs + 2),
        out_specs=[VMEM] * (1 + nsends),
        out_shape=[jax.ShapeDtypeStruct(t_local.shape, F32)]
        + [jax.ShapeDtypeStruct((RADIUS * ny + 16, depth), BF16)] * nsends,
        scratch_shapes=[pltpu.VMEM((nslabs,) + own.shape, F32)],
        compiler_params=pltpu.CompilerParams(vmem_limit_bytes=28 * MIB),
        name="couple",
    )(own, *msgs, *in_vmem(t_local), umap)


def sided(even, got):
    a = got[0]
    b = got[1] if len(got) > 1 else jnp.zeros_like(a)
    return jnp.where(even, b, a), jnp.where(even, a, b)


def edge_kernel(shape, nx_sends, ny_sends, *refs):
    cases, nx, ny, depth = shape
    t_ref = refs[0]
    got_refs = refs[1 : 1 + nx_sends]
    own_send = refs[1 + nx_sends]
    sends = refs[2 + nx_sends : 2 + nx_sends + ny_sends]
    xb_ref, xa_ref, sums_ref, line = refs[2 + nx_sends + ny_sends :]
    taps = taps_1d()
    edge = RADIUS * ny
    even_x = lax.axis_index("gx") % 2 == 0
    flip_y = lax.axis_index("gy") % 2 == 1
    blocks = [r[0:edge, :].astype(F32) for r in got_refs]
    before, after = sided(even_x, blocks)
    xb_ref[...] = before
    xa_ref[...] = after
    total = sum3(own_send[edge : edge + 16, :].astype(F32), 0)
    for ref in got_refs:
        total = total + sum3(ref[edge : edge + 16, :].astype(F32), 0)
    sums_ref[...] = jnp.broadcast_to(total[0:8], (8, LANES))
    aux = put_lanes(split3(total)).astype(BF16)
    flat = t_ref.reshape(nx * ny, depth)
    columns = []
    for k in range(2 * RADIUS):
        y = k if k < RADIUS else ny - 2 * RADIUS + k
        line[8 : 8 + nx, :] = flat[pl.ds(y, nx, stride=ny), :]
        line[8 - RADIUS : 8, :] = xb_ref[pl.ds(y, RADIUS, stride=ny), :]
        line[8 + nx : 8 + nx + RADIUS, :] = xa_ref[pl.ds(y, RADIUS, stride=ny), :]
        acc = taps[RADIUS] * line[8 : 8 + nx, :]
        for d in range(1, RADIUS + 1):
            acc = acc + taps[RADIUS + d] * (line[8 - d : 8 - d + nx, :] + line[8 + d : 8 + d + nx, :])
        columns.append(acc)
    for m, ref in enumerate(sends):
        for k in range(RADIUS):
            first, last = columns[k], columns[RADIUS + k]
            pick = jnp.where(flip_y == (m == 0), first, last)
            ref[k * nx : (k + 1) * nx, :] = pick.astype(BF16)
        ref[RADIUS * nx :, :] = aux


def edge_call(t, got, own_send, ny_sends, cases):
    nx, ny, depth = t.shape
    return pl.pallas_call(
        functools.partial(edge_kernel, (cases, nx, ny, depth), len(got), ny_sends),
        in_specs=[VMEM] * (2 + len(got)),
        out_specs=[VMEM] * (ny_sends + 3),
        out_shape=[jax.ShapeDtypeStruct((RADIUS * nx + 16, depth), BF16)] * ny_sends
        + [jax.ShapeDtypeStruct((RADIUS * ny, depth), F32)] * 2
        + [jax.ShapeDtypeStruct((8, LANES), F32)],
        scratch_shapes=[pltpu.VMEM((nx + 16, depth), F32)],
        compiler_params=pltpu.CompilerParams(vmem_limit_bytes=16 * MIB),
        name="edge",
    )(t, *got, own_send)


def plane_kernel(shape, bx, *refs):
    nx, ny, depth = shape
    (t_ref, xb_ref, xa_ref, factor_ref, out_hbm, first_ref, last_ref,
     pad, line, out_ref, sem) = refs
    taps = taps_1d()
    steps = nx // bx
    pad[0:RADIUS] = xb_ref[...].reshape(RADIUS, ny, depth)
    pad[RADIUS : 2 * RADIUS] = t_ref[0:RADIUS]
    pad[2 * RADIUS : 3 * RADIUS] = t_ref[RADIUS : 2 * RADIUS]
    tail = 3 * RADIUS
    pad[tail : tail + 2 * RADIUS] = t_ref[nx - 2 * RADIUS : nx]
    pad[tail + 2 * RADIUS :] = xa_ref[...].reshape(RADIUS, ny, depth)
    zeros = jnp.zeros((8, depth), F32)
    for slot in range(2):
        line[slot, 0:8, :] = zeros
        line[slot, 8 + ny :, :] = zeros

    def row(ref, x, at, slot):
        acc = taps[RADIUS] * ref[at]
        for d in range(1, RADIUS + 1):
            acc = acc + taps[RADIUS + d] * (ref[at - d] + ref[at + d])
        line[slot, 8 : 8 + ny, :] = acc
        res = taps[RADIUS] * acc
        for d in range(1, RADIUS + 1):
            res = res + taps[RADIUS + d] * (line[slot, 8 - d : 8 - d + ny, :] + line[slot, 8 + d : 8 + d + ny, :])
        res = res * factor_ref[x]
        out_ref[x] = res
        first_ref[x] = res[0:8]
        last_ref[x] = res[ny - 8 : ny]

    copies = [
        pltpu.make_async_copy(out_ref.at[pl.ds(s * bx, bx)], out_hbm.at[pl.ds(s * bx, bx)], sem.at[s])
        for s in range(steps)
    ]
    for s in range(steps):
        lo, hi = s * bx, (s + 1) * bx
        if s == 0:
            for x in range(RADIUS):
                row(pad, x, x + RADIUS, x % 2)
            lo = RADIUS
        if s == steps - 1:
            for x in range(nx - RADIUS, nx):
                row(pad, x, x - (nx - RADIUS) + tail + RADIUS, x % 2)
            hi = nx - RADIUS

        def pair(i, carry):
            row(t_ref, i, i, i % 2)
            return carry

        lax.fori_loop(lo, hi, pair, 0)
        copies[s].start()
    for copy in copies:
        copy.wait()


def plane_call(t, xb, xa, factor):
    nx, ny, depth = t.shape
    bx = 8
    return pl.pallas_call(
        functools.partial(plane_kernel, t.shape, bx),
        in_specs=[VMEM] * 4,
        out_specs=[HBM, VMEM, VMEM],
        out_shape=[
            jax.ShapeDtypeStruct(t.shape, F32),
            jax.ShapeDtypeStruct((nx, 8, depth), F32),
            jax.ShapeDtypeStruct((nx, 8, depth), F32),
        ],
        scratch_shapes=[
            pltpu.VMEM((7 * RADIUS - RADIUS, ny, depth), F32),
            pltpu.VMEM((2, ny + 16, depth), F32),
            pltpu.VMEM(t.shape, F32),
            pltpu.SemaphoreType.DMA((nx // bx,)),
        ],
        compiler_params=pltpu.CompilerParams(vmem_limit_bytes=20 * MIB),
        name="plane",
    )(*in_vmem(t, xb, xa, factor))


def finish_kernel(shape, cells, ngot, nextra, cases, *refs):
    nx, ny, depth = shape
    got_refs = refs[:ngot]
    sums_ref = refs[ngot]
    extra_refs = refs[1 + ngot : 1 + ngot + nextra]
    first_ref, last_ref, factor_ref, _, out_hbm, comp_ref, strip, sem = refs[1 + ngot + nextra :]
    taps = taps_1d()
    edge = RADIUS * nx
    even_y = lax.axis_index("gy") % 2 == 0
    blocks = [r[0:edge, :].astype(F32) for r in got_refs]
    before, after = sided(even_y, blocks) if blocks else (jnp.zeros((edge, depth), F32),) * 2
    flat = factor_ref.reshape(nx * ny, depth)
    for ref, side in ((first_ref, 0), (last_ref, 1)):
        strip[side] = ref[...]
        view = strip.at[side].reshape(nx * 8, depth)
        for y in range(RADIUS):
            add = jnp.zeros((nx, depth), F32)
            for k in range(RADIUS):
                if side == 0:
                    d, halo, own = y + RADIUS - k, before[k * nx : (k + 1) * nx], y
                else:
                    d, halo, own = k + 1 + RADIUS - 1 - y, after[k * nx : (k + 1) * nx], ny - RADIUS + y
                if d <= RADIUS:
                    add = add + taps[RADIUS + d] * halo
            at = own if side == 0 else own - (ny - 8)
            view[pl.ds(at, nx, stride=8), :] += flat[pl.ds(own, nx, stride=ny), :] * add
    copies = [
        pltpu.make_async_copy(strip.at[0], out_hbm.at[:, 0:8, :], sem.at[0]),
        pltpu.make_async_copy(strip.at[1], out_hbm.at[:, ny - 8 : ny, :], sem.at[1]),
    ]
    for copy in copies:
        copy.start()
    total = sums_ref[...]
    for ref in extra_refs:
        total = total + ref[...]
    for c in range(cases):
        comp_ref[c] = total[c, 0] / cells
    for copy in copies:
        copy.wait()


def finish_call(got, sums, extra, first, last, factor, out, cells, cases):
    nx, ny, depth = out.shape
    nin = len(got) + 1 + len(extra)
    return pl.pallas_call(
        functools.partial(finish_kernel, out.shape, cells, len(got), len(extra), cases),
        in_specs=[VMEM] * (nin + 3) + [HBM],
        out_specs=[HBM, SMEM],
        out_shape=[jax.ShapeDtypeStruct(out.shape, F32), jax.ShapeDtypeStruct((cases,), F32)],
        input_output_aliases={nin + 3: 0},
        scratch_shapes=[pltpu.VMEM((2, nx, 8, depth), F32), pltpu.SemaphoreType.DMA((2,))],
        compiler_params=pltpu.CompilerParams(vmem_limit_bytes=16 * MIB),
        name="finish",
    )(*got, sums, *extra, *in_vmem(first, last, factor), *in_hbm(out))


def swap_pairs(count, first):
    return [q for i in range(first, count - 1, 2) for q in ((i, i + 1), (i + 1, i))]


def swaps_of(count):
    return min(count - 1, 2)


def xor_pairs(count, m):
    return [(i, i ^ m) for i in range(count)]


def shards(density, design_mask, energy, decay, case_index, case_weight):
    cases = energy.shape[0]
    nx, ny, depth = density.shape
    nz, gx, gy = (lax.axis_size(a) for a in ("gz", "gx", "gy"))
    send, own, source = faces_call(density, design_mask, energy, decay, case_index, case_weight)
    swapped = nz in (1, 2, 4)
    if swapped:
        msgs = [lax.ppermute(send, "gz", xor_pairs(nz, m)) for m in range(1, nz)]
    else:
        every = lax.all_gather(send, "gz")
        own, *msgs = [every[j] for j in range(nz)]
    t_local, factor, umap = local_call(density, design_mask, source, decay, case_index, case_weight)
    t, *x_sends = couple_call(own, msgs, t_local, umap, max(swaps_of(gx), 1), swapped)
    x_got = [lax.ppermute(x_sends[k], "gx", swap_pairs(gx, k)) for k in range(swaps_of(gx))]
    *y_sends, xb, xa, sums = edge_call(t, x_got, x_sends[0], swaps_of(gy), cases)
    y_got = [lax.ppermute(y_sends[k], "gy", swap_pairs(gy, k)) for k in range(swaps_of(gy))]
    extra = [lax.ppermute(sums, "gy", xor_pairs(gy, m)) for m in range(1, gy)]
    partial, first, last = plane_call(t, xb, xa, factor)
    cells = nx * ny * depth * nz * gx * gy
    return tuple(finish_call(y_got, sums, extra, first, last, factor, partial, float(cells), cases))


def solution(mesh):
    placed = (
        P("gx", "gy", "gz"),
        P("gx", "gy", "gz"),
        P(None, "gx", "gy", "gz"),
        P(None, "gz"),
        P(),
        P(),
    )
    return jax.shard_map(
        shards, mesh=mesh, in_specs=placed, out_specs=(P("gx", "gy", "gz"), P()), check_vma=False
    )
```

```python
import functools
import math
import jax
import jax.numpy as jnp
from jax import lax
from jax.experimental import pallas as pl
from jax.experimental.pallas import tpu as pltpu
from jax.sharding import PartitionSpec as P

RADIUS = 3
AHEAD = 2
LANES = 128
MIB = 2**20
F32 = jnp.float32
BF16 = jnp.bfloat16
HIGH = lax.Precision.HIGHEST
HBM = pl.BlockSpec(memory_space=pltpu.HBM)
VMEM = pl.BlockSpec(memory_space=pltpu.VMEM)
SMEM = pl.BlockSpec(memory_space=pltpu.SMEM)


def in_hbm(*arrays):
    return [pltpu.with_memory_space_constraint(a, pltpu.HBM) for a in arrays]


def in_vmem(*arrays):
    return [pltpu.with_memory_space_constraint(a, pltpu.VMEM) for a in arrays]


def taps_1d():
    raw = [math.exp(-2.0 * k * k / (RADIUS * RADIUS)) for k in range(-RADIUS, RADIUS + 1)]
    total = sum(raw)
    return [r / total for r in raw]


def dot_high(a, b, dims=((1,), (0,))):
    return lax.dot_general(a, b, (dims, ((), ())), precision=HIGH, preferred_element_type=F32)


def split2(v):
    hi = v.astype(BF16)
    return hi, (v - hi.astype(F32)).astype(BF16)


def split3(v):
    a = v.astype(BF16).astype(F32)
    b = (v - a).astype(BF16).astype(F32)
    return a, b, v - a - b


def put_lanes(columns):
    rows = columns[0].shape[0]
    lane = lax.broadcasted_iota(jnp.int32, (rows, LANES), 1)
    out = jnp.zeros((rows, LANES), F32)
    for k, col in enumerate(columns):
        out = jnp.where(lane == k, col, out)
    return out


def pad_rows(v, rows):
    return jnp.concatenate([v, jnp.zeros((rows - v.shape[0],) + v.shape[1:], v.dtype)], axis=0)


def sum3(block, at):
    return block[:, at : at + 1] + block[:, at + 1 : at + 2] + block[:, at + 2 : at + 3]


class Slab:
    def __init__(self, decay):
        cases, depth = decay.shape
        self.decay = decay
        self.row = lax.broadcasted_iota(jnp.int32, (depth, depth), 0)
        self.col = lax.broadcasted_iota(jnp.int32, (depth, depth), 1)
        logs = jnp.log(decay)
        self.up = dot_high(logs, (self.row <= self.col).astype(F32))
        self.up_ex = self.up - logs
        wide = lambda v: jnp.transpose(pad_rows(v, 8))
        self.up_t = wide(self.up)
        self.up_ex_t = wide(self.up_ex)
        self.keep_t = wide(1.0 - decay)
        self.total = self.up[:, depth - 1 : depth]

    def forward_t(self, c):
        gap = self.up[c : c + 1, :] - self.up_t[:, c : c + 1]
        weight = jnp.exp(jnp.minimum(gap, 0.0)) * self.keep_t[:, c : c + 1]
        return jnp.where(self.col >= self.row, weight, 0.0)

    def backward_t(self, c):
        gap = self.up_ex_t[:, c : c + 1] - self.up_ex[c : c + 1, :]
        weight = jnp.exp(jnp.minimum(gap, 0.0)) * self.keep_t[:, c : c + 1]
        return jnp.where(self.col <= self.row, weight, 0.0)


def case_scale(weight_ref, index_ref, c):
    return -3.0 * weight_ref[index_ref[c]]


def faces_kernel(shape, bx, *refs):
    cases, nx, ny, depth = shape
    (index_hbm, weight_hbm, decay_hbm, density_hbm, mask_hbm, energy_hbm,
     send_ref, own_ref, source_ref,
     index_ref, weight_ref, decay_ref, density_ref, mask_ref, energy_ref, small_sem, sem) = refs
    steps, cols = nx // bx, bx * ny
    small = [
        pltpu.make_async_copy(decay_hbm, decay_ref, small_sem.at[0]),
        pltpu.make_async_copy(index_hbm, index_ref, small_sem.at[1]),
        pltpu.make_async_copy(weight_hbm, weight_ref, small_sem.at[2]),
    ]
    big = []
    for s in range(steps):
        at = pl.ds(s * bx, bx)
        big.append([
            pltpu.make_async_copy(density_hbm.at[at], density_ref.at[at], sem.at[0, s]),
            pltpu.make_async_copy(mask_hbm.at[at], mask_ref.at[at], sem.at[1, s]),
            pltpu.make_async_copy(energy_hbm.at[:, at], energy_ref.at[:, at], sem.at[2, s]),
        ])
    for copy in small:
        copy.start()
    for group in big[:AHEAD]:
        for copy in group:
            copy.start()
    for copy in small:
        copy.wait()

    decay = decay_ref[...]
    slab = Slab(decay)
    for group in big[AHEAD : AHEAD + 1]:
        for copy in group:
            copy.start()
    zero_row = jnp.zeros((1, depth), F32)
    e_rows, h_rows, turns = [], [], []
    for c in range(cases):
        scale = case_scale(weight_ref, index_ref, c)
        f_t = slab.forward_t(c)
        keep = 1.0 - decay[c : c + 1, :]
        e_row = jnp.exp(slab.total[c : c + 1] - slab.up[c : c + 1, :]) * keep
        b_row = jnp.exp(slab.up_ex[c : c + 1, :]) * keep
        h_row = dot_high(b_row, f_t, ((1,), (1,)))
        turns.append(jnp.sum(b_row * jnp.exp(slab.up[c : c + 1, :]), axis=1, keepdims=True))
        place = lambda r: jnp.concatenate([zero_row] * c + [r * scale] + [zero_row] * (cases - 1 - c), axis=1)
        e_rows.append(place(e_row))
        h_rows.append(place(h_row))
    w_hi, w_lo = split2(jnp.concatenate(e_rows + h_rows, axis=0))
    wmat = jnp.concatenate([w_hi, w_lo], axis=0)

    sums = [jnp.zeros((8, depth), F32) for _ in range(cases)]

    def faces_of(s):
        span = pl.ds(s * cols, cols)
        faces = lax.dot_general(
            wmat, source_ref[span, :], (((1,), (1,)), ((), ())), preferred_element_type=F32)
        faces = faces[0 : 2 * cases] + faces[2 * cases : 4 * cases]
        own_ref[:, span] = faces
        send_ref[:, span] = faces.astype(BF16)

    for s in range(steps):
        for copy in big[s]:
            copy.wait()
        for group in big[s + AHEAD + 1 : s + AHEAD + 2]:
            for copy in group:
                copy.start()
        at = pl.ds(s * bx, bx)
        mask = mask_ref[at]
        dense = jnp.where(mask == 1, 0.001, jnp.where(mask == 2, 1.0, density_ref[at]))
        cube = dense * dense * dense
        span = pl.ds(s * cols, cols)
        for c in range(cases):
            work = cube * energy_ref[c, at].astype(F32)
            sums[c] = sums[c] + jnp.sum(work.reshape(cols // 8, 8, depth), axis=0)
            source_ref[span, c * depth : (c + 1) * depth] = work.astype(BF16).reshape(cols, depth)
        if s > 0:
            faces_of(s - 1)
    faces_of(steps - 1)

    total = jnp.concatenate([jnp.sum(jnp.sum(v, axis=0, keepdims=True), axis=1, keepdims=True) for v in sums], axis=0)
    turn = jnp.concatenate(turns, axis=0)
    aux = put_lanes(split3(jnp.exp(slab.total)) + split3(turn) + split3(total))
    aux = pad_rows(aux, 2 * cases)
    tail = pl.ds(nx * ny, LANES)
    own_ref[:, tail] = aux
    send_ref[:, tail] = aux.astype(BF16)


def faces_call(density, design_mask, energy, decay, case_index, case_weight):
    cases, nx, ny, depth = energy.shape
    bx = 16
    width = nx * ny + LANES
    return pl.pallas_call(
        functools.partial(faces_kernel, energy.shape, bx),
        in_specs=[HBM] * 6,
        out_specs=[VMEM] * 3,
        out_shape=[
            pltpu.VMEM((2 * cases, width), BF16),
            pltpu.VMEM((2 * cases, width), F32),
            pltpu.VMEM((nx * ny, cases * depth), BF16),
        ],
        scratch_shapes=[
            pltpu.SMEM(case_index.shape, case_index.dtype),
            pltpu.SMEM(case_weight.shape, F32),
            pltpu.VMEM(decay.shape, F32),
            pltpu.VMEM(density.shape, F32),
            pltpu.VMEM(density.shape, jnp.int32),
            pltpu.VMEM(energy.shape, BF16),
            pltpu.SemaphoreType.DMA((3,)),
            pltpu.SemaphoreType.DMA((3, nx // bx)),
        ],
        compiler_params=pltpu.CompilerParams(vmem_limit_bytes=20 * MIB),
        name="faces",
    )(*in_hbm(case_index, case_weight, decay, density, design_mask, energy))


def local_kernel(shape, bx, *refs):
    cases, nx, ny, depth = shape
    (index_hbm, weight_hbm, decay_hbm, density_hbm, mask_hbm, source_ref,
     t_ref, factor_ref, umap_ref,
     index_ref, weight_ref, decay_ref, mask_ref, rmat, small_sem, sem) = refs
    steps, cols = nx // bx, bx * ny
    small = [
        pltpu.make_async_copy(decay_hbm, decay_ref, small_sem.at[0]),
        pltpu.make_async_copy(index_hbm, index_ref, small_sem.at[1]),
        pltpu.make_async_copy(weight_hbm, weight_ref, small_sem.at[2]),
    ]
    big = [
        pltpu.make_async_copy(density_hbm, factor_ref, sem.at[0]),
        pltpu.make_async_copy(mask_hbm, mask_ref, sem.at[1]),
    ]
    for copy in small + big:
        copy.start()
    for copy in small:
        copy.wait()
    slab = Slab(decay_ref[...])
    a_rows, c_rows = [], []
    for c in range(cases):
        f_t, b_t = slab.forward_t(c), slab.backward_t(c)
        hi, lo = split2(dot_high(f_t, b_t) * case_scale(weight_ref, index_ref, c))
        rmat[c * depth : (c + 1) * depth, 0:depth] = hi
        rmat[c * depth : (c + 1) * depth, depth : 2 * depth] = lo
        a_rows.append(dot_high(jnp.exp(slab.up[c : c + 1, :]), b_t))
        c_rows.append(jnp.exp(slab.total[c : c + 1] - slab.up_ex[c : c + 1, :]))
    u_all = jnp.concatenate(a_rows + c_rows, axis=0)
    u_hi = u_all.astype(BF16).astype(F32)
    umap_ref[...] = jnp.concatenate([u_hi, u_hi, u_all - u_hi, jnp.zeros_like(u_hi)], axis=0).astype(BF16)
    for copy in big:
        copy.wait()

    def one(s, carry):
        span = pl.ds(pl.multiple_of(s * cols, cols), cols)
        both = lax.dot_general(
            source_ref[span, :], rmat[...], (((1,), (0,)), ((), ())), preferred_element_type=F32)
        at = pl.ds(s * bx, bx)
        t_ref[at] = (both[:, 0:depth] + both[:, depth : 2 * depth]).reshape(bx, ny, depth)
        factor_ref[at] = jnp.where(mask_ref[at] == 0, 1.0 / jnp.maximum(factor_ref[at], 0.1), 0.0)
        return carry

    lax.fori_loop(0, steps, one, 0)


def local_call(density, design_mask, source, decay, case_index, case_weight):
    nx, ny, depth = density.shape
    cases = decay.shape[0]
    return pl.pallas_call(
        functools.partial(local_kernel, (cases, nx, ny, depth), 8),
        in_specs=[HBM] * 5 + [VMEM],
        out_specs=[VMEM] * 3,
        out_shape=[
            pltpu.VMEM(density.shape, F32),
            pltpu.VMEM(density.shape, F32),
            pltpu.VMEM((8 * cases, depth), BF16),
        ],
        scratch_shapes=[
            pltpu.SMEM(case_index.shape, case_index.dtype),
            pltpu.SMEM(case_weight.shape, F32),
            pltpu.VMEM(decay.shape, F32),
            pltpu.VMEM(density.shape, jnp.int32),
            pltpu.VMEM((cases * depth, 2 * depth), BF16),
            pltpu.SemaphoreType.DMA((3,)),
            pltpu.SemaphoreType.DMA((2,)),
        ],
        compiler_params=pltpu.CompilerParams(vmem_limit_bytes=20 * MIB),
        name="local",
    )(*in_hbm(case_index, case_weight, decay, density, design_mask), *in_vmem(source))


def couple_kernel(shape, nslabs, nsends, swapped, *refs):
    cases, nx, ny, depth = shape
    own_ref = refs[0]
    msgs = refs[1:nslabs]
    t_ref, umap_ref, out_ref = refs[nslabs : 3 + nslabs]
    sends = refs[3 + nslabs : 3 + nslabs + nsends]
    stack = refs[-1]
    cols = nx * ny
    mine = lax.axis_index("gz")
    high = (1 - lax.axis_index("gx") % 2) * (nx - RADIUS)
    stack[0] = own_ref[...].astype(F32)
    for m, msg in enumerate(msgs):
        stack[m + 1] = msg[...].astype(F32)
    total = jnp.zeros((cases, 1), F32)
    for m in range(nslabs):
        total = total + sum3(stack[m, 0:cases, cols : cols + LANES], 6)
    state = jnp.zeros((cases, cols), F32)
    entering, above = state, state
    tops, gains = [], []
    for j in range(nslabs):
        at = mine ^ j if swapped else j
        aux = stack[at, 0:cases, cols : cols + LANES]
        gains.append(sum3(aux, 0))
        entering = jnp.where(mine == j, state, entering)
        tops.append(stack[at, cases : 2 * cases, 0:cols] + sum3(aux, 3) * state)
        state = gains[j] * state + stack[at, 0:cases, 0:cols]
    state = jnp.zeros((cases, cols), F32)
    for j in reversed(range(nslabs)):
        above = jnp.where(mine == j, state, above)
        state = tops[j] + gains[j] * state
    faces = jnp.concatenate([entering, above], axis=0)
    hi = faces.astype(BF16).astype(F32)
    lhs = jnp.concatenate([hi, faces - hi, hi, jnp.zeros_like(hi)], axis=0).astype(BF16)
    add = lax.dot_general(lhs, umap_ref[...], (((0,), (0,)), ((), ())), preferred_element_type=F32)
    out_ref[...] = t_ref[...] + add.reshape(nx, ny, depth)
    aux = pad_rows(put_lanes(split3(total)), 16).astype(BF16)
    for k, ref in enumerate(sends):
        edge = out_ref[pl.ds(high if k == 0 else nx - RADIUS - high, RADIUS)]
        ref[0 : RADIUS * ny, :] = edge.reshape(RADIUS * ny, depth).astype(BF16)
        ref[RADIUS * ny :, :] = aux


def couple_call(own, msgs, t_local, umap, nsends, swapped):
    nx, ny, depth = t_local.shape
    cases = own.shape[0] // 2
    nslabs = len(msgs) + 1
    return pl.pallas_call(
        functools.partial(couple_kernel, (cases, nx, ny, depth), nslabs, nsends, swapped),
        in_specs=[VMEM] * (nslabs + 2),
        out_specs=[VMEM] * (1 + nsends),
        out_shape=[jax.ShapeDtypeStruct(t_local.shape, F32)]
        + [jax.ShapeDtypeStruct((RADIUS * ny + 16, depth), BF16)] * nsends,
        scratch_shapes=[pltpu.VMEM((nslabs,) + own.shape, F32)],
        compiler_params=pltpu.CompilerParams(vmem_limit_bytes=28 * MIB),
        name="couple",
    )(own, *msgs, *in_vmem(t_local), umap)


def sided(even, got):
    a = got[0]
    b = got[1] if len(got) > 1 else jnp.zeros_like(a)
    return jnp.where(even, b, a), jnp.where(even, a, b)


def edge_kernel(shape, nx_sends, ny_sends, *refs):
    cases, nx, ny, depth = shape
    t_ref = refs[0]
    got_refs = refs[1 : 1 + nx_sends]
    own_send = refs[1 + nx_sends]
    sends = refs[3 + nx_sends : 3 + nx_sends + ny_sends]
    xb_ref, xa_ref, sums_ref, line = refs[3 + nx_sends + ny_sends :]
    taps = taps_1d()
    edge = RADIUS * ny
    even_x = lax.axis_index("gx") % 2 == 0
    flip_y = lax.axis_index("gy") % 2 == 1
    blocks = [r[0:edge, :].astype(F32) for r in got_refs]
    before, after = sided(even_x, blocks)
    xb_ref[...] = before
    xa_ref[...] = after
    total = sum3(own_send[edge : edge + 16, :].astype(F32), 0)
    for ref in got_refs:
        total = total + sum3(ref[edge : edge + 16, :].astype(F32), 0)
    sums_ref[...] = jnp.broadcast_to(total[0:8], (8, LANES))
    aux = put_lanes(split3(total)).astype(BF16)
    flat = t_ref.reshape(nx * ny, depth)
    columns = []
    for k in range(2 * RADIUS):
        y = k if k < RADIUS else ny - 2 * RADIUS + k
        line[8 : 8 + nx, :] = flat[pl.ds(y, nx, stride=ny), :]
        line[8 - RADIUS : 8, :] = xb_ref[pl.ds(y, RADIUS, stride=ny), :]
        line[8 + nx : 8 + nx + RADIUS, :] = xa_ref[pl.ds(y, RADIUS, stride=ny), :]
        acc = taps[RADIUS] * line[8 : 8 + nx, :]
        for d in range(1, RADIUS + 1):
            acc = acc + taps[RADIUS + d] * (line[8 - d : 8 - d + nx, :] + line[8 + d : 8 + d + nx, :])
        columns.append(acc)
    for m, ref in enumerate(sends):
        for k in range(RADIUS):
            first, last = columns[k], columns[RADIUS + k]
            pick = jnp.where(flip_y == (m == 0), first, last)
            ref[k * nx : (k + 1) * nx, :] = pick.astype(BF16)
        ref[RADIUS * nx :, :] = aux


def edge_call(t, got, own_send, behind, ny_sends, cases):
    nx, ny, depth = t.shape
    return pl.pallas_call(
        functools.partial(edge_kernel, (cases, nx, ny, depth), len(got), ny_sends),
        in_specs=[VMEM] * (3 + len(got)),
        out_specs=[VMEM] * (ny_sends + 3),
        out_shape=[jax.ShapeDtypeStruct((RADIUS * nx + 16, depth), BF16)] * ny_sends
        + [jax.ShapeDtypeStruct((RADIUS * ny, depth), F32)] * 2
        + [jax.ShapeDtypeStruct((8, LANES), F32)],
        scratch_shapes=[pltpu.VMEM((nx + 16, depth), F32)],
        compiler_params=pltpu.CompilerParams(vmem_limit_bytes=16 * MIB),
        name="edge",
    )(t, *got, own_send, behind)


def filter_row(ny, read, line, factor):
    taps = taps_1d()
    acc = taps[RADIUS] * read(0)
    for d in range(1, RADIUS + 1):
        acc = acc + taps[RADIUS + d] * (read(-d) + read(d))
    line[8 : 8 + ny, :] = acc
    res = taps[RADIUS] * acc
    for d in range(1, RADIUS + 1):
        res = res + taps[RADIUS + d] * (line[8 - d : 8 - d + ny, :] + line[8 + d : 8 + d + ny, :])
    return res * factor


def clear_line(line, ny):
    zeros = jnp.zeros((8, line.shape[-1]), F32)
    for k in range(line.shape[0]):
        line[k, 0:8, :] = zeros
        line[k, 8 + ny :, :] = zeros


def inner_kernel(shape, bx, t_ref, factor_ref, out_hbm, first_ref, last_ref, line, out_ref, sem):
    nx, ny, depth = shape
    steps = nx // bx
    clear_line(line, ny)
    copies = []
    for s in range(steps):
        lo, hi = max(s * bx, RADIUS), min((s + 1) * bx, nx - RADIUS)
        span = pl.ds(lo, hi - lo)
        copies.append(pltpu.make_async_copy(out_ref.at[span], out_hbm.at[span], sem.at[s]))

        def row(x, carry):
            res = filter_row(ny, lambda d: t_ref[x + d], line.at[x % 2], factor_ref[x])
            out_ref[x] = res
            first_ref[x] = res[0:8]
            last_ref[x] = res[ny - 8 : ny]
            return carry

        lax.fori_loop(lo, hi, row, 0)
        copies[s].start()
    for copy in copies:
        copy.wait()


def inner_call(t, factor):
    nx, ny, depth = t.shape
    bx = 8
    return pl.pallas_call(
        functools.partial(inner_kernel, t.shape, bx),
        in_specs=[VMEM] * 2,
        out_specs=[HBM, VMEM, VMEM],
        out_shape=[
            jax.ShapeDtypeStruct(t.shape, F32),
            jax.ShapeDtypeStruct((nx, 8, depth), F32),
            jax.ShapeDtypeStruct((nx, 8, depth), F32),
        ],
        scratch_shapes=[
            pltpu.VMEM((2, ny + 16, depth), F32),
            pltpu.VMEM(t.shape, F32),
            pltpu.SemaphoreType.DMA((nx // bx,)),
        ],
        compiler_params=pltpu.CompilerParams(vmem_limit_bytes=20 * MIB),
        name="inner",
    )(*in_vmem(t, factor))


def outer_kernel(shape, t_ref, xb_ref, xa_ref, factor_ref, _, __, ___, out_hbm, first_ref, last_ref, line, pad, out_ref, sem):
    nx, ny, depth = shape
    clear_line(line, ny)
    pad[0:RADIUS] = xb_ref[...].reshape(RADIUS, ny, depth)
    pad[RADIUS : 3 * RADIUS] = t_ref[0 : 2 * RADIUS]
    pad[3 * RADIUS : 5 * RADIUS] = t_ref[nx - 2 * RADIUS : nx]
    pad[5 * RADIUS :] = xa_ref[...].reshape(RADIUS, ny, depth)
    copies = []
    for side, start in ((0, 0), (1, nx - RADIUS)):
        for k in range(RADIUS):
            x = start + k
            mid = (RADIUS if side == 0 else 4 * RADIUS) + k
            res = filter_row(ny, lambda d: pad[mid + d], line.at[x % 2], factor_ref[x])
            out_ref[side, k] = res
            first_ref[x] = res[0:8]
            last_ref[x] = res[ny - 8 : ny]
        copies.append(pltpu.make_async_copy(out_ref.at[side], out_hbm.at[pl.ds(start, RADIUS)], sem.at[side]))
        copies[side].start()
    for copy in copies:
        copy.wait()


def outer_call(t, xb, xa, factor, out, first, last):
    nx, ny, depth = t.shape
    return pl.pallas_call(
        functools.partial(outer_kernel, t.shape),
        in_specs=[VMEM] * 4 + [HBM, VMEM, VMEM],
        out_specs=[HBM, VMEM, VMEM],
        out_shape=[
            jax.ShapeDtypeStruct(out.shape, F32),
            jax.ShapeDtypeStruct(first.shape, F32),
            jax.ShapeDtypeStruct(last.shape, F32),
        ],
        input_output_aliases={4: 0, 5: 1, 6: 2},
        scratch_shapes=[
            pltpu.VMEM((2, ny + 16, depth), F32),
            pltpu.VMEM((6 * RADIUS, ny, depth), F32),
            pltpu.VMEM((2, RADIUS, ny, depth), F32),
            pltpu.SemaphoreType.DMA((2,)),
        ],
        compiler_params=pltpu.CompilerParams(vmem_limit_bytes=16 * MIB),
        name="outer",
    )(*in_vmem(t, xb, xa, factor), *in_hbm(out), *in_vmem(first, last))


def finish_kernel(shape, cells, ngot, nextra, cases, ring, *refs):
    nx, ny, depth = shape
    got_refs = refs[:ngot]
    sums_ref = refs[ngot]
    extra_refs = refs[1 + ngot : 1 + ngot + nextra]
    first_ref, last_ref, factor_ref, _, out_hbm, comp_ref, strip, sem = refs[1 + ngot + nextra :]
    taps = taps_1d()
    edge = RADIUS * nx
    place, count = lax.axis_index("gy"), lax.axis_size("gy")
    blocks = [r[0:edge, :].astype(F32) for r in got_refs]
    before, after = sided(place % 2 == 0, blocks) if blocks else (jnp.zeros((edge, depth), F32),) * 2
    before = jnp.where(place == 0, 0.0, before)
    after = jnp.where(place == count - 1, 0.0, after)
    flat = factor_ref.reshape(nx * ny, depth)
    copies = []
    for ref, side in ((first_ref, 0), (last_ref, 1)):
        strip[side] = ref[...]
        view = strip.at[side].reshape(nx * 8, depth)
        for y in range(RADIUS):
            add = jnp.zeros((nx, depth), F32)
            for k in range(RADIUS):
                if side == 0:
                    d, halo, own = y + RADIUS - k, before[k * nx : (k + 1) * nx], y
                else:
                    d, halo, own = k + RADIUS - y, after[k * nx : (k + 1) * nx], ny - RADIUS + y
                if d <= RADIUS:
                    add = add + taps[RADIUS + d] * halo
            at = own if side == 0 else own - (ny - 8)
            view[pl.ds(at, nx, stride=8), :] += flat[pl.ds(own, nx, stride=ny), :] * add
        target = out_hbm.at[:, 0:8, :] if side == 0 else out_hbm.at[:, ny - 8 : ny, :]
        copies.append(pltpu.make_async_copy(strip.at[side], target, sem.at[side]))
        copies[side].start()
    total = sums_ref[...]
    for ref in extra_refs:
        total = total + ref[...]
    if ring:
        for ref in got_refs:
            total = total + sum3(ref[edge : edge + 16, :].astype(F32), 0)[0:8]
    for c in range(cases):
        comp_ref[c] = total[c, 0] / cells
    for copy in copies:
        copy.wait()


def finish_call(got, sums, extra, first, last, factor, out, cells, cases, ring):
    nx, ny, depth = out.shape
    nin = len(got) + 1 + len(extra)
    return pl.pallas_call(
        functools.partial(finish_kernel, out.shape, cells, len(got), len(extra), cases, ring),
        in_specs=[VMEM] * (nin + 3) + [HBM],
        out_specs=[HBM, SMEM],
        out_shape=[jax.ShapeDtypeStruct(out.shape, F32), jax.ShapeDtypeStruct((cases,), F32)],
        input_output_aliases={nin + 3: 0},
        scratch_shapes=[pltpu.VMEM((2, nx, 8, depth), F32), pltpu.SemaphoreType.DMA((2,))],
        compiler_params=pltpu.CompilerParams(vmem_limit_bytes=16 * MIB),
        name="finish",
    )(*got, sums, *extra, *in_vmem(first, last, factor), *in_hbm(out))


def swap_pairs(count, first):
    return [q for i in range(first, count - 1, 2) for q in ((i, i + 1), (i + 1, i))]


def swaps_of(count):
    return min(count - 1, 2)


def xor_pairs(count, m):
    return [(i, i ^ m) for i in range(count)]


def shards(density, design_mask, energy, decay, case_index, case_weight):
    cases = energy.shape[0]
    nx, ny, depth = density.shape
    nz, gx, gy = (lax.axis_size(a) for a in ("gz", "gx", "gy"))
    send, own, source = faces_call(density, design_mask, energy, decay, case_index, case_weight)
    swapped = nz in (1, 2, 4)
    if swapped:
        msgs = [lax.ppermute(send, "gz", xor_pairs(nz, m)) for m in range(1, nz)]
    else:
        every = lax.all_gather(send, "gz")
        own, *msgs = [every[j] for j in range(nz)]
    t_local, factor, umap = local_call(density, design_mask, source, decay, case_index, case_weight)
    t, *x_sends = couple_call(own, msgs, t_local, umap, max(swaps_of(gx), 1), swapped)
    x_got = [lax.ppermute(x_sends[k], "gx", swap_pairs(gx, k)) for k in range(swaps_of(gx))]
    partial, first, last = inner_call(t, factor)
    *y_sends, xb, xa, sums = edge_call(t, x_got, x_sends[0], first, swaps_of(gy), cases)
    ring = gy == 4
    ends = [(0, gy - 1), (gy - 1, 0)] if ring else []
    y_got = [lax.ppermute(y_sends[k], "gy", swap_pairs(gy, k) + (ends if k else [])) for k in range(swaps_of(gy))]
    extra = [lax.ppermute(sums, "gy", xor_pairs(gy, m)) for m in ([2] if ring else range(1, gy))]
    partial, first, last = outer_call(t, xb, xa, factor, partial, first, last)
    cells = nx * ny * depth * nz * gx * gy
    return tuple(finish_call(y_got, sums, extra, first, last, factor, partial, float(cells), cases, ring))


def solution(mesh):
    placed = (
        P("gx", "gy", "gz"),
        P("gx", "gy", "gz"),
        P(None, "gx", "gy", "gz"),
        P(None, "gz"),
        P(),
        P(),
    )
    return jax.shard_map(
        shards, mesh=mesh, in_specs=placed, out_specs=(P("gx", "gy", "gz"), P()), check_vma=False
    )
```

```python
import functools
import math
import jax
import jax.numpy as jnp
from jax import lax
from jax.experimental import pallas as pl
from jax.experimental.pallas import tpu as pltpu
from jax.sharding import PartitionSpec as P

RADIUS = 3
AHEAD = 2
LANES = 128
MIB = 2**20
F32 = jnp.float32
BF16 = jnp.bfloat16
HIGH = lax.Precision.HIGHEST
HBM = pl.BlockSpec(memory_space=pltpu.HBM)
VMEM = pl.BlockSpec(memory_space=pltpu.VMEM)
SMEM = pl.BlockSpec(memory_space=pltpu.SMEM)


def in_hbm(*arrays):
    return [pltpu.with_memory_space_constraint(a, pltpu.HBM) for a in arrays]


def in_vmem(*arrays):
    return [pltpu.with_memory_space_constraint(a, pltpu.VMEM) for a in arrays]


def taps_1d():
    raw = [math.exp(-2.0 * k * k / (RADIUS * RADIUS)) for k in range(-RADIUS, RADIUS + 1)]
    total = sum(raw)
    return [r / total for r in raw]


def dot_high(a, b, dims=((1,), (0,))):
    return lax.dot_general(a, b, (dims, ((), ())), precision=HIGH, preferred_element_type=F32)


def split2(v):
    hi = v.astype(BF16)
    return hi, (v - hi.astype(F32)).astype(BF16)


def split3(v):
    a = v.astype(BF16).astype(F32)
    b = (v - a).astype(BF16).astype(F32)
    return a, b, v - a - b


def put_lanes(columns):
    rows = columns[0].shape[0]
    lane = lax.broadcasted_iota(jnp.int32, (rows, LANES), 1)
    out = jnp.zeros((rows, LANES), F32)
    for k, col in enumerate(columns):
        out = jnp.where(lane == k, col, out)
    return out


def pad_rows(v, rows):
    return jnp.concatenate([v, jnp.zeros((rows - v.shape[0],) + v.shape[1:], v.dtype)], axis=0)


def sum3(block, at):
    return block[:, at : at + 1] + block[:, at + 1 : at + 2] + block[:, at + 2 : at + 3]


class Slab:
    def __init__(self, decay):
        cases, depth = decay.shape
        self.decay = decay
        self.row = lax.broadcasted_iota(jnp.int32, (depth, depth), 0)
        self.col = lax.broadcasted_iota(jnp.int32, (depth, depth), 1)
        logs = jnp.log(decay)
        self.up = dot_high(logs, (self.row <= self.col).astype(F32))
        self.up_ex = self.up - logs
        wide = lambda v: jnp.transpose(pad_rows(v, 8))
        self.up_t = wide(self.up)
        self.up_ex_t = wide(self.up_ex)
        self.keep_t = wide(1.0 - decay)
        self.total = self.up[:, depth - 1 : depth]

    def forward_t(self, c):
        gap = self.up[c : c + 1, :] - self.up_t[:, c : c + 1]
        weight = jnp.exp(jnp.minimum(gap, 0.0)) * self.keep_t[:, c : c + 1]
        return jnp.where(self.col >= self.row, weight, 0.0)


def case_scale(weight_ref, index_ref, c):
    return -3.0 * weight_ref[index_ref[c]]


def faces_kernel(shape, bx, *refs):
    cases, nx, ny, depth = shape
    (index_hbm, weight_hbm, decay_hbm, density_hbm, mask_hbm, energy_hbm,
     send_ref, own_ref, source_ref, density_ref, mask_ref, map_ref, rows_ref,
     index_ref, weight_ref, decay_ref, energy_ref, small_sem, sem) = refs
    steps, cols = nx // bx, bx * ny
    small = [
        pltpu.make_async_copy(decay_hbm, decay_ref, small_sem.at[0]),
        pltpu.make_async_copy(index_hbm, index_ref, small_sem.at[1]),
        pltpu.make_async_copy(weight_hbm, weight_ref, small_sem.at[2]),
    ]
    big = []
    for s in range(steps):
        at = pl.ds(s * bx, bx)
        big.append([
            pltpu.make_async_copy(density_hbm.at[at], density_ref.at[at], sem.at[0, s]),
            pltpu.make_async_copy(mask_hbm.at[at], mask_ref.at[at], sem.at[1, s]),
            pltpu.make_async_copy(energy_hbm.at[:, at], energy_ref.at[:, at], sem.at[2, s]),
        ])
    for copy in small:
        copy.start()
    for group in big[:AHEAD]:
        for copy in group:
            copy.start()
    for copy in small:
        copy.wait()

    decay = decay_ref[...]
    slab = Slab(decay)
    for group in big[AHEAD : AHEAD + 1]:
        for copy in group:
            copy.start()
    zero_row = jnp.zeros((1, depth), F32)
    e_rows, h_rows, turns = [], [], []
    for c in range(cases):
        scale = case_scale(weight_ref, index_ref, c)
        f_t = slab.forward_t(c) * scale
        map_ref[c] = f_t
        keep = 1.0 - decay[c : c + 1, :]
        e_row = jnp.exp(slab.total[c : c + 1] - slab.up[c : c + 1, :]) * keep * scale
        b_row = jnp.exp(slab.up_ex[c : c + 1, :]) * keep
        h_row = dot_high(b_row, f_t, ((1,), (1,)))
        turns.append(jnp.sum(b_row * jnp.exp(slab.up[c : c + 1, :]), axis=1, keepdims=True))
        place = lambda r: jnp.concatenate([zero_row] * c + [r] + [zero_row] * (cases - 1 - c), axis=1)
        e_rows.append(place(e_row))
        h_rows.append(place(h_row))
    w_hi, w_lo = split2(jnp.concatenate(e_rows + h_rows, axis=0))
    wmat = jnp.concatenate([w_hi, w_lo], axis=0)
    rows_ref[...] = jnp.concatenate([pad_rows(v, 8) for v in (slab.up, slab.up_ex, 1.0 - decay)], axis=0)

    sums = [jnp.zeros((8, depth), F32) for _ in range(cases)]

    def faces_of(s):
        span = pl.ds(s * cols, cols)
        faces = lax.dot_general(
            wmat, source_ref[span, :], (((1,), (1,)), ((), ())), preferred_element_type=F32)
        faces = faces[0 : 2 * cases] + faces[2 * cases : 4 * cases]
        own_ref[:, span] = faces
        send_ref[:, span] = faces.astype(BF16)

    for s in range(steps):
        for copy in big[s]:
            copy.wait()
        for group in big[s + AHEAD + 1 : s + AHEAD + 2]:
            for copy in group:
                copy.start()
        at = pl.ds(s * bx, bx)
        mask = mask_ref[at]
        dense = jnp.where(mask == 1, 0.001, jnp.where(mask == 2, 1.0, density_ref[at]))
        cube = dense * dense * dense
        span = pl.ds(s * cols, cols)
        for c in range(cases):
            work = cube * energy_ref[c, at].astype(F32)
            sums[c] = sums[c] + jnp.sum(work.reshape(cols // 8, 8, depth), axis=0)
            source_ref[span, c * depth : (c + 1) * depth] = work.astype(BF16).reshape(cols, depth)
        if s > 0:
            faces_of(s - 1)
    faces_of(steps - 1)

    total = jnp.concatenate([jnp.sum(jnp.sum(v, axis=0, keepdims=True), axis=1, keepdims=True) for v in sums], axis=0)
    turn = jnp.concatenate(turns, axis=0)
    aux = put_lanes(split3(jnp.exp(slab.total)) + split3(turn) + split3(total))
    aux = pad_rows(aux, 2 * cases)
    tail = pl.ds(nx * ny, LANES)
    own_ref[:, tail] = aux
    send_ref[:, tail] = aux.astype(BF16)


def faces_call(density, design_mask, energy, decay, case_index, case_weight):
    cases, nx, ny, depth = energy.shape
    bx = 16
    width = nx * ny + LANES
    return pl.pallas_call(
        functools.partial(faces_kernel, energy.shape, bx),
        in_specs=[HBM] * 6,
        out_specs=[VMEM] * 7,
        out_shape=[
            pltpu.VMEM((2 * cases, width), BF16),
            pltpu.VMEM((2 * cases, width), F32),
            pltpu.VMEM((nx * ny, cases * depth), BF16),
            pltpu.VMEM(density.shape, F32),
            pltpu.VMEM(density.shape, jnp.int32),
            pltpu.VMEM((cases, depth, depth), F32),
            pltpu.VMEM((24, depth), F32),
        ],
        scratch_shapes=[
            pltpu.SMEM(case_index.shape, case_index.dtype),
            pltpu.SMEM(case_weight.shape, F32),
            pltpu.VMEM(decay.shape, F32),
            pltpu.VMEM(energy.shape, BF16),
            pltpu.SemaphoreType.DMA((3,)),
            pltpu.SemaphoreType.DMA((3, nx // bx)),
        ],
        compiler_params=pltpu.CompilerParams(vmem_limit_bytes=20 * MIB),
        name="faces",
    )(*in_hbm(case_index, case_weight, decay, density, design_mask, energy))


def local_kernel(shape, bx, source_ref, density_ref, mask_ref, map_ref, rows_ref, t_ref, factor_ref, umap_ref, rmat):
    cases, nx, ny, depth = shape
    steps, cols = nx // bx, bx * ny
    row = lax.broadcasted_iota(jnp.int32, (depth, depth), 0)
    col = lax.broadcasted_iota(jnp.int32, (depth, depth), 1)
    up, up_ex = rows_ref[0:8, :], rows_ref[8:16, :]
    up_ex_t, keep_t = jnp.transpose(up_ex), jnp.transpose(rows_ref[16:24, :])
    total = up[:, depth - 1 : depth]
    lead = jnp.exp(up)
    a_rows = []
    for c in range(cases):
        gap = up_ex_t[:, c : c + 1] - up_ex[c : c + 1, :]
        weight = jnp.exp(jnp.minimum(gap, 0.0)) * keep_t[:, c : c + 1]
        b_t = jnp.where(col <= row, weight, 0.0)
        both = dot_high(jnp.concatenate([map_ref[c], lead], axis=0), b_t)
        hi, lo = split2(both[0:depth])
        rmat[c * depth : (c + 1) * depth, 0:depth] = hi
        rmat[c * depth : (c + 1) * depth, depth : 2 * depth] = lo
        a_rows.append(both[depth + c : depth + c + 1])
    u_all = jnp.concatenate(a_rows + [jnp.exp(total - up_ex)[0:cases]], axis=0)
    u_hi = u_all.astype(BF16).astype(F32)
    umap_ref[...] = jnp.concatenate([u_hi, u_hi, u_all - u_hi, jnp.zeros_like(u_hi)], axis=0).astype(BF16)

    for s in range(steps):
        both = lax.dot_general(
            source_ref[s * cols : (s + 1) * cols, :], rmat[...], (((1,), (0,)), ((), ())),
            preferred_element_type=F32)
        at = slice(s * bx, (s + 1) * bx)
        t_ref[at] = (both[:, 0:depth] + both[:, depth : 2 * depth]).reshape(bx, ny, depth)
        factor_ref[at] = jnp.where(mask_ref[at] == 0, 1.0 / jnp.maximum(density_ref[at], 0.1), 0.0)


def local_call(source, density, mask, maps, rows):
    nx, ny, depth = density.shape
    cases = maps.shape[0]
    return pl.pallas_call(
        functools.partial(local_kernel, (cases, nx, ny, depth), 16),
        in_specs=[VMEM] * 5,
        out_specs=[VMEM] * 3,
        out_shape=[
            pltpu.VMEM(density.shape, F32),
            pltpu.VMEM(density.shape, F32),
            pltpu.VMEM((8 * cases, depth), BF16),
        ],
        scratch_shapes=[pltpu.VMEM((cases * depth, 2 * depth), BF16)],
        compiler_params=pltpu.CompilerParams(vmem_limit_bytes=16 * MIB),
        name="local",
    )(*in_vmem(source, density, mask, maps, rows))


def head_kernel(shape, nslabs, nsends, swapped, *refs):
    cases, nx, ny, depth = shape
    own_ref = refs[0]
    msgs = refs[1:nslabs]
    t_ref, umap_ref, lhs_ref = refs[nslabs : 3 + nslabs]
    sends = refs[3 + nslabs : 3 + nslabs + nsends]
    stack = refs[-1]
    cols = nx * ny
    mine = lax.axis_index("gz")
    low = lax.axis_index("gx") % 2 == 1
    stack[0] = own_ref[...].astype(F32)
    for m, msg in enumerate(msgs):
        stack[m + 1] = msg[...].astype(F32)
    total = jnp.zeros((cases, 1), F32)
    for m in range(nslabs):
        total = total + sum3(stack[m, 0:cases, cols : cols + LANES], 6)
    state = jnp.zeros((cases, cols), F32)
    entering, above = state, state
    tops, gains = [], []
    for j in range(nslabs):
        at = mine ^ j if swapped else j
        aux = stack[at, 0:cases, cols : cols + LANES]
        gains.append(sum3(aux, 0))
        entering = jnp.where(mine == j, state, entering)
        tops.append(stack[at, cases : 2 * cases, 0:cols] + sum3(aux, 3) * state)
        state = gains[j] * state + stack[at, 0:cases, 0:cols]
    state = jnp.zeros((cases, cols), F32)
    for j in reversed(range(nslabs)):
        above = jnp.where(mine == j, state, above)
        state = tops[j] + gains[j] * state
    faces = jnp.concatenate([entering, above], axis=0)
    hi = faces.astype(BF16).astype(F32)
    lhs_ref[...] = jnp.concatenate([hi, faces - hi, hi, jnp.zeros_like(hi)], axis=0).astype(BF16)
    aux = pad_rows(put_lanes(split3(total)), 16).astype(BF16)
    rows = RADIUS + 1
    wide, edge = rows * ny, RADIUS * ny
    for k, ref in enumerate(sends):
        bottom = low if k == 0 else jnp.logical_not(low)
        start = jnp.where(bottom, 0, nx - rows)
        part = lhs_ref[:, pl.ds(pl.multiple_of(start * ny, wide), wide)]
        add = lax.dot_general(part, umap_ref[...], (((0,), (0,)), ((), ())), preferred_element_type=F32)
        full = t_ref[pl.ds(start, rows)].reshape(wide, depth) + add
        ref[0:edge, :] = jnp.where(bottom, full[0:edge], full[ny:wide]).astype(BF16)
        ref[edge:, :] = aux


def head_call(own, msgs, t_local, umap, nsends, swapped):
    nx, ny, depth = t_local.shape
    cases = own.shape[0] // 2
    nslabs = len(msgs) + 1
    return pl.pallas_call(
        functools.partial(head_kernel, (cases, nx, ny, depth), nslabs, nsends, swapped),
        in_specs=[VMEM] * (nslabs + 2),
        out_specs=[VMEM] * (1 + nsends),
        out_shape=[pltpu.VMEM((8 * cases, nx * ny), BF16)]
        + [jax.ShapeDtypeStruct((RADIUS * ny + 16, depth), BF16)] * nsends,
        scratch_shapes=[pltpu.VMEM((nslabs,) + own.shape, F32)],
        compiler_params=pltpu.CompilerParams(vmem_limit_bytes=20 * MIB),
        name="head",
    )(own, *msgs, *in_vmem(t_local), umap)


def sided(even, got):
    a = got[0]
    b = got[1] if len(got) > 1 else jnp.zeros_like(a)
    return jnp.where(even, b, a), jnp.where(even, a, b)


def edge_kernel(shape, nx_sends, ny_sends, *refs):
    cases, nx, ny, depth = shape
    t_ref = refs[0]
    got_refs = refs[1 : 1 + nx_sends]
    own_send = refs[1 + nx_sends]
    sends = refs[2 + nx_sends : 2 + nx_sends + ny_sends]
    xb_ref, xa_ref, sums_ref, line = refs[2 + nx_sends + ny_sends :]
    taps = taps_1d()
    edge = RADIUS * ny
    even_x = lax.axis_index("gx") % 2 == 0
    flip_y = lax.axis_index("gy") % 2 == 1
    blocks = [r[0:edge, :].astype(F32) for r in got_refs]
    before, after = sided(even_x, blocks)
    xb_ref[...] = before
    xa_ref[...] = after
    total = sum3(own_send[edge : edge + 16, :].astype(F32), 0)
    for ref in got_refs:
        total = total + sum3(ref[edge : edge + 16, :].astype(F32), 0)
    sums_ref[...] = jnp.broadcast_to(total[0:8], (8, LANES))
    aux = put_lanes(split3(total)).astype(BF16)
    flat = t_ref.reshape(nx * ny, depth)
    columns = []
    for k in range(2 * RADIUS):
        y = k if k < RADIUS else ny - 2 * RADIUS + k
        line[8 : 8 + nx, :] = flat[pl.ds(y, nx, stride=ny), :]
        line[8 - RADIUS : 8, :] = xb_ref[pl.ds(y, RADIUS, stride=ny), :]
        line[8 + nx : 8 + nx + RADIUS, :] = xa_ref[pl.ds(y, RADIUS, stride=ny), :]
        acc = taps[RADIUS] * line[8 : 8 + nx, :]
        for d in range(1, RADIUS + 1):
            acc = acc + taps[RADIUS + d] * (line[8 - d : 8 - d + nx, :] + line[8 + d : 8 + d + nx, :])
        columns.append(acc)
    for m, ref in enumerate(sends):
        for k in range(RADIUS):
            first, last = columns[k], columns[RADIUS + k]
            pick = jnp.where(flip_y == (m == 0), first, last)
            ref[k * nx : (k + 1) * nx, :] = pick.astype(BF16)
        ref[RADIUS * nx :, :] = aux


def edge_call(t, got, own_send, ny_sends, cases):
    nx, ny, depth = t.shape
    return pl.pallas_call(
        functools.partial(edge_kernel, (cases, nx, ny, depth), len(got), ny_sends),
        in_specs=[VMEM] * (2 + len(got)),
        out_specs=[VMEM] * (ny_sends + 3),
        out_shape=[jax.ShapeDtypeStruct((RADIUS * nx + 16, depth), BF16)] * ny_sends
        + [jax.ShapeDtypeStruct((RADIUS * ny, depth), F32)] * 2
        + [jax.ShapeDtypeStruct((8, LANES), F32)],
        scratch_shapes=[pltpu.VMEM((nx + 16, depth), F32)],
        compiler_params=pltpu.CompilerParams(vmem_limit_bytes=16 * MIB),
        name="edge",
    )(t, *got, own_send)


def filter_row(ny, read, line, factor):
    taps = taps_1d()
    acc = taps[RADIUS] * read(0)
    for d in range(1, RADIUS + 1):
        acc = acc + taps[RADIUS + d] * (read(-d) + read(d))
    line[8 : 8 + ny, :] = acc
    res = taps[RADIUS] * acc
    for d in range(1, RADIUS + 1):
        res = res + taps[RADIUS + d] * (line[8 - d : 8 - d + ny, :] + line[8 + d : 8 + d + ny, :])
    return res * factor


def clear_line(line, ny):
    zeros = jnp.zeros((8, line.shape[-1]), F32)
    for k in range(line.shape[0]):
        line[k, 0:8, :] = zeros
        line[k, 8 + ny :, :] = zeros


def filter_rows(lo, hi, chunk, read, line, factor_ref, first_ref, last_ref, out_ref, out_hbm, sem):
    ny = factor_ref.shape[1]
    copies = []

    def row(x, carry):
        res = filter_row(ny, lambda d: read(x + d), line.at[x % 2], factor_ref[x])
        out_ref[x] = res
        first_ref[x] = res[0:8]
        last_ref[x] = res[ny - 8 : ny]
        return carry

    for s, start in enumerate(range(lo, hi, chunk)):
        stop = min(start + chunk, hi)
        lax.fori_loop(start, stop, row, 0)
        span = pl.ds(start, stop - start)
        copies.append(pltpu.make_async_copy(out_ref.at[span], out_hbm.at[span], sem.at[s]))
        copies[s].start()
    return copies


def split_row(nx):
    return nx * 9 // 16


def body_kernel(shape, chunk, lhs_ref, umap_ref, part_ref, factor_ref, t_ref, out_hbm, first_ref, last_ref, line, out_ref, sem):
    nx, ny, depth = shape
    add = lax.dot_general(lhs_ref[...], umap_ref[...], (((0,), (0,)), ((), ())), preferred_element_type=F32)
    t_ref[...] = part_ref[...] + add.reshape(nx, ny, depth)
    clear_line(line, ny)
    copies = filter_rows(
        RADIUS, split_row(nx), chunk, lambda x: t_ref[x], line, factor_ref, first_ref, last_ref, out_ref, out_hbm, sem)
    for copy in copies:
        copy.wait()


def body_call(lhs, umap, part, factor):
    nx, ny, depth = part.shape
    chunk = 11
    return pl.pallas_call(
        functools.partial(body_kernel, part.shape, chunk),
        in_specs=[VMEM] * 4,
        out_specs=[VMEM, HBM, VMEM, VMEM],
        out_shape=[
            pltpu.VMEM(part.shape, F32),
            jax.ShapeDtypeStruct(part.shape, F32),
            pltpu.VMEM((nx, 8, depth), F32),
            pltpu.VMEM((nx, 8, depth), F32),
        ],
        scratch_shapes=[
            pltpu.VMEM((2, ny + 16, depth), F32),
            pltpu.VMEM(part.shape, F32),
            pltpu.SemaphoreType.DMA((-(-nx // chunk),)),
        ],
        compiler_params=pltpu.CompilerParams(vmem_limit_bytes=20 * MIB),
        name="body",
    )(*in_vmem(lhs, umap, part, factor))


def rest_kernel(shape, chunk, t_ref, xb_ref, xa_ref, factor_ref, _, __, ___, out_hbm, first_ref, last_ref,
                line, pad, out_ref, sem, side_sem):
    nx, ny, depth = shape
    clear_line(line, ny)
    pad[0:RADIUS] = xb_ref[...].reshape(RADIUS, ny, depth)
    pad[RADIUS : 3 * RADIUS] = t_ref[0 : 2 * RADIUS]
    pad[3 * RADIUS : 5 * RADIUS] = t_ref[nx - 2 * RADIUS : nx]
    pad[5 * RADIUS :] = xa_ref[...].reshape(RADIUS, ny, depth)
    copies = []
    for side, start in ((0, 0), (1, nx - RADIUS)):
        for k in range(RADIUS):
            x = start + k
            mid = (RADIUS if side == 0 else 4 * RADIUS) + k
            res = filter_row(ny, lambda d: pad[mid + d], line.at[x % 2], factor_ref[x])
            out_ref[x] = res
            first_ref[x] = res[0:8]
            last_ref[x] = res[ny - 8 : ny]
        span = pl.ds(start, RADIUS)
        copies.append(pltpu.make_async_copy(out_ref.at[span], out_hbm.at[span], side_sem.at[side]))
        copies[side].start()
    copies += filter_rows(
        split_row(nx), nx - RADIUS, chunk, lambda x: t_ref[x], line, factor_ref, first_ref, last_ref, out_ref, out_hbm, sem)
    for copy in copies:
        copy.wait()


def rest_call(t, xb, xa, factor, out, first, last):
    nx, ny, depth = t.shape
    chunk = 9
    return pl.pallas_call(
        functools.partial(rest_kernel, t.shape, chunk),
        in_specs=[VMEM] * 4 + [HBM, VMEM, VMEM],
        out_specs=[HBM, VMEM, VMEM],
        out_shape=[
            jax.ShapeDtypeStruct(out.shape, F32),
            pltpu.VMEM(first.shape, F32),
            pltpu.VMEM(last.shape, F32),
        ],
        input_output_aliases={4: 0, 5: 1, 6: 2},
        scratch_shapes=[
            pltpu.VMEM((2, ny + 16, depth), F32),
            pltpu.VMEM((6 * RADIUS, ny, depth), F32),
            pltpu.VMEM(t.shape, F32),
            pltpu.SemaphoreType.DMA((-(-nx // chunk),)),
            pltpu.SemaphoreType.DMA((2,)),
        ],
        compiler_params=pltpu.CompilerParams(vmem_limit_bytes=20 * MIB),
        name="rest",
    )(*in_vmem(t, xb, xa, factor), *in_hbm(out), *in_vmem(first, last))


def finish_kernel(shape, ngot, *refs):
    nx, ny, depth = shape
    got_refs = refs[:ngot]
    first_ref, last_ref, factor_ref, _, out_hbm, done_ref, strip, sem = refs[ngot:]
    taps = taps_1d()
    edge = RADIUS * nx
    place, count = lax.axis_index("gy"), lax.axis_size("gy")
    blocks = [r[0:edge, :].astype(F32) for r in got_refs]
    before, after = sided(place % 2 == 0, blocks) if blocks else (jnp.zeros((edge, depth), F32),) * 2
    before = jnp.where(place == 0, 0.0, before)
    after = jnp.where(place == count - 1, 0.0, after)
    flat = factor_ref.reshape(nx * ny, depth)
    copies = []
    for ref, side in ((first_ref, 0), (last_ref, 1)):
        strip[side] = ref[...]
        view = strip.at[side].reshape(nx * 8, depth)
        for y in range(RADIUS):
            add = jnp.zeros((nx, depth), F32)
            for k in range(RADIUS):
                if side == 0:
                    d, halo, own = y + RADIUS - k, before[k * nx : (k + 1) * nx], y
                else:
                    d, halo, own = k + RADIUS - y, after[k * nx : (k + 1) * nx], ny - RADIUS + y
                if d <= RADIUS:
                    add = add + taps[RADIUS + d] * halo
            at = own if side == 0 else own - (ny - 8)
            view[pl.ds(at, nx, stride=8), :] += flat[pl.ds(own, nx, stride=ny), :] * add
        target = out_hbm.at[:, 0:8, :] if side == 0 else out_hbm.at[:, ny - 8 : ny, :]
        copies.append(pltpu.make_async_copy(strip.at[side], target, sem.at[side]))
        copies[side].start()
    done_ref[...] = jnp.zeros_like(done_ref)
    for copy in copies:
        copy.wait()


def finish_call(got, first, last, factor, out):
    nx, ny, depth = out.shape
    nin = len(got)
    return pl.pallas_call(
        functools.partial(finish_kernel, out.shape, len(got)),
        in_specs=[VMEM] * (nin + 3) + [HBM],
        out_specs=[HBM, VMEM],
        out_shape=[jax.ShapeDtypeStruct(out.shape, F32), pltpu.VMEM((8, LANES), F32)],
        input_output_aliases={nin + 3: 0},
        scratch_shapes=[pltpu.VMEM((2, nx, 8, depth), F32), pltpu.SemaphoreType.DMA((2,))],
        compiler_params=pltpu.CompilerParams(vmem_limit_bytes=16 * MIB),
        name="finish",
    )(*got, *in_vmem(first, last, factor), *in_hbm(out))


def mean_kernel(cells, cases, *refs):
    total = refs[0][...]
    for ref in refs[2:-1]:
        block = ref[...] if ref.shape[0] == 8 else sum3(ref[ref.shape[0] - 16 :, :].astype(F32), 0)[0:8]
        total = total + block
    for c in range(cases):
        refs[-1][c] = total[c, 0] / cells


def mean_call(sums, behind, got, cells, cases):
    return pl.pallas_call(
        functools.partial(mean_kernel, cells, cases),
        in_specs=[VMEM] * (2 + len(got)),
        out_specs=SMEM,
        out_shape=jax.ShapeDtypeStruct((cases,), F32),
        compiler_params=pltpu.CompilerParams(vmem_limit_bytes=4 * MIB),
        name="mean",
    )(sums, behind, *got)


def swap_pairs(count, first):
    return [q for i in range(first, count - 1, 2) for q in ((i, i + 1), (i + 1, i))]


def swaps_of(count):
    return min(count - 1, 2)


def xor_pairs(count, m):
    return [(i, i ^ m) for i in range(count)]


def shards(density, design_mask, energy, decay, case_index, case_weight):
    cases = energy.shape[0]
    nx, ny, depth = density.shape
    nz, gx, gy = (lax.axis_size(a) for a in ("gz", "gx", "gy"))
    send, own, source, density_v, mask_v, maps, rows = faces_call(
        density, design_mask, energy, decay, case_index, case_weight)
    swapped = nz in (1, 2, 4)
    if swapped:
        msgs = [lax.ppermute(send, "gz", xor_pairs(nz, m)) for m in range(1, nz)]
    else:
        every = lax.all_gather(send, "gz")
        own, *msgs = [every[j] for j in range(nz)]
    part, factor, umap = local_call(source, density_v, mask_v, maps, rows)
    lhs, *x_sends = head_call(own, msgs, part, umap, max(swaps_of(gx), 1), swapped)
    x_got = [lax.ppermute(x_sends[k], "gx", swap_pairs(gx, k)) for k in range(swaps_of(gx))]
    t, out, first, last = body_call(lhs, umap, part, factor)
    *y_sends, xb, xa, sums = edge_call(t, x_got, x_sends[0], swaps_of(gy), cases)
    ring = gy == 4
    ends = [(0, gy - 1), (gy - 1, 0)] if ring else []
    y_got = [lax.ppermute(y_sends[k], "gy", swap_pairs(gy, k) + (ends if k else [])) for k in range(swaps_of(gy))]
    out, first, last = rest_call(t, xb, xa, factor, out, first, last)
    if ring:
        y_got[1], first = lax.optimization_barrier((y_got[1], first))
        more = y_got + [lax.ppermute(y_got[1], "gy", swap_pairs(gy, 0))]
    else:
        more = [lax.ppermute(sums, "gy", xor_pairs(gy, m)) for m in range(1, gy)]
    out, behind = finish_call(y_got, first, last, factor, out)
    cells = nx * ny * depth * nz * gx * gy
    return out, mean_call(sums, behind, more, float(cells), cases)


def solution(mesh):
    placed = (
        P("gx", "gy", "gz"),
        P("gx", "gy", "gz"),
        P(None, "gx", "gy", "gz"),
        P(None, "gz"),
        P(),
        P(),
    )
    return jax.shard_map(
        shards, mesh=mesh, in_specs=placed, out_specs=(P("gx", "gy", "gz"), P()), check_vma=False
    )
```

```python
import functools
import math
import jax
import jax.numpy as jnp
from jax import lax
from jax.experimental import pallas as pl
from jax.experimental.pallas import tpu as pltpu
from jax.sharding import PartitionSpec as P

RADIUS = 3
AHEAD = 2
LANES = 128
MIB = 2**20
F32 = jnp.float32
BF16 = jnp.bfloat16
HIGH = lax.Precision.HIGHEST
HBM = pl.BlockSpec(memory_space=pltpu.HBM)
VMEM = pl.BlockSpec(memory_space=pltpu.VMEM)
SMEM = pl.BlockSpec(memory_space=pltpu.SMEM)


def in_hbm(*arrays):
    return [pltpu.with_memory_space_constraint(a, pltpu.HBM) for a in arrays]


def in_vmem(*arrays):
    return [pltpu.with_memory_space_constraint(a, pltpu.VMEM) for a in arrays]


def taps_1d():
    raw = [math.exp(-2.0 * k * k / (RADIUS * RADIUS)) for k in range(-RADIUS, RADIUS + 1)]
    total = sum(raw)
    return [r / total for r in raw]


def dot_high(a, b, dims=((1,), (0,))):
    return lax.dot_general(a, b, (dims, ((), ())), precision=HIGH, preferred_element_type=F32)


def split2(v):
    hi = v.astype(BF16)
    return hi, (v - hi.astype(F32)).astype(BF16)


def split3(v):
    a = v.astype(BF16).astype(F32)
    b = (v - a).astype(BF16).astype(F32)
    return a, b, v - a - b


def put_lanes(columns):
    rows = columns[0].shape[0]
    lane = lax.broadcasted_iota(jnp.int32, (rows, LANES), 1)
    out = jnp.zeros((rows, LANES), F32)
    for k, col in enumerate(columns):
        out = jnp.where(lane == k, col, out)
    return out


def pad_rows(v, rows):
    return jnp.concatenate([v, jnp.zeros((rows - v.shape[0],) + v.shape[1:], v.dtype)], axis=0)


def sum3(block, at):
    return block[:, at : at + 1] + block[:, at + 1 : at + 2] + block[:, at + 2 : at + 3]


class Slab:
    def __init__(self, decay):
        cases, depth = decay.shape
        self.decay = decay
        self.row = lax.broadcasted_iota(jnp.int32, (depth, depth), 0)
        self.col = lax.broadcasted_iota(jnp.int32, (depth, depth), 1)
        logs = jnp.log(decay)
        upto = (self.row <= self.col).astype(BF16)
        parts = jnp.concatenate(split3(pad_rows(logs, 8)), axis=0).astype(BF16)
        sums = lax.dot_general(parts, upto, (((1,), (0,)), ((), ())), preferred_element_type=F32)
        self.up = (sums[0:8] + sums[8:16] + sums[16:24])[0:cases]
        self.up_ex = self.up - logs
        wide = lambda v: jnp.transpose(pad_rows(v, 8))
        self.up_t = wide(self.up)
        self.up_ex_t = wide(self.up_ex)
        self.keep_t = wide(1.0 - decay)
        self.total = self.up[:, depth - 1 : depth]

    def forward_t(self, c):
        gap = self.up[c : c + 1, :] - self.up_t[:, c : c + 1]
        weight = jnp.exp(jnp.minimum(gap, 0.0)) * self.keep_t[:, c : c + 1]
        return jnp.where(self.col >= self.row, weight, 0.0)


def case_scale(weight_ref, index_ref, c):
    return -3.0 * weight_ref[index_ref[c]]


def faces_kernel(shape, cuts, *refs):
    cases, nx, ny, depth = shape
    (index_hbm, weight_hbm, decay_hbm, density_hbm, mask_hbm, energy_hbm,
     send_ref, own_ref, source_ref, density_ref, mask_ref, map_ref, rows_ref,
     index_ref, weight_ref, decay_ref, energy_ref, small_sem, sem) = refs
    small = [
        pltpu.make_async_copy(decay_hbm, decay_ref, small_sem.at[0]),
        pltpu.make_async_copy(index_hbm, index_ref, small_sem.at[1]),
        pltpu.make_async_copy(weight_hbm, weight_ref, small_sem.at[2]),
    ]
    big = []
    for s, at in enumerate(pl.ds(*cut) for cut in cuts):
        big.append([
            pltpu.make_async_copy(density_hbm.at[at], density_ref.at[at], sem.at[0, s]),
            pltpu.make_async_copy(mask_hbm.at[at], mask_ref.at[at], sem.at[1, s]),
            pltpu.make_async_copy(energy_hbm.at[:, at], energy_ref.at[:, at], sem.at[2, s]),
        ])
    for copy in small:
        copy.start()
    for group in big[:AHEAD]:
        for copy in group:
            copy.start()
    for copy in small:
        copy.wait()

    decay = decay_ref[...]
    slab = Slab(decay)
    for group in big[AHEAD : AHEAD + 1]:
        for copy in group:
            copy.start()
    zero_row = jnp.zeros((1, depth), F32)
    e_rows, h_rows, turns = [], [], []
    for c in range(cases):
        scale = case_scale(weight_ref, index_ref, c)
        f_t = slab.forward_t(c) * scale
        map_ref[c] = f_t
        keep = 1.0 - decay[c : c + 1, :]
        e_row = jnp.exp(slab.total[c : c + 1] - slab.up[c : c + 1, :]) * keep * scale
        b_row = jnp.exp(slab.up_ex[c : c + 1, :]) * keep
        b_hi = b_row.astype(BF16).astype(F32)
        b_two = jnp.concatenate([b_hi, b_row - b_hi] + [zero_row] * 6, axis=0).astype(BF16)
        f_hi, f_lo = split2(f_t)
        twice = lax.dot_general(b_two, f_hi, (((1,), (1,)), ((), ())), preferred_element_type=F32)
        once = lax.dot_general(b_two, f_lo, (((1,), (1,)), ((), ())), preferred_element_type=F32)
        h_row = twice[0:1] + twice[1:2] + once[0:1]
        turns.append(jnp.sum(b_row * jnp.exp(slab.up[c : c + 1, :]), axis=1, keepdims=True))
        place = lambda r: jnp.concatenate([zero_row] * c + [r] + [zero_row] * (cases - 1 - c), axis=1)
        e_rows.append(place(e_row))
        h_rows.append(place(h_row))
    w_hi, w_lo = split2(jnp.concatenate(e_rows + h_rows, axis=0))
    wmat = jnp.concatenate([w_hi, w_lo], axis=0)
    rows_ref[...] = jnp.concatenate([pad_rows(v, 8) for v in (slab.up, slab.up_ex, 1.0 - decay)], axis=0)

    sums = [jnp.zeros((8, depth), F32) for _ in range(cases)]

    def faces_of(at, span):
        faces = lax.dot_general(
            wmat, source_ref[span, :], (((1,), (1,)), ((), ())), preferred_element_type=F32)
        faces = faces[0 : 2 * cases] + faces[2 * cases : 4 * cases]
        own_ref[:, span] = faces
        send_ref[:, span] = faces.astype(BF16)

    for s, (first, bx) in enumerate(cuts):
        cols = bx * ny
        for copy in big[s]:
            copy.wait()
        for group in big[s + AHEAD + 1 : s + AHEAD + 2]:
            for copy in group:
                copy.start()
        at = pl.ds(first, bx)
        mask = mask_ref[at]
        dense = jnp.where(mask == 1, 0.001, jnp.where(mask == 2, 1.0, density_ref[at]))
        cube = dense * dense * dense
        span = pl.ds(first * ny, cols)
        for c in range(cases):
            work = cube * energy_ref[c, at].astype(F32)
            sums[c] = sums[c] + jnp.sum(work.reshape(cols // 8, 8, depth), axis=0)
            source_ref[span, c * depth : (c + 1) * depth] = work.astype(BF16).reshape(cols, depth)
        faces_of(at, span)

    total = jnp.concatenate([jnp.sum(jnp.sum(v, axis=0, keepdims=True), axis=1, keepdims=True) for v in sums], axis=0)
    turn = jnp.concatenate(turns, axis=0)
    aux = put_lanes(split3(jnp.exp(slab.total)) + split3(turn) + split3(total))
    aux = pad_rows(aux, 2 * cases)
    tail = pl.ds(nx * ny, LANES)
    own_ref[:, tail] = aux
    send_ref[:, tail] = aux.astype(BF16)


def row_cuts(nx):
    rows = 16 if nx % 16 == 0 else nx
    return [(start, rows) for start in range(0, nx, rows)]


def faces_call(density, design_mask, energy, decay, case_index, case_weight):
    cases, nx, ny, depth = energy.shape
    cuts = row_cuts(nx)
    width = nx * ny + LANES
    return pl.pallas_call(
        functools.partial(faces_kernel, energy.shape, cuts),
        in_specs=[HBM] * 6,
        out_specs=[VMEM] * 7,
        out_shape=[
            pltpu.VMEM((2 * cases, width), BF16),
            pltpu.VMEM((2 * cases, width), F32),
            pltpu.VMEM((nx * ny, cases * depth), BF16),
            pltpu.VMEM(density.shape, F32),
            pltpu.VMEM(density.shape, jnp.int32),
            pltpu.VMEM((cases, depth, depth), F32),
            pltpu.VMEM((24, depth), F32),
        ],
        scratch_shapes=[
            pltpu.SMEM(case_index.shape, case_index.dtype),
            pltpu.SMEM(case_weight.shape, F32),
            pltpu.VMEM(decay.shape, F32),
            pltpu.VMEM(energy.shape, BF16),
            pltpu.SemaphoreType.DMA((3,)),
            pltpu.SemaphoreType.DMA((3, len(cuts))),
        ],
        compiler_params=pltpu.CompilerParams(vmem_limit_bytes=20 * MIB),
        name="faces",
    )(*in_hbm(case_index, case_weight, decay, density, design_mask, energy))


def local_kernel(shape, bx, source_ref, density_ref, mask_ref, map_ref, rows_ref, t_ref, factor_ref, umap_ref, rmat):
    cases, nx, ny, depth = shape
    steps, cols = nx // bx, bx * ny
    row = lax.broadcasted_iota(jnp.int32, (depth, depth), 0)
    col = lax.broadcasted_iota(jnp.int32, (depth, depth), 1)
    up, up_ex = rows_ref[0:8, :], rows_ref[8:16, :]
    up_ex_t, keep_t = jnp.transpose(up_ex), jnp.transpose(rows_ref[16:24, :])
    total = up[:, depth - 1 : depth]
    lead = jnp.exp(up)
    a_rows = []
    for c in range(cases):
        gap = up_ex_t[:, c : c + 1] - up_ex[c : c + 1, :]
        weight = jnp.exp(jnp.minimum(gap, 0.0)) * keep_t[:, c : c + 1]
        b_t = jnp.where(col <= row, weight, 0.0)
        both = dot_high(jnp.concatenate([map_ref[c], lead], axis=0), b_t)
        hi, lo = split2(both[0:depth])
        rmat[c * depth : (c + 1) * depth, 0:depth] = hi
        rmat[c * depth : (c + 1) * depth, depth : 2 * depth] = lo
        a_rows.append(both[depth + c : depth + c + 1])
    u_all = jnp.concatenate(a_rows + [jnp.exp(total - up_ex)[0:cases]], axis=0)
    u_hi = u_all.astype(BF16).astype(F32)
    umap_ref[...] = jnp.concatenate([u_hi, u_hi, u_all - u_hi, jnp.zeros_like(u_hi)], axis=0).astype(BF16)

    for s in range(steps):
        both = lax.dot_general(
            source_ref[s * cols : (s + 1) * cols, :], rmat[...], (((1,), (0,)), ((), ())),
            preferred_element_type=F32)
        at = slice(s * bx, (s + 1) * bx)
        t_ref[at] = (both[:, 0:depth] + both[:, depth : 2 * depth]).reshape(bx, ny, depth)
        factor_ref[at] = jnp.where(mask_ref[at] == 0, 1.0 / jnp.maximum(density_ref[at], 0.1), 0.0)


def local_call(source, density, mask, maps, rows):
    nx, ny, depth = density.shape
    cases = maps.shape[0]
    return pl.pallas_call(
        functools.partial(local_kernel, (cases, nx, ny, depth), 16),
        in_specs=[VMEM] * 5,
        out_specs=[VMEM] * 3,
        out_shape=[
            pltpu.VMEM(density.shape, F32),
            pltpu.VMEM(density.shape, F32),
            pltpu.VMEM((8 * cases, depth), BF16),
        ],
        scratch_shapes=[pltpu.VMEM((cases * depth, 2 * depth), BF16)],
        compiler_params=pltpu.CompilerParams(vmem_limit_bytes=16 * MIB),
        name="local",
    )(*in_vmem(source, density, mask, maps, rows))


def head_kernel(shape, nslabs, nsends, swapped, *refs):
    cases, nx, ny, depth = shape
    own_ref = refs[0]
    msgs = refs[1:nslabs]
    t_ref, umap_ref, lhs_ref = refs[nslabs : 3 + nslabs]
    sends = refs[3 + nslabs : 3 + nslabs + nsends]
    stack = refs[-1]
    cols = nx * ny
    mine = lax.axis_index("gz")
    low = lax.axis_index("gx") % 2 == 1
    stack[0] = own_ref[...].astype(F32)
    for m, msg in enumerate(reversed(msgs) if swapped else msgs):
        stack[m + 1] = msg[...].astype(F32)
    total = jnp.zeros((cases, 1), F32)
    for m in range(nslabs):
        total = total + sum3(stack[m, 0:cases, cols : cols + LANES], 6)
    state = jnp.zeros((cases, cols), F32)
    entering, above = state, state
    tops, gains = [], []
    for j in range(nslabs):
        at = mine ^ j if swapped else j
        aux = stack[at, 0:cases, cols : cols + LANES]
        gains.append(sum3(aux, 0))
        entering = jnp.where(mine == j, state, entering)
        tops.append(stack[at, cases : 2 * cases, 0:cols] + sum3(aux, 3) * state)
        state = gains[j] * state + stack[at, 0:cases, 0:cols]
    state = jnp.zeros((cases, cols), F32)
    for j in reversed(range(nslabs)):
        above = jnp.where(mine == j, state, above)
        state = tops[j] + gains[j] * state
    faces = jnp.concatenate([entering, above], axis=0)
    hi = faces.astype(BF16).astype(F32)
    lhs_ref[...] = jnp.concatenate([hi, faces - hi, hi, jnp.zeros_like(hi)], axis=0).astype(BF16)
    aux = pad_rows(put_lanes(split3(total)), 16).astype(BF16)
    rows = RADIUS + 1
    wide, edge = rows * ny, RADIUS * ny
    for k, ref in enumerate(sends):
        bottom = low if k == 0 else jnp.logical_not(low)
        start = jnp.where(bottom, 0, nx - rows)
        part = lhs_ref[:, pl.ds(pl.multiple_of(start * ny, wide), wide)]
        add = lax.dot_general(part, umap_ref[...], (((0,), (0,)), ((), ())), preferred_element_type=F32)
        full = t_ref[pl.ds(start, rows)].reshape(wide, depth) + add
        ref[0:edge, :] = jnp.where(bottom, full[0:edge], full[ny:wide]).astype(BF16)
        ref[edge:, :] = aux


def head_call(own, msgs, t_local, umap, nsends, swapped):
    nx, ny, depth = t_local.shape
    cases = own.shape[0] // 2
    nslabs = len(msgs) + 1
    return pl.pallas_call(
        functools.partial(head_kernel, (cases, nx, ny, depth), nslabs, nsends, swapped),
        in_specs=[VMEM] * (nslabs + 2),
        out_specs=[VMEM] * (1 + nsends),
        out_shape=[pltpu.VMEM((8 * cases, nx * ny), BF16)]
        + [jax.ShapeDtypeStruct((RADIUS * ny + 16, depth), BF16)] * nsends,
        scratch_shapes=[pltpu.VMEM((nslabs,) + own.shape, F32)],
        compiler_params=pltpu.CompilerParams(vmem_limit_bytes=20 * MIB),
        name="head",
    )(own, *msgs, *in_vmem(t_local), umap)


def sided(even, got):
    a = got[0]
    b = got[1] if len(got) > 1 else jnp.zeros_like(a)
    return jnp.where(even, b, a), jnp.where(even, a, b)


def edge_kernel(shape, nx_sends, ny_sends, *refs):
    cases, nx, ny, depth = shape
    t_ref = refs[0]
    got_refs = refs[1 : 1 + nx_sends]
    own_send = refs[1 + nx_sends]
    sends = refs[2 + nx_sends : 2 + nx_sends + ny_sends]
    xb_ref, xa_ref, sums_ref, line = refs[2 + nx_sends + ny_sends :]
    taps = taps_1d()
    edge = RADIUS * ny
    even_x = lax.axis_index("gx") % 2 == 0
    flip_y = lax.axis_index("gy") % 2 == 1
    blocks = [r[0:edge, :].astype(F32) for r in got_refs]
    before, after = sided(even_x, blocks)
    xb_ref[...] = before
    xa_ref[...] = after
    total = sum3(own_send[edge : edge + 16, :].astype(F32), 0)
    for ref in got_refs:
        total = total + sum3(ref[edge : edge + 16, :].astype(F32), 0)
    sums_ref[...] = jnp.broadcast_to(total[0:8], (8, LANES))
    aux = put_lanes(split3(total)).astype(BF16)
    flat = t_ref.reshape(nx * ny, depth)
    columns = []
    for k in range(2 * RADIUS):
        y = k if k < RADIUS else ny - 2 * RADIUS + k
        line[8 : 8 + nx, :] = flat[pl.ds(y, nx, stride=ny), :]
        line[8 - RADIUS : 8, :] = xb_ref[pl.ds(y, RADIUS, stride=ny), :]
        line[8 + nx : 8 + nx + RADIUS, :] = xa_ref[pl.ds(y, RADIUS, stride=ny), :]
        acc = taps[RADIUS] * line[8 : 8 + nx, :]
        for d in range(1, RADIUS + 1):
            acc = acc + taps[RADIUS + d] * (line[8 - d : 8 - d + nx, :] + line[8 + d : 8 + d + nx, :])
        columns.append(acc)
    for m, ref in enumerate(sends):
        for k in range(RADIUS):
            first, last = columns[k], columns[RADIUS + k]
            pick = jnp.where(flip_y == (m == 0), first, last)
            ref[k * nx : (k + 1) * nx, :] = pick.astype(BF16)
        ref[RADIUS * nx :, :] = aux


def edge_call(t, got, own_send, ny_sends, cases):
    nx, ny, depth = t.shape
    return pl.pallas_call(
        functools.partial(edge_kernel, (cases, nx, ny, depth), len(got), ny_sends),
        in_specs=[VMEM] * (2 + len(got)),
        out_specs=[VMEM] * (ny_sends + 3),
        out_shape=[jax.ShapeDtypeStruct((RADIUS * nx + 16, depth), BF16)] * ny_sends
        + [jax.ShapeDtypeStruct((RADIUS * ny, depth), F32)] * 2
        + [jax.ShapeDtypeStruct((8, LANES), F32)],
        scratch_shapes=[pltpu.VMEM((nx + 16, depth), F32)],
        compiler_params=pltpu.CompilerParams(vmem_limit_bytes=16 * MIB),
        name="edge",
    )(t, *got, own_send)


def filter_row(ny, read, line, factor):
    taps = taps_1d()
    acc = taps[RADIUS] * read(0)
    for d in range(1, RADIUS + 1):
        acc = acc + taps[RADIUS + d] * (read(-d) + read(d))
    line[8 : 8 + ny, :] = acc
    res = taps[RADIUS] * acc
    for d in range(1, RADIUS + 1):
        res = res + taps[RADIUS + d] * (line[8 - d : 8 - d + ny, :] + line[8 + d : 8 + d + ny, :])
    return res * factor


def clear_line(line, ny):
    zeros = jnp.zeros((8, line.shape[-1]), F32)
    for k in range(line.shape[0]):
        line[k, 0:8, :] = zeros
        line[k, 8 + ny :, :] = zeros


def filter_rows(lo, hi, chunk, read, line, factor_ref, first_ref, last_ref, out_ref, out_hbm, sem):
    ny = factor_ref.shape[1]
    copies = []

    def row(x, carry):
        res = filter_row(ny, lambda d: read(x + d), line.at[x % 2], factor_ref[x])
        out_ref[x] = res
        first_ref[x] = res[0:8]
        last_ref[x] = res[ny - 8 : ny]
        return carry

    for s, start in enumerate(range(lo, hi, chunk)):
        stop = min(start + chunk, hi)
        lax.fori_loop(start, stop, row, 0)
        span = pl.ds(start, stop - start)
        copies.append(pltpu.make_async_copy(out_ref.at[span], out_hbm.at[span], sem.at[s]))
        copies[s].start()
    return copies


def split_row(nx):
    return nx * 9 // 16


def body_kernel(shape, chunk, lhs_ref, umap_ref, part_ref, factor_ref, t_ref, out_hbm, first_ref, last_ref, line, out_ref, sem):
    nx, ny, depth = shape
    add = lax.dot_general(lhs_ref[...], umap_ref[...], (((0,), (0,)), ((), ())), preferred_element_type=F32)
    t_ref[...] = part_ref[...] + add.reshape(nx, ny, depth)
    clear_line(line, ny)
    copies = filter_rows(
        RADIUS, split_row(nx), chunk, lambda x: t_ref[x], line, factor_ref, first_ref, last_ref, out_ref, out_hbm, sem)
    for copy in copies:
        copy.wait()


def body_call(lhs, umap, part, factor):
    nx, ny, depth = part.shape
    chunk = 11
    return pl.pallas_call(
        functools.partial(body_kernel, part.shape, chunk),
        in_specs=[VMEM] * 4,
        out_specs=[VMEM, HBM, VMEM, VMEM],
        out_shape=[
            pltpu.VMEM(part.shape, F32),
            jax.ShapeDtypeStruct(part.shape, F32),
            pltpu.VMEM((nx, 8, depth), F32),
            pltpu.VMEM((nx, 8, depth), F32),
        ],
        scratch_shapes=[
            pltpu.VMEM((2, ny + 16, depth), F32),
            pltpu.VMEM(part.shape, F32),
            pltpu.SemaphoreType.DMA((-(-nx // chunk),)),
        ],
        compiler_params=pltpu.CompilerParams(vmem_limit_bytes=20 * MIB),
        name="body",
    )(*in_vmem(lhs, umap, part, factor))


def rest_kernel(shape, chunk, t_ref, xb_ref, xa_ref, factor_ref, _, __, ___, out_hbm, first_ref, last_ref,
                line, pad, out_ref, sem, side_sem):
    nx, ny, depth = shape
    clear_line(line, ny)
    pad[0:RADIUS] = xb_ref[...].reshape(RADIUS, ny, depth)
    pad[RADIUS : 3 * RADIUS] = t_ref[0 : 2 * RADIUS]
    pad[3 * RADIUS : 5 * RADIUS] = t_ref[nx - 2 * RADIUS : nx]
    pad[5 * RADIUS :] = xa_ref[...].reshape(RADIUS, ny, depth)
    copies = []
    for side, start in ((0, 0), (1, nx - RADIUS)):
        for k in range(RADIUS):
            x = start + k
            mid = (RADIUS if side == 0 else 4 * RADIUS) + k
            res = filter_row(ny, lambda d: pad[mid + d], line.at[x % 2], factor_ref[x])
            out_ref[x] = res
            first_ref[x] = res[0:8]
            last_ref[x] = res[ny - 8 : ny]
        span = pl.ds(start, RADIUS)
        copies.append(pltpu.make_async_copy(out_ref.at[span], out_hbm.at[span], side_sem.at[side]))
        copies[side].start()
    copies += filter_rows(
        split_row(nx), nx - RADIUS, chunk, lambda x: t_ref[x], line, factor_ref, first_ref, last_ref, out_ref, out_hbm, sem)
    for copy in copies:
        copy.wait()


def rest_call(t, xb, xa, factor, out, first, last):
    nx, ny, depth = t.shape
    chunk = 9
    return pl.pallas_call(
        functools.partial(rest_kernel, t.shape, chunk),
        in_specs=[VMEM] * 4 + [HBM, VMEM, VMEM],
        out_specs=[HBM, VMEM, VMEM],
        out_shape=[
            jax.ShapeDtypeStruct(out.shape, F32),
            pltpu.VMEM(first.shape, F32),
            pltpu.VMEM(last.shape, F32),
        ],
        input_output_aliases={4: 0, 5: 1, 6: 2},
        scratch_shapes=[
            pltpu.VMEM((2, ny + 16, depth), F32),
            pltpu.VMEM((6 * RADIUS, ny, depth), F32),
            pltpu.VMEM(t.shape, F32),
            pltpu.SemaphoreType.DMA((-(-nx // chunk),)),
            pltpu.SemaphoreType.DMA((2,)),
        ],
        compiler_params=pltpu.CompilerParams(vmem_limit_bytes=20 * MIB),
        name="rest",
    )(*in_vmem(t, xb, xa, factor), *in_hbm(out), *in_vmem(first, last))


def finish_kernel(shape, ngot, *refs):
    nx, ny, depth = shape
    got_refs = refs[:ngot]
    first_ref, last_ref, factor_ref, _, out_hbm, done_ref, strip, sem = refs[ngot:]
    taps = taps_1d()
    edge = RADIUS * nx
    place, count = lax.axis_index("gy"), lax.axis_size("gy")
    blocks = [r[0:edge, :].astype(F32) for r in got_refs]
    before, after = sided(place % 2 == 0, blocks) if blocks else (jnp.zeros((edge, depth), F32),) * 2
    before = jnp.where(place == 0, 0.0, before)
    after = jnp.where(place == count - 1, 0.0, after)
    flat = factor_ref.reshape(nx * ny, depth)
    copies = []
    for ref, side in ((first_ref, 0), (last_ref, 1)):
        strip[side] = ref[...]
        view = strip.at[side].reshape(nx * 8, depth)
        for y in range(RADIUS):
            add = jnp.zeros((nx, depth), F32)
            for k in range(RADIUS):
                if side == 0:
                    d, halo, own = y + RADIUS - k, before[k * nx : (k + 1) * nx], y
                else:
                    d, halo, own = k + RADIUS - y, after[k * nx : (k + 1) * nx], ny - RADIUS + y
                if d <= RADIUS:
                    add = add + taps[RADIUS + d] * halo
            at = own if side == 0 else own - (ny - 8)
            view[pl.ds(at, nx, stride=8), :] += flat[pl.ds(own, nx, stride=ny), :] * add
        target = out_hbm.at[:, 0:8, :] if side == 0 else out_hbm.at[:, ny - 8 : ny, :]
        copies.append(pltpu.make_async_copy(strip.at[side], target, sem.at[side]))
        copies[side].start()
    done_ref[...] = jnp.zeros_like(done_ref)
    for copy in copies:
        copy.wait()


def finish_call(got, first, last, factor, out):
    nx, ny, depth = out.shape
    nin = len(got)
    return pl.pallas_call(
        functools.partial(finish_kernel, out.shape, len(got)),
        in_specs=[VMEM] * (nin + 3) + [HBM],
        out_specs=[HBM, VMEM],
        out_shape=[jax.ShapeDtypeStruct(out.shape, F32), pltpu.VMEM((8, LANES), F32)],
        input_output_aliases={nin + 3: 0},
        scratch_shapes=[pltpu.VMEM((2, nx, 8, depth), F32), pltpu.SemaphoreType.DMA((2,))],
        compiler_params=pltpu.CompilerParams(vmem_limit_bytes=16 * MIB),
        name="finish",
    )(*got, *in_vmem(first, last, factor), *in_hbm(out))


def mean_kernel(cells, cases, *refs):
    total = refs[0][...]
    for ref in refs[2:-1]:
        block = ref[...] if ref.shape[0] == 8 else sum3(ref[ref.shape[0] - 16 :, :].astype(F32), 0)[0:8]
        total = total + block
    for c in range(cases):
        refs[-1][c] = total[c, 0] / cells


def mean_call(sums, behind, got, cells, cases):
    return pl.pallas_call(
        functools.partial(mean_kernel, cells, cases),
        in_specs=[VMEM] * (2 + len(got)),
        out_specs=SMEM,
        out_shape=jax.ShapeDtypeStruct((cases,), F32),
        compiler_params=pltpu.CompilerParams(vmem_limit_bytes=4 * MIB),
        name="mean",
    )(sums, behind, *got)


def swap_pairs(count, first):
    return [q for i in range(first, count - 1, 2) for q in ((i, i + 1), (i + 1, i))]


def swaps_of(count):
    return min(count - 1, 2)


def xor_pairs(count, m):
    return [(i, i ^ m) for i in range(count)]


def shards(density, design_mask, energy, decay, case_index, case_weight):
    cases = energy.shape[0]
    nx, ny, depth = density.shape
    nz, gx, gy = (lax.axis_size(a) for a in ("gz", "gx", "gy"))
    send, own, source, density_v, mask_v, maps, rows = faces_call(
        density, design_mask, energy, decay, case_index, case_weight)
    swapped = nz in (1, 2, 4)
    if swapped:
        msgs = [lax.ppermute(send, "gz", xor_pairs(nz, m)) for m in range(nz - 1, 0, -1)]
    else:
        every = lax.all_gather(send, "gz")
        own, *msgs = [every[j] for j in range(nz)]
    part, factor, umap = local_call(source, density_v, mask_v, maps, rows)
    lhs, *x_sends = head_call(own, msgs, part, umap, max(swaps_of(gx), 1), swapped)
    x_got = [lax.ppermute(x_sends[k], "gx", swap_pairs(gx, k)) for k in range(swaps_of(gx))]
    t, out, first, last = body_call(lhs, umap, part, factor)
    *y_sends, xb, xa, sums = edge_call(t, x_got, x_sends[0], swaps_of(gy), cases)
    ring = gy == 4
    ends = [(0, gy - 1), (gy - 1, 0)] if ring else []
    y_got = [lax.ppermute(y_sends[k], "gy", swap_pairs(gy, k) + (ends if k else [])) for k in range(swaps_of(gy))]
    out, first, last = rest_call(t, xb, xa, factor, out, first, last)
    if ring:
        y_got[1], first = lax.optimization_barrier((y_got[1], first))
        more = y_got + [lax.ppermute(y_got[1], "gy", swap_pairs(gy, 0))]
    else:
        more = [lax.ppermute(sums, "gy", xor_pairs(gy, m)) for m in range(1, gy)]
    out, behind = finish_call(y_got, first, last, factor, out)
    cells = nx * ny * depth * nz * gx * gy
    return out, mean_call(sums, behind, more, float(cells), cases)


def solution(mesh):
    placed = (
        P("gx", "gy", "gz"),
        P("gx", "gy", "gz"),
        P(None, "gx", "gy", "gz"),
        P(None, "gz"),
        P(),
        P(),
    )
    return jax.shard_map(
        shards, mesh=mesh, in_specs=placed, out_specs=(P("gx", "gy", "gz"), P()), check_vma=False
    )
```

```python
import functools
import math
import jax
import jax.numpy as jnp
from jax import lax
from jax.experimental import pallas as pl
from jax.experimental.pallas import tpu as pltpu
from jax.sharding import PartitionSpec as P

RADIUS = 3
AHEAD = 2
LANES = 128
MIB = 2**20
F32 = jnp.float32
BF16 = jnp.bfloat16
HIGH = lax.Precision.HIGHEST
HBM = pl.BlockSpec(memory_space=pltpu.HBM)
VMEM = pl.BlockSpec(memory_space=pltpu.VMEM)
SMEM = pl.BlockSpec(memory_space=pltpu.SMEM)


def in_hbm(*arrays):
    return [pltpu.with_memory_space_constraint(a, pltpu.HBM) for a in arrays]


def in_vmem(*arrays):
    return [pltpu.with_memory_space_constraint(a, pltpu.VMEM) for a in arrays]


def taps_1d():
    raw = [math.exp(-2.0 * k * k / (RADIUS * RADIUS)) for k in range(-RADIUS, RADIUS + 1)]
    total = sum(raw)
    return [r / total for r in raw]


def dot_high(a, b, dims=((1,), (0,))):
    return lax.dot_general(a, b, (dims, ((), ())), precision=HIGH, preferred_element_type=F32)


def split2(v):
    hi = v.astype(BF16)
    return hi, (v - hi.astype(F32)).astype(BF16)


def split3(v):
    a = v.astype(BF16).astype(F32)
    b = (v - a).astype(BF16).astype(F32)
    return a, b, v - a - b


def put_lanes(columns):
    rows = columns[0].shape[0]
    lane = lax.broadcasted_iota(jnp.int32, (rows, LANES), 1)
    out = jnp.zeros((rows, LANES), F32)
    for k, col in enumerate(columns):
        out = jnp.where(lane == k, col, out)
    return out


def pad_rows(v, rows):
    return jnp.concatenate([v, jnp.zeros((rows - v.shape[0],) + v.shape[1:], v.dtype)], axis=0)


def sum3(block, at):
    return block[:, at : at + 1] + block[:, at + 1 : at + 2] + block[:, at + 2 : at + 3]


class Slab:
    def __init__(self, decay):
        cases, depth = decay.shape
        self.decay = decay
        self.row = lax.broadcasted_iota(jnp.int32, (depth, depth), 0)
        self.col = lax.broadcasted_iota(jnp.int32, (depth, depth), 1)
        logs = jnp.log(decay)
        upto = (self.row <= self.col).astype(BF16)
        parts = jnp.concatenate(split3(pad_rows(logs, 8)), axis=0).astype(BF16)
        sums = lax.dot_general(parts, upto, (((1,), (0,)), ((), ())), preferred_element_type=F32)
        self.up = (sums[0:8] + sums[8:16] + sums[16:24])[0:cases]
        self.up_ex = self.up - logs
        wide = lambda v: jnp.transpose(pad_rows(v, 8))
        self.up_t = wide(self.up)
        self.up_ex_t = wide(self.up_ex)
        self.keep_t = wide(1.0 - decay)
        self.total = self.up[:, depth - 1 : depth]

    def forward_t(self, c):
        gap = self.up[c : c + 1, :] - self.up_t[:, c : c + 1]
        weight = jnp.exp(jnp.minimum(gap, 0.0)) * self.keep_t[:, c : c + 1]
        return jnp.where(self.col >= self.row, weight, 0.0)


def case_scale(weight_ref, index_ref, c):
    return -3.0 * weight_ref[index_ref[c]]


def faces_kernel(shape, cuts, *refs):
    cases, nx, ny, depth = shape
    (index_hbm, weight_hbm, decay_hbm, density_hbm, mask_hbm, energy_hbm,
     send_ref, own_ref, source_ref, density_ref, mask_ref, map_ref, rows_ref,
     index_ref, weight_ref, decay_ref, energy_ref, small_sem, sem) = refs
    small = [
        pltpu.make_async_copy(decay_hbm, decay_ref, small_sem.at[0]),
        pltpu.make_async_copy(index_hbm, index_ref, small_sem.at[1]),
        pltpu.make_async_copy(weight_hbm, weight_ref, small_sem.at[2]),
    ]
    big = []
    for s, at in enumerate(pl.ds(*cut) for cut in cuts):
        big.append([
            pltpu.make_async_copy(density_hbm.at[at], density_ref.at[at], sem.at[0, s]),
            pltpu.make_async_copy(mask_hbm.at[at], mask_ref.at[at], sem.at[1, s]),
            pltpu.make_async_copy(energy_hbm.at[:, at], energy_ref.at[:, at], sem.at[2, s]),
        ])
    for copy in small:
        copy.start()
    for group in big[:AHEAD]:
        for copy in group:
            copy.start()
    for copy in small:
        copy.wait()

    decay = decay_ref[...]
    slab = Slab(decay)
    for group in big[AHEAD : AHEAD + 1]:
        for copy in group:
            copy.start()
    zero_row = jnp.zeros((1, depth), F32)
    e_rows, h_rows, turns = [], [], []
    for c in range(cases):
        scale = case_scale(weight_ref, index_ref, c)
        f_t = slab.forward_t(c) * scale
        map_ref[c] = f_t
        keep = 1.0 - decay[c : c + 1, :]
        e_row = jnp.exp(slab.total[c : c + 1] - slab.up[c : c + 1, :]) * keep * scale
        b_row = jnp.exp(slab.up_ex[c : c + 1, :]) * keep
        b_hi = b_row.astype(BF16).astype(F32)
        b_two = jnp.concatenate([b_hi, b_row - b_hi] + [zero_row] * 6, axis=0).astype(BF16)
        f_hi, f_lo = split2(f_t)
        twice = lax.dot_general(b_two, f_hi, (((1,), (1,)), ((), ())), preferred_element_type=F32)
        once = lax.dot_general(b_two, f_lo, (((1,), (1,)), ((), ())), preferred_element_type=F32)
        h_row = twice[0:1] + twice[1:2] + once[0:1]
        turns.append(jnp.sum(b_row * jnp.exp(slab.up[c : c + 1, :]), axis=1, keepdims=True))
        place = lambda r: jnp.concatenate([zero_row] * c + [r] + [zero_row] * (cases - 1 - c), axis=1)
        e_rows.append(place(e_row))
        h_rows.append(place(h_row))
    w_hi, w_lo = split2(jnp.concatenate(e_rows + h_rows, axis=0))
    wmat = jnp.concatenate([w_hi, w_lo], axis=0)
    rows_ref[...] = jnp.concatenate([pad_rows(v, 8) for v in (slab.up, slab.up_ex, 1.0 - decay)], axis=0)

    sums = [jnp.zeros((8, depth), F32) for _ in range(cases)]

    def faces_of(at, span):
        faces = lax.dot_general(
            wmat, source_ref[span, :], (((1,), (1,)), ((), ())), preferred_element_type=F32)
        faces = faces[0 : 2 * cases] + faces[2 * cases : 4 * cases]
        own_ref[:, span] = faces
        send_ref[:, span] = faces.astype(BF16)

    for s, (first, bx) in enumerate(cuts):
        cols = bx * ny
        for copy in big[s]:
            copy.wait()
        for group in big[s + AHEAD + 1 : s + AHEAD + 2]:
            for copy in group:
                copy.start()
        at = pl.ds(first, bx)
        mask = mask_ref[at]
        dense = jnp.where(mask == 1, 0.001, jnp.where(mask == 2, 1.0, density_ref[at]))
        cube = dense * dense * dense
        span = pl.ds(first * ny, cols)
        for c in range(cases):
            work = cube * energy_ref[c, at].astype(F32)
            sums[c] = sums[c] + jnp.sum(work.reshape(cols // 8, 8, depth), axis=0)
            source_ref[span, c * depth : (c + 1) * depth] = work.astype(BF16).reshape(cols, depth)
        faces_of(at, span)

    total = jnp.concatenate([jnp.sum(jnp.sum(v, axis=0, keepdims=True), axis=1, keepdims=True) for v in sums], axis=0)
    turn = jnp.concatenate(turns, axis=0)
    aux = put_lanes(split3(jnp.exp(slab.total)) + split3(turn) + split3(total))
    aux = pad_rows(aux, 2 * cases)
    tail = pl.ds(nx * ny, LANES)
    own_ref[:, tail] = aux
    send_ref[:, tail] = aux.astype(BF16)


def row_cuts(nx):
    rows = 16 if nx % 16 == 0 else nx
    return [(start, rows) for start in range(0, nx, rows)]


def faces_call(density, design_mask, energy, decay, case_index, case_weight):
    cases, nx, ny, depth = energy.shape
    cuts = row_cuts(nx)
    width = nx * ny + LANES
    return pl.pallas_call(
        functools.partial(faces_kernel, energy.shape, cuts),
        in_specs=[HBM] * 6,
        out_specs=[VMEM] * 7,
        out_shape=[
            pltpu.VMEM((2 * cases, width), BF16),
            pltpu.VMEM((2 * cases, width), F32),
            pltpu.VMEM((nx * ny, cases * depth), BF16),
            pltpu.VMEM(density.shape, F32),
            pltpu.VMEM(density.shape, jnp.int32),
            pltpu.VMEM((cases, depth, depth), F32),
            pltpu.VMEM((24, depth), F32),
        ],
        scratch_shapes=[
            pltpu.SMEM(case_index.shape, case_index.dtype),
            pltpu.SMEM(case_weight.shape, F32),
            pltpu.VMEM(decay.shape, F32),
            pltpu.VMEM(energy.shape, BF16),
            pltpu.SemaphoreType.DMA((3,)),
            pltpu.SemaphoreType.DMA((3, len(cuts))),
        ],
        compiler_params=pltpu.CompilerParams(vmem_limit_bytes=20 * MIB),
        name="faces",
    )(*in_hbm(case_index, case_weight, decay, density, design_mask, energy))


def local_kernel(shape, bx, source_ref, density_ref, mask_ref, map_ref, rows_ref, t_ref, factor_ref, umap_ref, rmat):
    cases, nx, ny, depth = shape
    steps, cols = nx // bx, bx * ny
    row = lax.broadcasted_iota(jnp.int32, (depth, depth), 0)
    col = lax.broadcasted_iota(jnp.int32, (depth, depth), 1)
    up, up_ex = rows_ref[0:8, :], rows_ref[8:16, :]
    up_ex_t, keep_t = jnp.transpose(up_ex), jnp.transpose(rows_ref[16:24, :])
    total = up[:, depth - 1 : depth]
    lead = jnp.exp(up)
    a_rows = []
    for c in range(cases):
        gap = up_ex_t[:, c : c + 1] - up_ex[c : c + 1, :]
        weight = jnp.exp(jnp.minimum(gap, 0.0)) * keep_t[:, c : c + 1]
        b_t = jnp.where(col <= row, weight, 0.0)
        both = dot_high(jnp.concatenate([map_ref[c], lead], axis=0), b_t)
        hi, lo = split2(both[0:depth])
        rmat[c * depth : (c + 1) * depth, 0:depth] = hi
        rmat[c * depth : (c + 1) * depth, depth : 2 * depth] = lo
        a_rows.append(both[depth + c : depth + c + 1])
    u_all = jnp.concatenate(a_rows + [jnp.exp(total - up_ex)[0:cases]], axis=0)
    u_hi = u_all.astype(BF16).astype(F32)
    umap_ref[...] = jnp.concatenate([u_hi, u_hi, u_all - u_hi, jnp.zeros_like(u_hi)], axis=0).astype(BF16)

    for s in range(steps):
        both = lax.dot_general(
            source_ref[s * cols : (s + 1) * cols, :], rmat[...], (((1,), (0,)), ((), ())),
            preferred_element_type=F32)
        at = slice(s * bx, (s + 1) * bx)
        t_ref[at] = (both[:, 0:depth] + both[:, depth : 2 * depth]).reshape(bx, ny, depth)
        factor_ref[at] = jnp.where(mask_ref[at] == 0, 1.0 / jnp.maximum(density_ref[at], 0.1), 0.0)


def local_call(source, density, mask, maps, rows):
    nx, ny, depth = density.shape
    cases = maps.shape[0]
    return pl.pallas_call(
        functools.partial(local_kernel, (cases, nx, ny, depth), 16),
        in_specs=[VMEM] * 5,
        out_specs=[VMEM] * 3,
        out_shape=[
            pltpu.VMEM(density.shape, F32),
            pltpu.VMEM(density.shape, F32),
            pltpu.VMEM((8 * cases, depth), BF16),
        ],
        scratch_shapes=[pltpu.VMEM((cases * depth, 2 * depth), BF16)],
        compiler_params=pltpu.CompilerParams(vmem_limit_bytes=16 * MIB),
        name="local",
    )(*in_vmem(source, density, mask, maps, rows))


def head_kernel(shape, nslabs, nsends, swapped, *refs):
    cases, nx, ny, depth = shape
    own_ref = refs[0]
    msgs = refs[1:nslabs]
    t_ref, umap_ref, lhs_ref = refs[nslabs : 3 + nslabs]
    sends = refs[3 + nslabs : 3 + nslabs + nsends]
    stack = refs[-1]
    cols = nx * ny
    mine = lax.axis_index("gz")
    low = lax.axis_index("gx") % 2 == 1
    stack[0] = own_ref[...].astype(F32)
    for m, msg in zip(swap_order(nslabs) if swapped else range(1, nslabs), msgs):
        stack[m] = msg[...].astype(F32)
    total = jnp.zeros((cases, 1), F32)
    for m in range(nslabs):
        total = total + sum3(stack[m, 0:cases, cols : cols + LANES], 6)
    state = jnp.zeros((cases, cols), F32)
    entering, above = state, state
    tops, gains = [], []
    for j in range(nslabs):
        at = mine ^ j if swapped else j
        aux = stack[at, 0:cases, cols : cols + LANES]
        gains.append(sum3(aux, 0))
        entering = jnp.where(mine == j, state, entering)
        tops.append(stack[at, cases : 2 * cases, 0:cols] + sum3(aux, 3) * state)
        state = gains[j] * state + stack[at, 0:cases, 0:cols]
    state = jnp.zeros((cases, cols), F32)
    for j in reversed(range(nslabs)):
        above = jnp.where(mine == j, state, above)
        state = tops[j] + gains[j] * state
    faces = jnp.concatenate([entering, above], axis=0)
    hi = faces.astype(BF16).astype(F32)
    lhs_ref[...] = jnp.concatenate([hi, faces - hi, hi, jnp.zeros_like(hi)], axis=0).astype(BF16)
    aux = pad_rows(put_lanes(split3(total)), 16).astype(BF16)
    rows = RADIUS + 1
    wide, edge = rows * ny, RADIUS * ny
    for k, ref in enumerate(sends):
        bottom = low if k == 0 else jnp.logical_not(low)
        start = jnp.where(bottom, 0, nx - rows)
        part = lhs_ref[:, pl.ds(pl.multiple_of(start * ny, wide), wide)]
        add = lax.dot_general(part, umap_ref[...], (((0,), (0,)), ((), ())), preferred_element_type=F32)
        full = t_ref[pl.ds(start, rows)].reshape(wide, depth) + add
        ref[0:edge, :] = jnp.where(bottom, full[0:edge], full[ny:wide]).astype(BF16)
        ref[edge:, :] = aux


def head_call(own, msgs, t_local, umap, nsends, swapped):
    nx, ny, depth = t_local.shape
    cases = own.shape[0] // 2
    nslabs = len(msgs) + 1
    return pl.pallas_call(
        functools.partial(head_kernel, (cases, nx, ny, depth), nslabs, nsends, swapped),
        in_specs=[VMEM] * (nslabs + 2),
        out_specs=[VMEM] * (1 + nsends),
        out_shape=[pltpu.VMEM((8 * cases, nx * ny), BF16)]
        + [jax.ShapeDtypeStruct((RADIUS * ny + 16, depth), BF16)] * nsends,
        scratch_shapes=[pltpu.VMEM((nslabs,) + own.shape, F32)],
        compiler_params=pltpu.CompilerParams(vmem_limit_bytes=20 * MIB),
        name="head",
    )(own, *msgs, *in_vmem(t_local), umap)


def sided(even, got):
    a = got[0]
    b = got[1] if len(got) > 1 else jnp.zeros_like(a)
    return jnp.where(even, b, a), jnp.where(even, a, b)


def edge_kernel(shape, nx_sends, ny_sends, *refs):
    cases, nx, ny, depth = shape
    t_ref = refs[0]
    got_refs = refs[1 : 1 + nx_sends]
    own_send = refs[1 + nx_sends]
    sends = refs[2 + nx_sends : 2 + nx_sends + ny_sends]
    xb_ref, xa_ref, sums_ref, line = refs[2 + nx_sends + ny_sends :]
    taps = taps_1d()
    edge = RADIUS * ny
    even_x = lax.axis_index("gx") % 2 == 0
    flip_y = lax.axis_index("gy") % 2 == 1
    blocks = [r[0:edge, :].astype(F32) for r in got_refs]
    before, after = sided(even_x, blocks)
    xb_ref[...] = before
    xa_ref[...] = after
    total = sum3(own_send[edge : edge + 16, :].astype(F32), 0)
    for ref in got_refs:
        total = total + sum3(ref[edge : edge + 16, :].astype(F32), 0)
    sums_ref[...] = jnp.broadcast_to(total[0:8], (8, LANES))
    aux = put_lanes(split3(total)).astype(BF16)
    flat = t_ref.reshape(nx * ny, depth)
    columns = []
    for k in range(2 * RADIUS):
        y = k if k < RADIUS else ny - 2 * RADIUS + k
        line[8 : 8 + nx, :] = flat[pl.ds(y, nx, stride=ny), :]
        line[8 - RADIUS : 8, :] = xb_ref[pl.ds(y, RADIUS, stride=ny), :]
        line[8 + nx : 8 + nx + RADIUS, :] = xa_ref[pl.ds(y, RADIUS, stride=ny), :]
        acc = taps[RADIUS] * line[8 : 8 + nx, :]
        for d in range(1, RADIUS + 1):
            acc = acc + taps[RADIUS + d] * (line[8 - d : 8 - d + nx, :] + line[8 + d : 8 + d + nx, :])
        columns.append(acc)
    for m, ref in enumerate(sends):
        for k in range(RADIUS):
            first, last = columns[k], columns[RADIUS + k]
            pick = jnp.where(flip_y == (m == 0), first, last)
            ref[k * nx : (k + 1) * nx, :] = pick.astype(BF16)
        ref[RADIUS * nx :, :] = aux


def edge_call(t, got, own_send, ny_sends, cases):
    nx, ny, depth = t.shape
    return pl.pallas_call(
        functools.partial(edge_kernel, (cases, nx, ny, depth), len(got), ny_sends),
        in_specs=[VMEM] * (2 + len(got)),
        out_specs=[VMEM] * (ny_sends + 3),
        out_shape=[jax.ShapeDtypeStruct((RADIUS * nx + 16, depth), BF16)] * ny_sends
        + [jax.ShapeDtypeStruct((RADIUS * ny, depth), F32)] * 2
        + [jax.ShapeDtypeStruct((8, LANES), F32)],
        scratch_shapes=[pltpu.VMEM((nx + 16, depth), F32)],
        compiler_params=pltpu.CompilerParams(vmem_limit_bytes=16 * MIB),
        name="edge",
    )(t, *got, own_send)


def filter_row(ny, read, line, factor):
    taps = taps_1d()
    acc = taps[RADIUS] * read(0)
    for d in range(1, RADIUS + 1):
        acc = acc + taps[RADIUS + d] * (read(-d) + read(d))
    line[8 : 8 + ny, :] = acc
    res = taps[RADIUS] * acc
    for d in range(1, RADIUS + 1):
        res = res + taps[RADIUS + d] * (line[8 - d : 8 - d + ny, :] + line[8 + d : 8 + d + ny, :])
    return res * factor


def clear_line(line, ny):
    zeros = jnp.zeros((8, line.shape[-1]), F32)
    for k in range(line.shape[0]):
        line[k, 0:8, :] = zeros
        line[k, 8 + ny :, :] = zeros


def filter_rows(lo, hi, chunk, read, line, factor_ref, first_ref, last_ref, out_ref, out_hbm, sem):
    ny = factor_ref.shape[1]
    copies = []

    def row(x, carry):
        res = filter_row(ny, lambda d: read(x + d), line.at[x % 2], factor_ref[x])
        out_ref[x] = res
        first_ref[x] = res[0:8]
        last_ref[x] = res[ny - 8 : ny]
        return carry

    for s, start in enumerate(range(lo, hi, chunk)):
        stop = min(start + chunk, hi)
        lax.fori_loop(start, stop, row, 0)
        span = pl.ds(start, stop - start)
        copies.append(pltpu.make_async_copy(out_ref.at[span], out_hbm.at[span], sem.at[s]))
        copies[s].start()
    return copies


def split_row(nx):
    return nx * 9 // 16


def body_kernel(shape, chunk, lhs_ref, umap_ref, part_ref, factor_ref, t_ref, out_hbm, first_ref, last_ref, line, out_ref, sem):
    nx, ny, depth = shape
    add = lax.dot_general(lhs_ref[...], umap_ref[...], (((0,), (0,)), ((), ())), preferred_element_type=F32)
    t_ref[...] = part_ref[...] + add.reshape(nx, ny, depth)
    clear_line(line, ny)
    copies = filter_rows(
        RADIUS, split_row(nx), chunk, lambda x: t_ref[x], line, factor_ref, first_ref, last_ref, out_ref, out_hbm, sem)
    for copy in copies:
        copy.wait()


def body_call(lhs, umap, part, factor):
    nx, ny, depth = part.shape
    chunk = 11
    return pl.pallas_call(
        functools.partial(body_kernel, part.shape, chunk),
        in_specs=[VMEM] * 4,
        out_specs=[VMEM, HBM, VMEM, VMEM],
        out_shape=[
            pltpu.VMEM(part.shape, F32),
            jax.ShapeDtypeStruct(part.shape, F32),
            pltpu.VMEM((nx, 8, depth), F32),
            pltpu.VMEM((nx, 8, depth), F32),
        ],
        scratch_shapes=[
            pltpu.VMEM((2, ny + 16, depth), F32),
            pltpu.VMEM(part.shape, F32),
            pltpu.SemaphoreType.DMA((-(-nx // chunk),)),
        ],
        compiler_params=pltpu.CompilerParams(vmem_limit_bytes=20 * MIB),
        name="body",
    )(*in_vmem(lhs, umap, part, factor))


def rest_kernel(shape, chunk, t_ref, xb_ref, xa_ref, factor_ref, _, __, ___, out_hbm, first_ref, last_ref,
                line, pad, out_ref, sem, side_sem):
    nx, ny, depth = shape
    clear_line(line, ny)
    pad[0:RADIUS] = xb_ref[...].reshape(RADIUS, ny, depth)
    pad[RADIUS : 3 * RADIUS] = t_ref[0 : 2 * RADIUS]
    pad[3 * RADIUS : 5 * RADIUS] = t_ref[nx - 2 * RADIUS : nx]
    pad[5 * RADIUS :] = xa_ref[...].reshape(RADIUS, ny, depth)
    copies = []
    for side, start in ((0, 0), (1, nx - RADIUS)):
        for k in range(RADIUS):
            x = start + k
            mid = (RADIUS if side == 0 else 4 * RADIUS) + k
            res = filter_row(ny, lambda d: pad[mid + d], line.at[x % 2], factor_ref[x])
            out_ref[x] = res
            first_ref[x] = res[0:8]
            last_ref[x] = res[ny - 8 : ny]
        span = pl.ds(start, RADIUS)
        copies.append(pltpu.make_async_copy(out_ref.at[span], out_hbm.at[span], side_sem.at[side]))
        copies[side].start()
    copies += filter_rows(
        split_row(nx), nx - RADIUS, chunk, lambda x: t_ref[x], line, factor_ref, first_ref, last_ref, out_ref, out_hbm, sem)
    for copy in copies:
        copy.wait()


def rest_call(t, xb, xa, factor, out, first, last):
    nx, ny, depth = t.shape
    chunk = 9
    return pl.pallas_call(
        functools.partial(rest_kernel, t.shape, chunk),
        in_specs=[VMEM] * 4 + [HBM, VMEM, VMEM],
        out_specs=[HBM, VMEM, VMEM],
        out_shape=[
            jax.ShapeDtypeStruct(out.shape, F32),
            pltpu.VMEM(first.shape, F32),
            pltpu.VMEM(last.shape, F32),
        ],
        input_output_aliases={4: 0, 5: 1, 6: 2},
        scratch_shapes=[
            pltpu.VMEM((2, ny + 16, depth), F32),
            pltpu.VMEM((6 * RADIUS, ny, depth), F32),
            pltpu.VMEM(t.shape, F32),
            pltpu.SemaphoreType.DMA((-(-nx // chunk),)),
            pltpu.SemaphoreType.DMA((2,)),
        ],
        compiler_params=pltpu.CompilerParams(vmem_limit_bytes=20 * MIB),
        name="rest",
    )(*in_vmem(t, xb, xa, factor), *in_hbm(out), *in_vmem(first, last))


def finish_kernel(shape, ngot, *refs):
    nx, ny, depth = shape
    got_refs = refs[:ngot]
    first_ref, last_ref, factor_ref, _, out_hbm, done_ref, strip, sem = refs[ngot:]
    taps = taps_1d()
    edge = RADIUS * nx
    place, count = lax.axis_index("gy"), lax.axis_size("gy")
    blocks = [r[0:edge, :].astype(F32) for r in got_refs]
    before, after = sided(place % 2 == 0, blocks) if blocks else (jnp.zeros((edge, depth), F32),) * 2
    before = jnp.where(place == 0, 0.0, before)
    after = jnp.where(place == count - 1, 0.0, after)
    flat = factor_ref.reshape(nx * ny, depth)
    copies = []
    for ref, side in ((first_ref, 0), (last_ref, 1)):
        strip[side] = ref[...]
        view = strip.at[side].reshape(nx * 8, depth)
        for y in range(RADIUS):
            add = jnp.zeros((nx, depth), F32)
            for k in range(RADIUS):
                if side == 0:
                    d, halo, own = y + RADIUS - k, before[k * nx : (k + 1) * nx], y
                else:
                    d, halo, own = k + RADIUS - y, after[k * nx : (k + 1) * nx], ny - RADIUS + y
                if d <= RADIUS:
                    add = add + taps[RADIUS + d] * halo
            at = own if side == 0 else own - (ny - 8)
            view[pl.ds(at, nx, stride=8), :] += flat[pl.ds(own, nx, stride=ny), :] * add
        target = out_hbm.at[:, 0:8, :] if side == 0 else out_hbm.at[:, ny - 8 : ny, :]
        copies.append(pltpu.make_async_copy(strip.at[side], target, sem.at[side]))
        copies[side].start()
    done_ref[...] = jnp.zeros_like(done_ref)
    for copy in copies:
        copy.wait()


def finish_call(got, first, last, factor, out):
    nx, ny, depth = out.shape
    nin = len(got)
    return pl.pallas_call(
        functools.partial(finish_kernel, out.shape, len(got)),
        in_specs=[VMEM] * (nin + 3) + [HBM],
        out_specs=[HBM, VMEM],
        out_shape=[jax.ShapeDtypeStruct(out.shape, F32), pltpu.VMEM((8, LANES), F32)],
        input_output_aliases={nin + 3: 0},
        scratch_shapes=[pltpu.VMEM((2, nx, 8, depth), F32), pltpu.SemaphoreType.DMA((2,))],
        compiler_params=pltpu.CompilerParams(vmem_limit_bytes=16 * MIB),
        name="finish",
    )(*got, *in_vmem(first, last, factor), *in_hbm(out))


def mean_kernel(cells, cases, *refs):
    total = refs[0][...]
    for ref in refs[2:-1]:
        block = ref[...] if ref.shape[0] == 8 else sum3(ref[ref.shape[0] - 16 :, :].astype(F32), 0)[0:8]
        total = total + block
    for c in range(cases):
        refs[-1][c] = total[c, 0] / cells


def mean_call(sums, behind, got, cells, cases):
    return pl.pallas_call(
        functools.partial(mean_kernel, cells, cases),
        in_specs=[VMEM] * (2 + len(got)),
        out_specs=SMEM,
        out_shape=jax.ShapeDtypeStruct((cases,), F32),
        compiler_params=pltpu.CompilerParams(vmem_limit_bytes=4 * MIB),
        name="mean",
    )(sums, behind, *got)


def swap_pairs(count, first):
    return [q for i in range(first, count - 1, 2) for q in ((i, i + 1), (i + 1, i))]


def swaps_of(count):
    return min(count - 1, 2)


def swap_order(count):
    return {1: (), 2: (1,), 4: (2, 3, 1)}[count]


def xor_pairs(count, m):
    return [(i, i ^ m) for i in range(count)]


def shards(density, design_mask, energy, decay, case_index, case_weight):
    cases = energy.shape[0]
    nx, ny, depth = density.shape
    nz, gx, gy = (lax.axis_size(a) for a in ("gz", "gx", "gy"))
    send, own, source, density_v, mask_v, maps, rows = faces_call(
        density, design_mask, energy, decay, case_index, case_weight)
    swapped = nz in (1, 2, 4)
    if swapped:
        msgs = [lax.ppermute(send, "gz", xor_pairs(nz, m)) for m in swap_order(nz)]
    else:
        every = lax.all_gather(send, "gz")
        own, *msgs = [every[j] for j in range(nz)]
    part, factor, umap = local_call(source, density_v, mask_v, maps, rows)
    lhs, *x_sends = head_call(own, msgs, part, umap, max(swaps_of(gx), 1), swapped)
    x_got = [lax.ppermute(x_sends[k], "gx", swap_pairs(gx, k)) for k in range(swaps_of(gx))]
    t, out, first, last = body_call(lhs, umap, part, factor)
    *y_sends, xb, xa, sums = edge_call(t, x_got, x_sends[0], swaps_of(gy), cases)
    ring = gy == 4
    ends = [(0, gy - 1), (gy - 1, 0)] if ring else []
    y_got = [lax.ppermute(y_sends[k], "gy", swap_pairs(gy, k) + (ends if k else [])) for k in range(swaps_of(gy))]
    out, first, last = rest_call(t, xb, xa, factor, out, first, last)
    if ring:
        y_got[1], first = lax.optimization_barrier((y_got[1], first))
        more = y_got + [lax.ppermute(y_got[1], "gy", swap_pairs(gy, 0))]
    else:
        more = [lax.ppermute(sums, "gy", xor_pairs(gy, m)) for m in range(1, gy)]
    out, behind = finish_call(y_got, first, last, factor, out)
    cells = nx * ny * depth * nz * gx * gy
    return out, mean_call(sums, behind, more, float(cells), cases)


def solution(mesh):
    placed = (
        P("gx", "gy", "gz"),
        P("gx", "gy", "gz"),
        P(None, "gx", "gy", "gz"),
        P(None, "gz"),
        P(),
        P(),
    )
    return jax.shard_map(
        shards, mesh=mesh, in_specs=placed, out_specs=(P("gx", "gy", "gz"), P()), check_vma=False
    )
```

```python
import functools
import math
import jax
import jax.numpy as jnp
from jax import lax
from jax.experimental import pallas as pl
from jax.experimental.pallas import tpu as pltpu
from jax.sharding import PartitionSpec as P

RADIUS = 3
AHEAD = 2
LANES = 128
MIB = 2**20
F32 = jnp.float32
BF16 = jnp.bfloat16
HIGH = lax.Precision.HIGHEST
HBM = pl.BlockSpec(memory_space=pltpu.HBM)
VMEM = pl.BlockSpec(memory_space=pltpu.VMEM)
SMEM = pl.BlockSpec(memory_space=pltpu.SMEM)


def in_hbm(*arrays):
    return [pltpu.with_memory_space_constraint(a, pltpu.HBM) for a in arrays]


def in_vmem(*arrays):
    return [pltpu.with_memory_space_constraint(a, pltpu.VMEM) for a in arrays]


def taps_1d():
    raw = [math.exp(-2.0 * k * k / (RADIUS * RADIUS)) for k in range(-RADIUS, RADIUS + 1)]
    total = sum(raw)
    return [r / total for r in raw]


def dot_high(a, b, dims=((1,), (0,))):
    return lax.dot_general(a, b, (dims, ((), ())), precision=HIGH, preferred_element_type=F32)


def split2(v):
    hi = v.astype(BF16)
    return hi, (v - hi.astype(F32)).astype(BF16)


def split3(v):
    a = v.astype(BF16).astype(F32)
    b = (v - a).astype(BF16).astype(F32)
    return a, b, v - a - b


def put_lanes(columns):
    rows = columns[0].shape[0]
    lane = lax.broadcasted_iota(jnp.int32, (rows, LANES), 1)
    out = jnp.zeros((rows, LANES), F32)
    for k, col in enumerate(columns):
        out = jnp.where(lane == k, col, out)
    return out


def pad_rows(v, rows):
    return jnp.concatenate([v, jnp.zeros((rows - v.shape[0],) + v.shape[1:], v.dtype)], axis=0)


def sum3(block, at):
    return block[:, at : at + 1] + block[:, at + 1 : at + 2] + block[:, at + 2 : at + 3]


class Slab:
    def __init__(self, decay):
        cases, depth = decay.shape
        self.decay = decay
        self.row = lax.broadcasted_iota(jnp.int32, (depth, depth), 0)
        self.col = lax.broadcasted_iota(jnp.int32, (depth, depth), 1)
        logs = jnp.log(decay)
        upto = (self.row <= self.col).astype(BF16)
        parts = jnp.concatenate(split3(pad_rows(logs, 8)), axis=0).astype(BF16)
        sums = lax.dot_general(parts, upto, (((1,), (0,)), ((), ())), preferred_element_type=F32)
        self.up = (sums[0:8] + sums[8:16] + sums[16:24])[0:cases]
        self.up_ex = self.up - logs
        wide = lambda v: jnp.transpose(pad_rows(v, 8))
        self.up_t = wide(self.up)
        self.up_ex_t = wide(self.up_ex)
        self.keep_t = wide(1.0 - decay)
        self.total = self.up[:, depth - 1 : depth]

    def forward_t(self, c):
        gap = self.up[c : c + 1, :] - self.up_t[:, c : c + 1]
        weight = jnp.exp(jnp.minimum(gap, 0.0)) * self.keep_t[:, c : c + 1]
        return jnp.where(self.col >= self.row, weight, 0.0)


def case_scale(weight_ref, index_ref, c):
    return -3.0 * weight_ref[index_ref[c]]


def faces_kernel(shape, cuts, *refs):
    cases, nx, ny, depth = shape
    (index_hbm, weight_hbm, decay_hbm, density_hbm, mask_hbm, energy_hbm,
     send_ref, own_ref, source_ref, density_ref, mask_ref, map_ref, rows_ref,
     index_ref, weight_ref, decay_ref, energy_ref, small_sem, sem) = refs
    small = [
        pltpu.make_async_copy(decay_hbm, decay_ref, small_sem.at[0]),
        pltpu.make_async_copy(index_hbm, index_ref, small_sem.at[1]),
        pltpu.make_async_copy(weight_hbm, weight_ref, small_sem.at[2]),
    ]
    big = []
    for s, at in enumerate(pl.ds(*cut) for cut in cuts):
        big.append([
            pltpu.make_async_copy(density_hbm.at[at], density_ref.at[at], sem.at[0, s]),
            pltpu.make_async_copy(mask_hbm.at[at], mask_ref.at[at], sem.at[1, s]),
            pltpu.make_async_copy(energy_hbm.at[:, at], energy_ref.at[:, at], sem.at[2, s]),
        ])
    for copy in small:
        copy.start()
    for group in big[:AHEAD]:
        for copy in group:
            copy.start()
    for copy in small:
        copy.wait()

    decay = decay_ref[...]
    slab = Slab(decay)
    for group in big[AHEAD : AHEAD + 1]:
        for copy in group:
            copy.start()
    zero_row = jnp.zeros((1, depth), F32)
    e_rows, h_rows, turns = [], [], []
    for c in range(cases):
        scale = case_scale(weight_ref, index_ref, c)
        f_t = slab.forward_t(c) * scale
        map_ref[c] = f_t
        keep = 1.0 - decay[c : c + 1, :]
        e_row = jnp.exp(slab.total[c : c + 1] - slab.up[c : c + 1, :]) * keep * scale
        b_row = jnp.exp(slab.up_ex[c : c + 1, :]) * keep
        b_hi = b_row.astype(BF16).astype(F32)
        b_two = jnp.concatenate([b_hi, b_row - b_hi] + [zero_row] * 6, axis=0).astype(BF16)
        f_hi, f_lo = split2(f_t)
        twice = lax.dot_general(b_two, f_hi, (((1,), (1,)), ((), ())), preferred_element_type=F32)
        once = lax.dot_general(b_two, f_lo, (((1,), (1,)), ((), ())), preferred_element_type=F32)
        h_row = twice[0:1] + twice[1:2] + once[0:1]
        turns.append(jnp.sum(b_row * jnp.exp(slab.up[c : c + 1, :]), axis=1, keepdims=True))
        place = lambda r: jnp.concatenate([zero_row] * c + [r] + [zero_row] * (cases - 1 - c), axis=1)
        e_rows.append(place(e_row))
        h_rows.append(place(h_row))
    w_hi, w_lo = split2(jnp.concatenate(e_rows + h_rows, axis=0))
    wmat = jnp.concatenate([w_hi, w_lo], axis=0)
    rows_ref[...] = jnp.concatenate([pad_rows(v, 8) for v in (slab.up, slab.up_ex, 1.0 - decay)], axis=0)

    sums = [jnp.zeros((8, depth), F32) for _ in range(cases)]

    def faces_of(at, span):
        faces = lax.dot_general(
            wmat, source_ref[span, :], (((1,), (1,)), ((), ())), preferred_element_type=F32)
        faces = faces[0 : 2 * cases] + faces[2 * cases : 4 * cases]
        own_ref[:, span] = faces
        send_ref[:, span] = faces.astype(BF16)

    for s, (first, bx) in enumerate(cuts):
        cols = bx * ny
        for copy in big[s]:
            copy.wait()
        for group in big[s + AHEAD + 1 : s + AHEAD + 2]:
            for copy in group:
                copy.start()
        at = pl.ds(first, bx)
        mask = mask_ref[at]
        dense = jnp.where(mask == 1, 0.001, jnp.where(mask == 2, 1.0, density_ref[at]))
        cube = dense * dense * dense
        span = pl.ds(first * ny, cols)
        for c in range(cases):
            work = cube * energy_ref[c, at].astype(F32)
            sums[c] = sums[c] + jnp.sum(work.reshape(cols // 8, 8, depth), axis=0)
            source_ref[span, c * depth : (c + 1) * depth] = work.astype(BF16).reshape(cols, depth)
        faces_of(at, span)

    total = jnp.concatenate([jnp.sum(jnp.sum(v, axis=0, keepdims=True), axis=1, keepdims=True) for v in sums], axis=0)
    turn = jnp.concatenate(turns, axis=0)
    aux = put_lanes(split3(jnp.exp(slab.total)) + split3(turn) + split3(total))
    aux = pad_rows(aux, 2 * cases)
    tail = pl.ds(nx * ny, LANES)
    own_ref[:, tail] = aux
    send_ref[:, tail] = aux.astype(BF16)


def row_cuts(nx):
    rows = 16 if nx % 16 == 0 else nx
    return [(start, rows) for start in range(0, nx, rows)]


def faces_call(density, design_mask, energy, decay, case_index, case_weight):
    cases, nx, ny, depth = energy.shape
    cuts = row_cuts(nx)
    width = nx * ny + LANES
    return pl.pallas_call(
        functools.partial(faces_kernel, energy.shape, cuts),
        in_specs=[HBM] * 6,
        out_specs=[VMEM] * 7,
        out_shape=[
            pltpu.VMEM((2 * cases, width), BF16),
            pltpu.VMEM((2 * cases, width), F32),
            pltpu.VMEM((nx * ny, cases * depth), BF16),
            pltpu.VMEM(density.shape, F32),
            pltpu.VMEM(density.shape, jnp.int32),
            pltpu.VMEM((cases, depth, depth), F32),
            pltpu.VMEM((24, depth), F32),
        ],
        scratch_shapes=[
            pltpu.SMEM(case_index.shape, case_index.dtype),
            pltpu.SMEM(case_weight.shape, F32),
            pltpu.VMEM(decay.shape, F32),
            pltpu.VMEM(energy.shape, BF16),
            pltpu.SemaphoreType.DMA((3,)),
            pltpu.SemaphoreType.DMA((3, len(cuts))),
        ],
        compiler_params=pltpu.CompilerParams(vmem_limit_bytes=20 * MIB),
        name="faces",
    )(*in_hbm(case_index, case_weight, decay, density, design_mask, energy))


def local_kernel(shape, bx, source_ref, density_ref, mask_ref, map_ref, rows_ref, t_ref, factor_ref, umap_ref, *rest):
    cases, nx, ny, depth = shape
    *sends, rmat = rest
    steps, cols = nx // bx, bx * ny
    row = lax.broadcasted_iota(jnp.int32, (depth, depth), 0)
    col = lax.broadcasted_iota(jnp.int32, (depth, depth), 1)
    up, up_ex = rows_ref[0:8, :], rows_ref[8:16, :]
    up_ex_t, keep_t = jnp.transpose(up_ex), jnp.transpose(rows_ref[16:24, :])
    total = up[:, depth - 1 : depth]
    lead = jnp.exp(up)
    a_rows = []
    for c in range(cases):
        gap = up_ex_t[:, c : c + 1] - up_ex[c : c + 1, :]
        weight = jnp.exp(jnp.minimum(gap, 0.0)) * keep_t[:, c : c + 1]
        b_t = jnp.where(col <= row, weight, 0.0)
        both = dot_high(jnp.concatenate([map_ref[c], lead], axis=0), b_t)
        hi, lo = split2(both[0:depth])
        rmat[c * depth : (c + 1) * depth, 0:depth] = hi
        rmat[c * depth : (c + 1) * depth, depth : 2 * depth] = lo
        a_rows.append(both[depth + c : depth + c + 1])
    u_all = jnp.concatenate(a_rows + [jnp.exp(total - up_ex)[0:cases]], axis=0)
    u_hi = u_all.astype(BF16).astype(F32)
    umap_ref[...] = jnp.concatenate([u_hi, u_hi, u_all - u_hi, jnp.zeros_like(u_hi)], axis=0).astype(BF16)

    for s in range(steps):
        both = lax.dot_general(
            source_ref[s * cols : (s + 1) * cols, :], rmat[...], (((1,), (0,)), ((), ())),
            preferred_element_type=F32)
        at = slice(s * bx, (s + 1) * bx)
        t_ref[at] = (both[:, 0:depth] + both[:, depth : 2 * depth]).reshape(bx, ny, depth)
        factor_ref[at] = jnp.where(mask_ref[at] == 0, 1.0 / jnp.maximum(density_ref[at], 0.1), 0.0)
    low = lax.axis_index("gx") % 2 == 1
    for k, ref in enumerate(sends):
        bottom = low if k == 0 else jnp.logical_not(low)
        start = jnp.where(bottom, 0, nx - RADIUS)
        ref[...] = t_ref[pl.ds(start, RADIUS)].reshape(RADIUS * ny, depth).astype(BF16)


def local_call(source, density, mask, maps, rows, nsends):
    nx, ny, depth = density.shape
    cases = maps.shape[0]
    return pl.pallas_call(
        functools.partial(local_kernel, (cases, nx, ny, depth), 16),
        in_specs=[VMEM] * 5,
        out_specs=[VMEM] * (3 + nsends),
        out_shape=[
            pltpu.VMEM(density.shape, F32),
            pltpu.VMEM(density.shape, F32),
            pltpu.VMEM((8 * cases, depth), BF16),
        ]
        + [pltpu.VMEM((RADIUS * ny, depth), BF16)] * nsends,
        scratch_shapes=[pltpu.VMEM((cases * depth, 2 * depth), BF16)],
        compiler_params=pltpu.CompilerParams(vmem_limit_bytes=16 * MIB),
        name="local",
    )(*in_vmem(source, density, mask, maps, rows))


def head_kernel(shape, nslabs, nsends, swapped, *refs):
    cases, nx, ny, depth = shape
    own_ref = refs[0]
    msgs = refs[1:nslabs]
    lhs_ref = refs[nslabs]
    sends = refs[1 + nslabs : 1 + nslabs + nsends]
    stack = refs[-1]
    cols = nx * ny
    mine = lax.axis_index("gz")
    low = lax.axis_index("gx") % 2 == 1
    stack[0] = own_ref[...].astype(F32)
    for m, msg in zip(swap_order(nslabs) if swapped else range(1, nslabs), msgs):
        stack[m] = msg[...].astype(F32)
    total = jnp.zeros((cases, 1), F32)
    for m in range(nslabs):
        total = total + sum3(stack[m, 0:cases, cols : cols + LANES], 6)
    state = jnp.zeros((cases, cols), F32)
    entering, above = state, state
    tops, gains = [], []
    for j in range(nslabs):
        at = mine ^ j if swapped else j
        aux = stack[at, 0:cases, cols : cols + LANES]
        gains.append(sum3(aux, 0))
        entering = jnp.where(mine == j, state, entering)
        tops.append(stack[at, cases : 2 * cases, 0:cols] + sum3(aux, 3) * state)
        state = gains[j] * state + stack[at, 0:cases, 0:cols]
    state = jnp.zeros((cases, cols), F32)
    for j in reversed(range(nslabs)):
        above = jnp.where(mine == j, state, above)
        state = tops[j] + gains[j] * state
    faces = jnp.concatenate([entering, above], axis=0)
    hi = faces.astype(BF16).astype(F32)
    lhs_ref[...] = jnp.concatenate([hi, faces - hi, hi, jnp.zeros_like(hi)], axis=0).astype(BF16)
    aux = pad_rows(put_lanes(split3(total)), 16).astype(BF16)
    rows = RADIUS + 1
    wide = rows * ny
    for k, ref in enumerate(sends):
        bottom = low if k == 0 else jnp.logical_not(low)
        start = jnp.where(bottom, 0, nx - rows) * ny
        ref[0:16, :] = lhs_ref[0:16, pl.ds(pl.multiple_of(start, wide), wide)]
        ref[16:32, 0:LANES] = aux
        ref[16:32, LANES:] = jnp.zeros((16, wide - LANES), BF16)


def head_call(own, msgs, shape, nsends, swapped):
    nx, ny, depth = shape
    cases = own.shape[0] // 2
    nslabs = len(msgs) + 1
    return pl.pallas_call(
        functools.partial(head_kernel, (cases, nx, ny, depth), nslabs, nsends, swapped),
        in_specs=[VMEM] * nslabs,
        out_specs=[VMEM] * (1 + nsends),
        out_shape=[pltpu.VMEM((8 * cases, nx * ny), BF16)]
        + [pltpu.VMEM((32, (RADIUS + 1) * ny), BF16)] * nsends,
        scratch_shapes=[pltpu.VMEM((nslabs,) + own.shape, F32)],
        compiler_params=pltpu.CompilerParams(vmem_limit_bytes=20 * MIB),
        name="head",
    )(own, *msgs)


def sided(even, got):
    a = got[0]
    b = got[1] if len(got) > 1 else jnp.zeros_like(a)
    return jnp.where(even, b, a), jnp.where(even, a, b)


def edge_kernel(shape, nx_sends, ny_sends, *refs):
    cases, nx, ny, depth = shape
    t_ref, umap_ref = refs[0:2]
    part_refs = refs[2 : 2 + nx_sends]
    got_refs = refs[2 + nx_sends : 2 + 2 * nx_sends]
    own_send = refs[2 + 2 * nx_sends]
    sends = refs[3 + 2 * nx_sends : 3 + 2 * nx_sends + ny_sends]
    xb_ref, xa_ref, sums_ref, line = refs[3 + 2 * nx_sends + ny_sends :]
    taps = taps_1d()
    edge = RADIUS * ny
    even_x = lax.axis_index("gx") % 2 == 0
    flip_y = lax.axis_index("gy") % 2 == 1
    blocks = []
    for k, (part, got) in enumerate(zip(part_refs, got_refs)):
        lhs = got[0:16, :]
        lhs = jnp.concatenate([lhs, pad_rows(lhs[0:8], 16)], axis=0)
        add = lax.dot_general(lhs, umap_ref[...], (((0,), (0,)), ((), ())), preferred_element_type=F32)
        first_rows = even_x if k == 0 else jnp.logical_not(even_x)
        blocks.append(part[...].astype(F32) + jnp.where(first_rows, add[0:edge], add[ny:]))
    before, after = sided(even_x, blocks)
    xb_ref[...] = before
    xa_ref[...] = after
    total = sum3(own_send[16:32, 0:LANES].astype(F32), 0)
    for ref in got_refs:
        total = total + sum3(ref[16:32, 0:LANES].astype(F32), 0)
    sums_ref[...] = jnp.broadcast_to(total[0:8], (8, LANES))
    aux = put_lanes(split3(total)).astype(BF16)
    flat = t_ref.reshape(nx * ny, depth)
    columns = []
    for k in range(2 * RADIUS):
        y = k if k < RADIUS else ny - 2 * RADIUS + k
        line[8 : 8 + nx, :] = flat[pl.ds(y, nx, stride=ny), :]
        line[8 - RADIUS : 8, :] = xb_ref[pl.ds(y, RADIUS, stride=ny), :]
        line[8 + nx : 8 + nx + RADIUS, :] = xa_ref[pl.ds(y, RADIUS, stride=ny), :]
        acc = taps[RADIUS] * line[8 : 8 + nx, :]
        for d in range(1, RADIUS + 1):
            acc = acc + taps[RADIUS + d] * (line[8 - d : 8 - d + nx, :] + line[8 + d : 8 + d + nx, :])
        columns.append(acc)
    for m, ref in enumerate(sends):
        for k in range(RADIUS):
            first, last = columns[k], columns[RADIUS + k]
            pick = jnp.where(flip_y == (m == 0), first, last)
            ref[k * nx : (k + 1) * nx, :] = pick.astype(BF16)
        ref[RADIUS * nx :, :] = aux


def edge_call(t, umap, parts, got, own_send, ny_sends, cases):
    nx, ny, depth = t.shape
    return pl.pallas_call(
        functools.partial(edge_kernel, (cases, nx, ny, depth), len(got), ny_sends),
        in_specs=[VMEM] * (3 + 2 * len(got)),
        out_specs=[VMEM] * (ny_sends + 3),
        out_shape=[jax.ShapeDtypeStruct((RADIUS * nx + 16, depth), BF16)] * ny_sends
        + [jax.ShapeDtypeStruct((RADIUS * ny, depth), F32)] * 2
        + [jax.ShapeDtypeStruct((8, LANES), F32)],
        scratch_shapes=[pltpu.VMEM((nx + 16, depth), F32)],
        compiler_params=pltpu.CompilerParams(vmem_limit_bytes=16 * MIB),
        name="edge",
    )(t, umap, *parts, *got, own_send)


def filter_row(ny, read, line, factor):
    taps = taps_1d()
    acc = taps[RADIUS] * read(0)
    for d in range(1, RADIUS + 1):
        acc = acc + taps[RADIUS + d] * (read(-d) + read(d))
    line[8 : 8 + ny, :] = acc
    res = taps[RADIUS] * acc
    for d in range(1, RADIUS + 1):
        res = res + taps[RADIUS + d] * (line[8 - d : 8 - d + ny, :] + line[8 + d : 8 + d + ny, :])
    return res * factor


def clear_line(line, ny):
    zeros = jnp.zeros((8, line.shape[-1]), F32)
    for k in range(line.shape[0]):
        line[k, 0:8, :] = zeros
        line[k, 8 + ny :, :] = zeros


def filter_rows(lo, hi, chunk, read, line, factor_ref, first_ref, last_ref, out_ref, out_hbm, sem):
    ny = factor_ref.shape[1]
    copies = []

    def row(x, carry):
        res = filter_row(ny, lambda d: read(x + d), line.at[x % 2], factor_ref[x])
        out_ref[x] = res
        first_ref[x] = res[0:8]
        last_ref[x] = res[ny - 8 : ny]
        return carry

    for s, start in enumerate(range(lo, hi, chunk)):
        stop = min(start + chunk, hi)
        lax.fori_loop(start, stop, row, 0)
        span = pl.ds(start, stop - start)
        copies.append(pltpu.make_async_copy(out_ref.at[span], out_hbm.at[span], sem.at[s]))
        copies[s].start()
    return copies


def split_row(nx):
    return nx * 11 // 32


def body_kernel(shape, chunk, lhs_ref, umap_ref, part_ref, factor_ref, t_ref, out_hbm, first_ref, last_ref, line, out_ref, sem):
    nx, ny, depth = shape
    add = lax.dot_general(lhs_ref[...], umap_ref[...], (((0,), (0,)), ((), ())), preferred_element_type=F32)
    t_ref[...] = part_ref[...] + add.reshape(nx, ny, depth)
    clear_line(line, ny)
    copies = filter_rows(
        RADIUS, split_row(nx), chunk, lambda x: t_ref[x], line, factor_ref, first_ref, last_ref, out_ref, out_hbm, sem)
    for copy in copies:
        copy.wait()


def body_call(lhs, umap, part, factor):
    nx, ny, depth = part.shape
    chunk = 10
    return pl.pallas_call(
        functools.partial(body_kernel, part.shape, chunk),
        in_specs=[VMEM] * 4,
        out_specs=[VMEM, HBM, VMEM, VMEM],
        out_shape=[
            pltpu.VMEM(part.shape, F32),
            jax.ShapeDtypeStruct(part.shape, F32),
            pltpu.VMEM((nx, 8, depth), F32),
            pltpu.VMEM((nx, 8, depth), F32),
        ],
        scratch_shapes=[
            pltpu.VMEM((2, ny + 16, depth), F32),
            pltpu.VMEM(part.shape, F32),
            pltpu.SemaphoreType.DMA((-(-nx // chunk),)),
        ],
        compiler_params=pltpu.CompilerParams(vmem_limit_bytes=20 * MIB),
        name="body",
    )(*in_vmem(lhs, umap, part, factor))


def rest_kernel(shape, chunk, t_ref, xb_ref, xa_ref, factor_ref, _, __, ___, out_hbm, first_ref, last_ref,
                line, pad, out_ref, sem, side_sem):
    nx, ny, depth = shape
    clear_line(line, ny)
    pad[0:RADIUS] = xb_ref[...].reshape(RADIUS, ny, depth)
    pad[RADIUS : 3 * RADIUS] = t_ref[0 : 2 * RADIUS]
    pad[3 * RADIUS : 5 * RADIUS] = t_ref[nx - 2 * RADIUS : nx]
    pad[5 * RADIUS :] = xa_ref[...].reshape(RADIUS, ny, depth)
    copies = []
    for side, start in ((0, 0), (1, nx - RADIUS)):
        for k in range(RADIUS):
            x = start + k
            mid = (RADIUS if side == 0 else 4 * RADIUS) + k
            res = filter_row(ny, lambda d: pad[mid + d], line.at[x % 2], factor_ref[x])
            out_ref[x] = res
            first_ref[x] = res[0:8]
            last_ref[x] = res[ny - 8 : ny]
        span = pl.ds(start, RADIUS)
        copies.append(pltpu.make_async_copy(out_ref.at[span], out_hbm.at[span], side_sem.at[side]))
        copies[side].start()
    copies += filter_rows(
        split_row(nx), nx - RADIUS, chunk, lambda x: t_ref[x], line, factor_ref, first_ref, last_ref, out_ref, out_hbm, sem)
    for copy in copies:
        copy.wait()


def rest_call(t, xb, xa, factor, out, first, last):
    nx, ny, depth = t.shape
    chunk = 13
    return pl.pallas_call(
        functools.partial(rest_kernel, t.shape, chunk),
        in_specs=[VMEM] * 4 + [HBM, VMEM, VMEM],
        out_specs=[HBM, VMEM, VMEM],
        out_shape=[
            jax.ShapeDtypeStruct(out.shape, F32),
            pltpu.VMEM(first.shape, F32),
            pltpu.VMEM(last.shape, F32),
        ],
        input_output_aliases={4: 0, 5: 1, 6: 2},
        scratch_shapes=[
            pltpu.VMEM((2, ny + 16, depth), F32),
            pltpu.VMEM((6 * RADIUS, ny, depth), F32),
            pltpu.VMEM(t.shape, F32),
            pltpu.SemaphoreType.DMA((-(-nx // chunk),)),
            pltpu.SemaphoreType.DMA((2,)),
        ],
        compiler_params=pltpu.CompilerParams(vmem_limit_bytes=20 * MIB),
        name="rest",
    )(*in_vmem(t, xb, xa, factor), *in_hbm(out), *in_vmem(first, last))


def finish_kernel(shape, ngot, *refs):
    nx, ny, depth = shape
    got_refs = refs[:ngot]
    first_ref, last_ref, factor_ref, _, out_hbm, done_ref, strip, sem = refs[ngot:]
    taps = taps_1d()
    edge = RADIUS * nx
    place, count = lax.axis_index("gy"), lax.axis_size("gy")
    blocks = [r[0:edge, :].astype(F32) for r in got_refs]
    before, after = sided(place % 2 == 0, blocks) if blocks else (jnp.zeros((edge, depth), F32),) * 2
    before = jnp.where(place == 0, 0.0, before)
    after = jnp.where(place == count - 1, 0.0, after)
    flat = factor_ref.reshape(nx * ny, depth)
    copies = []
    for ref, side in ((first_ref, 0), (last_ref, 1)):
        strip[side] = ref[...]
        view = strip.at[side].reshape(nx * 8, depth)
        for y in range(RADIUS):
            add = jnp.zeros((nx, depth), F32)
            for k in range(RADIUS):
                if side == 0:
                    d, halo, own = y + RADIUS - k, before[k * nx : (k + 1) * nx], y
                else:
                    d, halo, own = k + RADIUS - y, after[k * nx : (k + 1) * nx], ny - RADIUS + y
                if d <= RADIUS:
                    add = add + taps[RADIUS + d] * halo
            at = own if side == 0 else own - (ny - 8)
            view[pl.ds(at, nx, stride=8), :] += flat[pl.ds(own, nx, stride=ny), :] * add
        target = out_hbm.at[:, 0:8, :] if side == 0 else out_hbm.at[:, ny - 8 : ny, :]
        copies.append(pltpu.make_async_copy(strip.at[side], target, sem.at[side]))
        copies[side].start()
    done_ref[...] = jnp.zeros_like(done_ref)
    for copy in copies:
        copy.wait()


def finish_call(got, first, last, factor, out):
    nx, ny, depth = out.shape
    nin = len(got)
    return pl.pallas_call(
        functools.partial(finish_kernel, out.shape, len(got)),
        in_specs=[VMEM] * (nin + 3) + [HBM],
        out_specs=[HBM, VMEM],
        out_shape=[jax.ShapeDtypeStruct(out.shape, F32), pltpu.VMEM((8, LANES), F32)],
        input_output_aliases={nin + 3: 0},
        scratch_shapes=[pltpu.VMEM((2, nx, 8, depth), F32), pltpu.SemaphoreType.DMA((2,))],
        compiler_params=pltpu.CompilerParams(vmem_limit_bytes=16 * MIB),
        name="finish",
    )(*got, *in_vmem(first, last, factor), *in_hbm(out))


def mean_kernel(cells, cases, *refs):
    total = refs[0][...]
    for ref in refs[2:-1]:
        block = ref[...] if ref.shape[0] == 8 else sum3(ref[ref.shape[0] - 16 :, :].astype(F32), 0)[0:8]
        total = total + block
    for c in range(cases):
        refs[-1][c] = total[c, 0] / cells


def mean_call(sums, behind, got, cells, cases):
    return pl.pallas_call(
        functools.partial(mean_kernel, cells, cases),
        in_specs=[VMEM] * (2 + len(got)),
        out_specs=SMEM,
        out_shape=jax.ShapeDtypeStruct((cases,), F32),
        compiler_params=pltpu.CompilerParams(vmem_limit_bytes=4 * MIB),
        name="mean",
    )(sums, behind, *got)


def swap_pairs(count, first):
    return [q for i in range(first, count - 1, 2) for q in ((i, i + 1), (i + 1, i))]


def swaps_of(count):
    return min(count - 1, 2)


def swap_order(count):
    return {1: (), 2: (1,), 4: (2, 3, 1)}[count]


def xor_pairs(count, m):
    return [(i, i ^ m) for i in range(count)]


def shards(density, design_mask, energy, decay, case_index, case_weight):
    cases = energy.shape[0]
    nx, ny, depth = density.shape
    nz, gx, gy = (lax.axis_size(a) for a in ("gz", "gx", "gy"))
    send, own, source, density_v, mask_v, maps, rows = faces_call(
        density, design_mask, energy, decay, case_index, case_weight)
    swapped = nz in (1, 2, 4)
    if swapped:
        msgs = [lax.ppermute(send, "gz", xor_pairs(nz, m)) for m in swap_order(nz)]
    else:
        every = lax.all_gather(send, "gz")
        own, *msgs = [every[j] for j in range(nz)]
    part, factor, umap, *x_parts = local_call(source, density_v, mask_v, maps, rows, swaps_of(gx))
    x_parts = [lax.ppermute(v, "gx", swap_pairs(gx, k)) for k, v in enumerate(x_parts)]
    lhs, *x_sends = head_call(own, msgs, part.shape, max(swaps_of(gx), 1), swapped)
    x_got = [lax.ppermute(x_sends[k], "gx", swap_pairs(gx, k)) for k in range(swaps_of(gx))]
    t, out, first, last = body_call(lhs, umap, part, factor)
    *y_sends, xb, xa, sums = edge_call(t, umap, x_parts, x_got, x_sends[0], swaps_of(gy), cases)
    ring = gy == 4
    ends = [(0, gy - 1), (gy - 1, 0)] if ring else []
    y_got = [lax.ppermute(y_sends[k], "gy", swap_pairs(gy, k) + (ends if k else [])) for k in range(swaps_of(gy))]
    out, first, last = rest_call(t, xb, xa, factor, out, first, last)
    if ring:
        y_got[1], first = lax.optimization_barrier((y_got[1], first))
        more = y_got + [lax.ppermute(y_got[1], "gy", swap_pairs(gy, 0))]
    else:
        more = [lax.ppermute(sums, "gy", xor_pairs(gy, m)) for m in range(1, gy)]
    out, behind = finish_call(y_got, first, last, factor, out)
    cells = nx * ny * depth * nz * gx * gy
    return out, mean_call(sums, behind, more, float(cells), cases)


def solution(mesh):
    placed = (
        P("gx", "gy", "gz"),
        P("gx", "gy", "gz"),
        P(None, "gx", "gy", "gz"),
        P(None, "gz"),
        P(),
        P(),
    )
    return jax.shard_map(
        shards, mesh=mesh, in_specs=placed, out_specs=(P("gx", "gy", "gz"), P()), check_vma=False
    )
```

```python
import functools
import math
import jax
import jax.numpy as jnp
from jax import lax
from jax.experimental import pallas as pl
from jax.experimental.pallas import tpu as pltpu
from jax.sharding import PartitionSpec as P

RADIUS = 3
AHEAD = 2
LANES = 128
MIB = 2**20
F32 = jnp.float32
BF16 = jnp.bfloat16
HIGH = lax.Precision.HIGHEST
HBM = pl.BlockSpec(memory_space=pltpu.HBM)
VMEM = pl.BlockSpec(memory_space=pltpu.VMEM)
SMEM = pl.BlockSpec(memory_space=pltpu.SMEM)


def in_hbm(*arrays):
    return [pltpu.with_memory_space_constraint(a, pltpu.HBM) for a in arrays]


def in_vmem(*arrays):
    return [pltpu.with_memory_space_constraint(a, pltpu.VMEM) for a in arrays]


def taps_1d():
    raw = [math.exp(-2.0 * k * k / (RADIUS * RADIUS)) for k in range(-RADIUS, RADIUS + 1)]
    total = sum(raw)
    return [r / total for r in raw]


def dot_high(a, b, dims=((1,), (0,))):
    return lax.dot_general(a, b, (dims, ((), ())), precision=HIGH, preferred_element_type=F32)


def split2(v):
    hi = v.astype(BF16)
    return hi, (v - hi.astype(F32)).astype(BF16)


def split3(v):
    a = v.astype(BF16).astype(F32)
    b = (v - a).astype(BF16).astype(F32)
    return a, b, v - a - b


def put_lanes(columns):
    rows = columns[0].shape[0]
    lane = lax.broadcasted_iota(jnp.int32, (rows, LANES), 1)
    out = jnp.zeros((rows, LANES), F32)
    for k, col in enumerate(columns):
        out = jnp.where(lane == k, col, out)
    return out


def pad_rows(v, rows):
    return jnp.concatenate([v, jnp.zeros((rows - v.shape[0],) + v.shape[1:], v.dtype)], axis=0)


def sum3(block, at):
    return block[:, at : at + 1] + block[:, at + 1 : at + 2] + block[:, at + 2 : at + 3]


class Slab:
    def __init__(self, decay):
        cases, depth = decay.shape
        self.row = lax.broadcasted_iota(jnp.int32, (depth, depth), 0)
        self.col = lax.broadcasted_iota(jnp.int32, (depth, depth), 1)
        logs = jnp.log(decay)
        upto = (self.row <= self.col).astype(BF16)
        parts = jnp.concatenate(split3(pad_rows(logs, 8)), axis=0).astype(BF16)
        sums = lax.dot_general(parts, upto, (((1,), (0,)), ((), ())), preferred_element_type=F32)
        self.up = (sums[0:8] + sums[8:16] + sums[16:24])[0:cases]
        self.up_ex = self.up - logs
        wide = lambda v: jnp.transpose(pad_rows(v, 8))
        self.up_t = wide(self.up)
        self.up_ex_t = wide(self.up_ex)
        self.keep_t = wide(1.0 - decay)
        self.total = self.up[:, depth - 1 : depth]

    def forward_t(self, c):
        gap = self.up[c : c + 1, :] - self.up_t[:, c : c + 1]
        weight = jnp.exp(jnp.minimum(gap, 0.0)) * self.keep_t[:, c : c + 1]
        return jnp.where(self.col >= self.row, weight, 0.0)


def case_scale(weight_ref, index_ref, c):
    return -3.0 * weight_ref[index_ref[c]]


def faces_kernel(shape, cuts, *refs):
    cases, nx, ny, depth = shape
    (index_hbm, weight_hbm, decay_hbm, density_hbm, mask_hbm, energy_hbm,
     send_ref, own_ref, source_ref, density_ref, mask_ref, map_ref, rows_ref,
     index_ref, weight_ref, decay_ref, energy_ref, small_sem, sem) = refs
    small = [
        pltpu.make_async_copy(decay_hbm, decay_ref, small_sem.at[0]),
        pltpu.make_async_copy(index_hbm, index_ref, small_sem.at[1]),
        pltpu.make_async_copy(weight_hbm, weight_ref, small_sem.at[2]),
    ]
    big = []
    for s, at in enumerate(pl.ds(*cut) for cut in cuts):
        big.append([
            pltpu.make_async_copy(density_hbm.at[at], density_ref.at[at], sem.at[0, s]),
            pltpu.make_async_copy(mask_hbm.at[at], mask_ref.at[at], sem.at[1, s]),
            pltpu.make_async_copy(energy_hbm.at[:, at], energy_ref.at[:, at], sem.at[2, s]),
        ])
    for copy in small:
        copy.start()
    for group in big[:AHEAD]:
        for copy in group:
            copy.start()
    for copy in small:
        copy.wait()

    decay = decay_ref[...]
    slab = Slab(decay)
    for group in big[AHEAD : AHEAD + 1]:
        for copy in group:
            copy.start()
    zero_row = jnp.zeros((1, depth), F32)
    e_rows, h_rows, turns = [], [], []
    for c in range(cases):
        scale = case_scale(weight_ref, index_ref, c)
        f_t = slab.forward_t(c) * scale
        map_ref[c] = f_t
        keep = 1.0 - decay[c : c + 1, :]
        e_row = jnp.exp(slab.total[c : c + 1] - slab.up[c : c + 1, :]) * keep * scale
        b_row = jnp.exp(slab.up_ex[c : c + 1, :]) * keep
        b_hi = b_row.astype(BF16).astype(F32)
        b_two = jnp.concatenate([b_hi, b_row - b_hi] + [zero_row] * 6, axis=0).astype(BF16)
        f_hi, f_lo = split2(f_t)
        twice = lax.dot_general(b_two, f_hi, (((1,), (1,)), ((), ())), preferred_element_type=F32)
        once = lax.dot_general(b_two, f_lo, (((1,), (1,)), ((), ())), preferred_element_type=F32)
        h_row = twice[0:1] + twice[1:2] + once[0:1]
        turns.append(jnp.sum(b_row * jnp.exp(slab.up[c : c + 1, :]), axis=1, keepdims=True))
        place = lambda r: jnp.concatenate([zero_row] * c + [r] + [zero_row] * (cases - 1 - c), axis=1)
        e_rows.append(place(e_row))
        h_rows.append(place(h_row))
    w_hi, w_lo = split2(jnp.concatenate(e_rows + h_rows, axis=0))
    wmat = jnp.concatenate([w_hi, w_lo], axis=0)
    rows_ref[...] = jnp.concatenate([pad_rows(v, 8) for v in (slab.up, slab.up_ex, 1.0 - decay)], axis=0)

    sums = [jnp.zeros((8, depth), F32) for _ in range(cases)]

    def faces_of(span):
        faces = lax.dot_general(
            wmat, source_ref[span, :], (((1,), (1,)), ((), ())), preferred_element_type=F32)
        faces = faces[0 : 2 * cases] + faces[2 * cases : 4 * cases]
        own_ref[:, span] = faces
        send_ref[:, span] = faces.astype(BF16)

    for s, (first, bx) in enumerate(cuts):
        cols = bx * ny
        for copy in big[s]:
            copy.wait()
        for group in big[s + AHEAD + 1 : s + AHEAD + 2]:
            for copy in group:
                copy.start()
        at = pl.ds(first, bx)
        mask = mask_ref[at]
        dense = jnp.where(mask == 1, 0.001, jnp.where(mask == 2, 1.0, density_ref[at]))
        cube = dense * dense * dense
        span = pl.ds(first * ny, cols)
        for c in range(cases):
            work = cube * energy_ref[c, at].astype(F32)
            sums[c] = sums[c] + jnp.sum(work.reshape(cols // 8, 8, depth), axis=0)
            source_ref[span, c * depth : (c + 1) * depth] = work.astype(BF16).reshape(cols, depth)
        faces_of(span)

    total = jnp.concatenate([jnp.sum(jnp.sum(v, axis=0, keepdims=True), axis=1, keepdims=True) for v in sums], axis=0)
    turn = jnp.concatenate(turns, axis=0)
    aux = put_lanes(split3(jnp.exp(slab.total)) + split3(turn) + split3(total))
    aux = pad_rows(aux, 2 * cases)
    tail = pl.ds(nx * ny, LANES)
    own_ref[:, tail] = aux
    send_ref[:, tail] = aux.astype(BF16)


def row_cuts(nx):
    rows = 16 if nx % 16 == 0 else nx
    return [(start, rows) for start in range(0, nx, rows)]


def faces_call(density, design_mask, energy, decay, case_index, case_weight):
    cases, nx, ny, depth = energy.shape
    cuts = row_cuts(nx)
    width = nx * ny + LANES
    return pl.pallas_call(
        functools.partial(faces_kernel, energy.shape, cuts),
        in_specs=[HBM] * 6,
        out_specs=[VMEM] * 7,
        out_shape=[
            pltpu.VMEM((2 * cases, width), BF16),
            pltpu.VMEM((2 * cases, width), F32),
            pltpu.VMEM((nx * ny, cases * depth), BF16),
            pltpu.VMEM(density.shape, F32),
            pltpu.VMEM(density.shape, jnp.int32),
            pltpu.VMEM((cases, depth, depth), F32),
            pltpu.VMEM((24, depth), F32),
        ],
        scratch_shapes=[
            pltpu.SMEM(case_index.shape, case_index.dtype),
            pltpu.SMEM(case_weight.shape, F32),
            pltpu.VMEM(decay.shape, F32),
            pltpu.VMEM(energy.shape, BF16),
            pltpu.SemaphoreType.DMA((3,)),
            pltpu.SemaphoreType.DMA((3, len(cuts))),
        ],
        compiler_params=pltpu.CompilerParams(vmem_limit_bytes=20 * MIB),
        name="faces",
    )(*in_hbm(case_index, case_weight, decay, density, design_mask, energy))


def local_kernel(shape, bx, source_ref, density_ref, mask_ref, map_ref, rows_ref, t_ref, factor_ref, umap_ref, *rest):
    cases, nx, ny, depth = shape
    *sends, rmat = rest
    steps, cols = nx // bx, bx * ny
    row = lax.broadcasted_iota(jnp.int32, (depth, depth), 0)
    col = lax.broadcasted_iota(jnp.int32, (depth, depth), 1)
    up, up_ex = rows_ref[0:8, :], rows_ref[8:16, :]
    up_ex_t, keep_t = jnp.transpose(up_ex), jnp.transpose(rows_ref[16:24, :])
    total = up[:, depth - 1 : depth]
    lead = jnp.exp(up)
    a_rows = []
    for c in range(cases):
        gap = up_ex_t[:, c : c + 1] - up_ex[c : c + 1, :]
        weight = jnp.exp(jnp.minimum(gap, 0.0)) * keep_t[:, c : c + 1]
        b_t = jnp.where(col <= row, weight, 0.0)
        both = dot_high(jnp.concatenate([map_ref[c], lead], axis=0), b_t)
        hi, lo = split2(both[0:depth])
        rmat[c * depth : (c + 1) * depth, 0:depth] = hi
        rmat[c * depth : (c + 1) * depth, depth : 2 * depth] = lo
        a_rows.append(both[depth + c : depth + c + 1])
    u_all = jnp.concatenate(a_rows + [jnp.exp(total - up_ex)[0:cases]], axis=0)
    u_hi = u_all.astype(BF16).astype(F32)
    umap_ref[...] = jnp.concatenate([u_hi, u_hi, u_all - u_hi, jnp.zeros_like(u_hi)], axis=0).astype(BF16)

    for s in range(steps):
        both = lax.dot_general(
            source_ref[s * cols : (s + 1) * cols, :], rmat[...], (((1,), (0,)), ((), ())),
            preferred_element_type=F32)
        at = slice(s * bx, (s + 1) * bx)
        t_ref[at] = (both[:, 0:depth] + both[:, depth : 2 * depth]).reshape(bx, ny, depth)
        factor_ref[at] = jnp.where(mask_ref[at] == 0, 1.0 / jnp.maximum(density_ref[at], 0.1), 0.0)
    low = lax.axis_index("gx") % 2 == 1
    for k, ref in enumerate(sends):
        bottom = low if k == 0 else jnp.logical_not(low)
        start = jnp.where(bottom, 0, nx - RADIUS)
        ref[...] = t_ref[pl.ds(start, RADIUS)].reshape(RADIUS * ny, depth).astype(BF16)


def local_call(source, density, mask, maps, rows, nsends):
    nx, ny, depth = density.shape
    cases = maps.shape[0]
    return pl.pallas_call(
        functools.partial(local_kernel, (cases, nx, ny, depth), 16),
        in_specs=[VMEM] * 5,
        out_specs=[VMEM] * (3 + nsends),
        out_shape=[
            pltpu.VMEM(density.shape, F32),
            pltpu.VMEM(density.shape, F32),
            pltpu.VMEM((8 * cases, depth), BF16),
        ]
        + [pltpu.VMEM((RADIUS * ny, depth), BF16)] * nsends,
        scratch_shapes=[pltpu.VMEM((cases * depth, 2 * depth), BF16)],
        compiler_params=pltpu.CompilerParams(vmem_limit_bytes=16 * MIB),
        name="local",
    )(*in_vmem(source, density, mask, maps, rows))


def head_kernel(shape, nslabs, nsends, swapped, *refs):
    cases, nx, ny, _ = shape
    own_ref = refs[0]
    msgs = refs[1:nslabs]
    lhs_ref = refs[nslabs]
    sends = refs[1 + nslabs : 1 + nslabs + nsends]
    stack = refs[-1]
    cols = nx * ny
    mine = lax.axis_index("gz")
    low = lax.axis_index("gx") % 2 == 1
    stack[0] = own_ref[...].astype(F32)
    for m, msg in zip(swap_order(nslabs) if swapped else range(1, nslabs), msgs):
        stack[m] = msg[...].astype(F32)
    total = jnp.zeros((cases, 1), F32)
    for m in range(nslabs):
        total = total + sum3(stack[m, 0:cases, cols : cols + LANES], 6)
    state = jnp.zeros((cases, cols), F32)
    entering, above = state, state
    tops, gains = [], []
    for j in range(nslabs):
        at = mine ^ j if swapped else j
        aux = stack[at, 0:cases, cols : cols + LANES]
        gains.append(sum3(aux, 0))
        entering = jnp.where(mine == j, state, entering)
        tops.append(stack[at, cases : 2 * cases, 0:cols] + sum3(aux, 3) * state)
        state = gains[j] * state + stack[at, 0:cases, 0:cols]
    state = jnp.zeros((cases, cols), F32)
    for j in reversed(range(nslabs)):
        above = jnp.where(mine == j, state, above)
        state = tops[j] + gains[j] * state
    faces = jnp.concatenate([entering, above], axis=0)
    hi = faces.astype(BF16).astype(F32)
    lhs_ref[...] = jnp.concatenate([hi, faces - hi, hi, jnp.zeros_like(hi)], axis=0).astype(BF16)
    aux = pad_rows(put_lanes(split3(total)), 16).astype(BF16)
    rows = RADIUS + 1
    wide = rows * ny
    for k, ref in enumerate(sends):
        bottom = low if k == 0 else jnp.logical_not(low)
        start = jnp.where(bottom, 0, nx - rows) * ny
        ref[0:16, :] = lhs_ref[0:16, pl.ds(pl.multiple_of(start, wide), wide)]
        ref[16:32, 0:LANES] = aux
        ref[16:32, LANES:] = jnp.zeros((16, wide - LANES), BF16)


def head_call(own, msgs, shape, nsends, swapped):
    nx, ny, depth = shape
    cases = own.shape[0] // 2
    nslabs = len(msgs) + 1
    return pl.pallas_call(
        functools.partial(head_kernel, (cases, nx, ny, depth), nslabs, nsends, swapped),
        in_specs=[VMEM] * nslabs,
        out_specs=[VMEM] * (1 + nsends),
        out_shape=[pltpu.VMEM((8 * cases, nx * ny), BF16)]
        + [pltpu.VMEM((32, (RADIUS + 1) * ny), BF16)] * nsends,
        scratch_shapes=[pltpu.VMEM((nslabs,) + own.shape, F32)],
        compiler_params=pltpu.CompilerParams(vmem_limit_bytes=20 * MIB),
        name="head",
    )(own, *msgs)


def sided(even, got):
    a = got[0]
    b = got[1] if len(got) > 1 else jnp.zeros_like(a)
    return jnp.where(even, b, a), jnp.where(even, a, b)


def edge_kernel(shape, nx_sends, ny_sends, *refs):
    _, nx, ny, depth = shape
    t_ref, umap_ref = refs[0:2]
    part_refs = refs[2 : 2 + nx_sends]
    got_refs = refs[2 + nx_sends : 2 + 2 * nx_sends]
    own_send = refs[2 + 2 * nx_sends]
    sends = refs[3 + 2 * nx_sends : 3 + 2 * nx_sends + ny_sends]
    xb_ref, xa_ref, sums_ref, line = refs[3 + 2 * nx_sends + ny_sends :]
    taps = taps_1d()
    edge = RADIUS * ny
    even_x = lax.axis_index("gx") % 2 == 0
    flip_y = lax.axis_index("gy") % 2 == 1
    blocks = []
    for k, (part, got) in enumerate(zip(part_refs, got_refs)):
        lhs = got[0:16, :]
        lhs = jnp.concatenate([lhs, pad_rows(lhs[0:8], 16)], axis=0)
        add = lax.dot_general(lhs, umap_ref[...], (((0,), (0,)), ((), ())), preferred_element_type=F32)
        first_rows = even_x if k == 0 else jnp.logical_not(even_x)
        blocks.append(part[...].astype(F32) + jnp.where(first_rows, add[0:edge], add[ny:]))
    before, after = sided(even_x, blocks)
    xb_ref[...] = before
    xa_ref[...] = after
    total = sum3(own_send[16:32, 0:LANES].astype(F32), 0)
    for ref in got_refs:
        total = total + sum3(ref[16:32, 0:LANES].astype(F32), 0)
    sums_ref[...] = jnp.broadcast_to(total[0:8], (8, LANES))
    aux = put_lanes(split3(total)).astype(BF16)
    flat = t_ref.reshape(nx * ny, depth)
    columns = []
    for k in range(2 * RADIUS):
        y = k if k < RADIUS else ny - 2 * RADIUS + k
        line[8 : 8 + nx, :] = flat[pl.ds(y, nx, stride=ny), :]
        line[8 - RADIUS : 8, :] = xb_ref[pl.ds(y, RADIUS, stride=ny), :]
        line[8 + nx : 8 + nx + RADIUS, :] = xa_ref[pl.ds(y, RADIUS, stride=ny), :]
        acc = taps[RADIUS] * line[8 : 8 + nx, :]
        for d in range(1, RADIUS + 1):
            acc = acc + taps[RADIUS + d] * (line[8 - d : 8 - d + nx, :] + line[8 + d : 8 + d + nx, :])
        columns.append(acc)
    for m, ref in enumerate(sends):
        for k in range(RADIUS):
            first, last = columns[k], columns[RADIUS + k]
            pick = jnp.where(flip_y == (m == 0), first, last)
            ref[k * nx : (k + 1) * nx, :] = pick.astype(BF16)
        ref[RADIUS * nx :, :] = aux


def edge_call(t, umap, parts, got, own_send, ny_sends, cases):
    nx, ny, depth = t.shape
    return pl.pallas_call(
        functools.partial(edge_kernel, (cases, nx, ny, depth), len(got), ny_sends),
        in_specs=[VMEM] * (3 + 2 * len(got)),
        out_specs=[VMEM] * (ny_sends + 3),
        out_shape=[jax.ShapeDtypeStruct((RADIUS * nx + 16, depth), BF16)] * ny_sends
        + [jax.ShapeDtypeStruct((RADIUS * ny, depth), F32)] * 2
        + [jax.ShapeDtypeStruct((8, LANES), F32)],
        scratch_shapes=[pltpu.VMEM((nx + 16, depth), F32)],
        compiler_params=pltpu.CompilerParams(vmem_limit_bytes=16 * MIB),
        name="edge",
    )(t, umap, *parts, *got, own_send)


def filter_row(ny, read, line, factor):
    taps = taps_1d()
    acc = taps[RADIUS] * read(0)
    for d in range(1, RADIUS + 1):
        acc = acc + taps[RADIUS + d] * (read(-d) + read(d))
    line[8 : 8 + ny, :] = acc
    res = taps[RADIUS] * acc
    for d in range(1, RADIUS + 1):
        res = res + taps[RADIUS + d] * (line[8 - d : 8 - d + ny, :] + line[8 + d : 8 + d + ny, :])
    return res * factor


def clear_line(line, ny):
    zeros = jnp.zeros((8, line.shape[-1]), F32)
    for k in range(line.shape[0]):
        line[k, 0:8, :] = zeros
        line[k, 8 + ny :, :] = zeros


def filter_rows(lo, hi, chunk, read, line, factor_ref, first_ref, last_ref, out_ref, out_hbm, sem):
    ny = factor_ref.shape[1]
    copies = []

    def row(x, carry):
        res = filter_row(ny, lambda d: read(x + d), line.at[x % 2], factor_ref[x])
        out_ref[x] = res
        first_ref[x] = res[0:8]
        last_ref[x] = res[ny - 8 : ny]
        return carry

    for s, start in enumerate(range(lo, hi, chunk)):
        stop = min(start + chunk, hi)
        lax.fori_loop(start, stop, row, 0)
        span = pl.ds(start, stop - start)
        copies.append(pltpu.make_async_copy(out_ref.at[span], out_hbm.at[span], sem.at[s]))
        copies[s].start()
    return copies


def split_row(nx):
    return nx * 28 // 64


def body_kernel(shape, chunk, lhs_ref, umap_ref, part_ref, factor_ref, t_ref, out_hbm, first_ref, last_ref, line, out_ref, sem):
    nx, ny, depth = shape
    add = lax.dot_general(lhs_ref[...], umap_ref[...], (((0,), (0,)), ((), ())), preferred_element_type=F32)
    t_ref[...] = part_ref[...] + add.reshape(nx, ny, depth)
    clear_line(line, ny)
    copies = filter_rows(
        RADIUS, split_row(nx), chunk, lambda x: t_ref[x], line, factor_ref, first_ref, last_ref, out_ref, out_hbm, sem)
    for copy in copies:
        copy.wait()


def body_call(lhs, umap, part, factor):
    nx, ny, depth = part.shape
    chunk = 10
    return pl.pallas_call(
        functools.partial(body_kernel, part.shape, chunk),
        in_specs=[VMEM] * 4,
        out_specs=[VMEM, HBM, VMEM, VMEM],
        out_shape=[
            pltpu.VMEM(part.shape, F32),
            jax.ShapeDtypeStruct(part.shape, F32),
            pltpu.VMEM((nx, 8, depth), F32),
            pltpu.VMEM((nx, 8, depth), F32),
        ],
        scratch_shapes=[
            pltpu.VMEM((2, ny + 16, depth), F32),
            pltpu.VMEM(part.shape, F32),
            pltpu.SemaphoreType.DMA((-(-nx // chunk),)),
        ],
        compiler_params=pltpu.CompilerParams(vmem_limit_bytes=20 * MIB),
        name="body",
    )(*in_vmem(lhs, umap, part, factor))


def rest_kernel(shape, chunk, t_ref, xb_ref, xa_ref, factor_ref, _, __, ___, out_hbm, first_ref, last_ref,
                line, pad, out_ref, sem, side_sem):
    nx, ny, depth = shape
    clear_line(line, ny)
    pad[0:RADIUS] = xb_ref[...].reshape(RADIUS, ny, depth)
    pad[RADIUS : 3 * RADIUS] = t_ref[0 : 2 * RADIUS]
    pad[3 * RADIUS : 5 * RADIUS] = t_ref[nx - 2 * RADIUS : nx]
    pad[5 * RADIUS :] = xa_ref[...].reshape(RADIUS, ny, depth)
    copies = []
    for side, start in ((0, 0), (1, nx - RADIUS)):
        for k in range(RADIUS):
            x = start + k
            mid = (RADIUS if side == 0 else 4 * RADIUS) + k
            res = filter_row(ny, lambda d: pad[mid + d], line.at[x % 2], factor_ref[x])
            out_ref[x] = res
            first_ref[x] = res[0:8]
            last_ref[x] = res[ny - 8 : ny]
        span = pl.ds(start, RADIUS)
        copies.append(pltpu.make_async_copy(out_ref.at[span], out_hbm.at[span], side_sem.at[side]))
        copies[side].start()
    copies += filter_rows(
        split_row(nx), nx - RADIUS, chunk, lambda x: t_ref[x], line, factor_ref, first_ref, last_ref, out_ref, out_hbm, sem)
    for copy in copies:
        copy.wait()


def rest_call(t, xb, xa, factor, out, first, last):
    nx, ny, depth = t.shape
    chunk = 13
    return pl.pallas_call(
        functools.partial(rest_kernel, t.shape, chunk),
        in_specs=[VMEM] * 4 + [HBM, VMEM, VMEM],
        out_specs=[HBM, VMEM, VMEM],
        out_shape=[
            jax.ShapeDtypeStruct(out.shape, F32),
            pltpu.VMEM(first.shape, F32),
            pltpu.VMEM(last.shape, F32),
        ],
        input_output_aliases={4: 0, 5: 1, 6: 2},
        scratch_shapes=[
            pltpu.VMEM((2, ny + 16, depth), F32),
            pltpu.VMEM((6 * RADIUS, ny, depth), F32),
            pltpu.VMEM(t.shape, F32),
            pltpu.SemaphoreType.DMA((-(-nx // chunk),)),
            pltpu.SemaphoreType.DMA((2,)),
        ],
        compiler_params=pltpu.CompilerParams(vmem_limit_bytes=20 * MIB),
        name="rest",
    )(*in_vmem(t, xb, xa, factor), *in_hbm(out), *in_vmem(first, last))


def finish_kernel(shape, ngot, *refs):
    nx, ny, depth = shape
    got_refs = refs[:ngot]
    first_ref, last_ref, factor_ref, _, out_hbm, done_ref, strip, sem = refs[ngot:]
    taps = taps_1d()
    edge = RADIUS * nx
    place, count = lax.axis_index("gy"), lax.axis_size("gy")
    blocks = [r[0:edge, :].astype(F32) for r in got_refs]
    before, after = sided(place % 2 == 0, blocks) if blocks else (jnp.zeros((edge, depth), F32),) * 2
    before = jnp.where(place == 0, 0.0, before)
    after = jnp.where(place == count - 1, 0.0, after)
    flat = factor_ref.reshape(nx * ny, depth)
    copies = []
    for ref, side in ((first_ref, 0), (last_ref, 1)):
        strip[side] = ref[...]
        view = strip.at[side].reshape(nx * 8, depth)
        for y in range(RADIUS):
            add = jnp.zeros((nx, depth), F32)
            for k in range(RADIUS):
                if side == 0:
                    d, halo, own = y + RADIUS - k, before[k * nx : (k + 1) * nx], y
                else:
                    d, halo, own = k + RADIUS - y, after[k * nx : (k + 1) * nx], ny - RADIUS + y
                if d <= RADIUS:
                    add = add + taps[RADIUS + d] * halo
            at = own if side == 0 else own - (ny - 8)
            view[pl.ds(at, nx, stride=8), :] += flat[pl.ds(own, nx, stride=ny), :] * add
        target = out_hbm.at[:, 0:8, :] if side == 0 else out_hbm.at[:, ny - 8 : ny, :]
        copies.append(pltpu.make_async_copy(strip.at[side], target, sem.at[side]))
        copies[side].start()
    done_ref[...] = jnp.zeros_like(done_ref)
    for copy in copies:
        copy.wait()


def finish_call(got, first, last, factor, out):
    nx, _, depth = out.shape
    nin = len(got)
    return pl.pallas_call(
        functools.partial(finish_kernel, out.shape, len(got)),
        in_specs=[VMEM] * (nin + 3) + [HBM],
        out_specs=[HBM, VMEM],
        out_shape=[jax.ShapeDtypeStruct(out.shape, F32), pltpu.VMEM((8, LANES), F32)],
        input_output_aliases={nin + 3: 0},
        scratch_shapes=[pltpu.VMEM((2, nx, 8, depth), F32), pltpu.SemaphoreType.DMA((2,))],
        compiler_params=pltpu.CompilerParams(vmem_limit_bytes=16 * MIB),
        name="finish",
    )(*got, *in_vmem(first, last, factor), *in_hbm(out))


def mean_kernel(cells, cases, *refs):
    total = refs[0][...]
    for ref in refs[2:-1]:
        block = ref[...] if ref.shape[0] == 8 else sum3(ref[ref.shape[0] - 16 :, :].astype(F32), 0)[0:8]
        total = total + block
    for c in range(cases):
        refs[-1][c] = total[c, 0] / cells


def mean_call(sums, behind, got, cells, cases):
    return pl.pallas_call(
        functools.partial(mean_kernel, cells, cases),
        in_specs=[VMEM] * (2 + len(got)),
        out_specs=SMEM,
        out_shape=jax.ShapeDtypeStruct((cases,), F32),
        compiler_params=pltpu.CompilerParams(vmem_limit_bytes=4 * MIB),
        name="mean",
    )(sums, behind, *got)


def swap_pairs(count, first):
    return [q for i in range(first, count - 1, 2) for q in ((i, i + 1), (i + 1, i))]


def swaps_of(count):
    return min(count - 1, 2)


def swap_order(count):
    return {1: (), 2: (1,), 4: (2, 3, 1)}[count]


def xor_pairs(count, m):
    return [(i, i ^ m) for i in range(count)]


def shards(density, design_mask, energy, decay, case_index, case_weight):
    cases = energy.shape[0]
    nx, ny, depth = density.shape
    nz, gx, gy = (lax.axis_size(a) for a in ("gz", "gx", "gy"))
    send, own, source, density_v, mask_v, maps, rows = faces_call(
        density, design_mask, energy, decay, case_index, case_weight)
    swapped = nz in (1, 2, 4)
    if swapped:
        msgs = [lax.ppermute(send, "gz", xor_pairs(nz, m)) for m in swap_order(nz)]
    else:
        every = lax.all_gather(send, "gz")
        own, *msgs = [every[j] for j in range(nz)]
    part, factor, umap, *x_parts = local_call(source, density_v, mask_v, maps, rows, swaps_of(gx))
    x_parts = [lax.ppermute(v, "gx", swap_pairs(gx, k)) for k, v in enumerate(x_parts)]
    lhs, *x_sends = head_call(own, msgs, part.shape, max(swaps_of(gx), 1), swapped)
    x_got = [lax.ppermute(x_sends[k], "gx", swap_pairs(gx, k)) for k in range(swaps_of(gx))]
    t, out, first, last = body_call(lhs, umap, part, factor)
    *y_sends, xb, xa, sums = edge_call(t, umap, x_parts, x_got, x_sends[0], swaps_of(gy), cases)
    ring = gy == 4
    ends = [(0, gy - 1), (gy - 1, 0)] if ring else []
    y_got = []
    for k in range(swaps_of(gy)):
        y_got.append(lax.ppermute(y_sends[k], "gy", swap_pairs(gy, k) + (ends if k else [])))
    out, first, last = rest_call(t, xb, xa, factor, out, first, last)
    if ring:
        y_got[1], first = lax.optimization_barrier((y_got[1], first))
        more = y_got + [lax.ppermute(y_got[1], "gy", swap_pairs(gy, 0))]
    else:
        more = [lax.ppermute(sums, "gy", xor_pairs(gy, m)) for m in range(1, gy)]
    out, behind = finish_call(y_got, first, last, factor, out)
    cells = nx * ny * depth * nz * gx * gy
    return out, mean_call(sums, behind, more, float(cells), cases)


def solution(mesh):
    placed = (
        P("gx", "gy", "gz"),
        P("gx", "gy", "gz"),
        P(None, "gx", "gy", "gz"),
        P(None, "gz"),
        P(),
        P(),
    )
    return jax.shard_map(
        shards, mesh=mesh, in_specs=placed, out_specs=(P("gx", "gy", "gz"), P()), check_vma=False
    )
```
